512 devices in a mesh: ty: 16 (over x_lo, z), tx: 32 (over y, x_hi, core).
Axes of the slice: x: 4 (x_hi: 2, x_lo: 2; x = x_hi * 2 + x_lo), y: 8, z: 8, core: 2. Of those that a mesh axis runs over, the one named last changes fastest.
Arguments:
- observed: float32 [6, 2048, 8192], P(None, 'ty', 'tx'), may hold values from -6 to 6
- inverse_variance: float32 [6, 2048, 8192], P(None, 'ty', 'tx'), may hold values from 0.5 to 4
- sed: float32 [16, 32, 6], P('ty', 'tx'), may hold values from 0.2 to 2
- morph: float32 [16, 32, 128, 128], P('ty', 'tx'), may hold values from 0.02 to 1
- foot_block: int32 [16, 32], P('ty', 'tx'), may hold values from 0 to 63, as said below
- gamma: float32 [16, 32], P('ty', 'tx'), may hold values from 0.3 to 1.5
- row_kernel: float32 [6, 41], replicated, may hold values from -1 to 1
- col_kernel: float32 [6, 41], replicated, may hold values from -1 to 1
Outputs:
- residual: float32 [6, 2048, 8192], P(None, 'ty', 'tx')
- new_morph: float32 [16, 32, 128, 128], P('ty', 'tx')
- new_sed: float32 [16, 32, 6], P('ty', 'tx')
The draws below stay inside these ranges and needn't reach their ends.
Inputs may be any that keep to these rules, and one draw needn't show every extreme that they name: A source's footprint lies in its own tile row, at box column foot_block counted over the whole row; in every tile row at most 2 sources lie in one tile of 2 box columns, and some tile holds exactly 2.
All inputs are finite; a program needn't handle non-finite values.
Results may differ from the reference program's by a relative error of at most 0.0003.
Values sent between devices are 32-bit elements; how exact they have to be, the bound alone decides.
A program may use at most 64 MiB of HBM per device.

```python
import math
import jax
import jax.numpy as jnp
from jax import lax

BANDS = 6
FOOT = 128
TAPS = 41
BPT = 2
S_DEV = 1
SOURCES_ROW = 32
TROWS = 16
HEIGHT = 2048
WIDTH = 8192
N_TY = 16
N_TX = 32


def draw_foot_block(key, part):
    tiles = SOURCES_ROW // S_DEV
    slots_tile = 2 * S_DEV
    total = tiles * slots_tile

    def one_row(index):
        row_key = jax.random.fold_in(jax.random.fold_in(key, 7103), index)
        key_rank, key_tile, key_order, key_box = jax.random.split(row_key, 4)
        ranking = jax.random.permutation(key_rank, total).astype(jnp.int32)
        chosen = jax.random.randint(key_tile, (), 0, tiles, dtype=jnp.int32)
        slot_ids = jnp.arange(total, dtype=jnp.int32)
        scores = ranking - total * (slot_ids // slots_tile == chosen).astype(jnp.int32)
        order = jnp.argsort(scores, stable=True)[:SOURCES_ROW].astype(jnp.int32)
        shuffle = jax.random.permutation(key_order, SOURCES_ROW).astype(jnp.int32)
        slot_of = order[shuffle]
        tile_of = slot_of // slots_tile
        offset = jax.random.randint(key_box, (SOURCES_ROW,), 0, BPT, dtype=jnp.int32)
        return tile_of * BPT + offset
    return jax.vmap(one_row)(jnp.arange(TROWS, dtype=jnp.int32))


def levels(rng, extent, cuts, least, high):
    factor_of = 1.0
    for position, blocks in cuts:
        draws = jax.random.uniform(jax.random.fold_in(jax.random.fold_in(rng, 6), position), (blocks,), jnp.float32, least / len(cuts), high / len(cuts))
        factor_of = factor_of * jnp.repeat(jnp.exp(draws), extent[position] // blocks).reshape((-1,) + (1,) * (len(extent) - 1 - position))
    return factor_of


def scatter_about(own_key, shape, width, most, cuts=(), kind=jnp.bfloat16):
    values = jax.random.normal(own_key, shape, jnp.float32) * width
    if len(cuts) > 0:
        values = levels(own_key, shape, cuts, -0.22, 0.18) * values
    return jnp.clip(values, min=-most, max=most).astype(kind)


def setup_inputs(seed: int = 0) -> dict:
    splits = jax.random.split(jax.random.key(seed), 9)
    observed = scatter_about(splits[0], (BANDS, HEIGHT, WIDTH), 1.0, 6.0, ((1, 16), (2, 32)), jnp.float32)
    inverse_variance = jnp.clip(jnp.exp(math.log(4.0) - 2.0794415 * jax.random.uniform(splits[1], (BANDS, HEIGHT, WIDTH), jnp.float32) ** levels(splits[1], (BANDS, HEIGHT, WIDTH), ((1, 16), (2, 32)), -0.2, 0.2)), 0.5, 4.0)
    sed = jnp.clip(jnp.exp(math.log(2.0) - 2.3025851 * jax.random.uniform(splits[2], (TROWS, SOURCES_ROW, BANDS), jnp.float32) ** levels(splits[2], (TROWS, SOURCES_ROW, BANDS), ((0, 16), (1, 32)), -0.2, 0.2)), 0.2, 2.0)
    morph = jnp.clip(jnp.exp(math.log(1.0) - 3.912023 * jax.random.uniform(splits[3], (TROWS, SOURCES_ROW, FOOT, FOOT), jnp.float32) ** levels(splits[3], (TROWS, SOURCES_ROW, FOOT, FOOT), ((0, 16), (1, 32)), -0.2, 0.2)), 0.02, 1.0)
    foot_block = draw_foot_block(jax.random.fold_in(splits[8], 71), 0)
    gamma = jnp.clip(jnp.exp(math.log(1.5) - 1.60943787 * jax.random.uniform(splits[5], (TROWS, SOURCES_ROW), jnp.float32) ** levels(splits[5], (TROWS, SOURCES_ROW), ((0, 16), (1, 32)), -0.2, 0.2)), 0.3, 1.5)
    row_kernel = scatter_about(splits[6], (BANDS, TAPS), TAPS ** -0.5, 1.0, (), jnp.float32)
    col_kernel = scatter_about(splits[7], (BANDS, TAPS), TAPS ** -0.5, 1.0, (), jnp.float32)
    return dict(observed=observed, inverse_variance=inverse_variance, sed=sed, morph=morph, foot_block=foot_block, gamma=gamma, row_kernel=row_kernel, col_kernel=col_kernel)


HIGHEST_PRECISION = lax.Precision.HIGHEST

def band_pass(items):
    image, seen, weights, krow, kcol = items
    reach = (krow.shape[0] - 1) // 2
    lhs = image[None, None]
    blurred = lax.conv_general_dilated(lhs, kcol[::-1][None, None, None, :], (1, 1), ((0, 0), (reach, reach)), precision=HIGHEST_PRECISION)
    predicted = lax.conv_general_dilated(blurred, krow[::-1][None, None, :, None], (1, 1), ((reach, reach), (0, 0)), precision=HIGHEST_PRECISION)
    resid = weights * (seen - predicted[0, 0])
    backrows = lax.conv_general_dilated(resid[None, None], krow[None, None, :, None], (1, 1), ((reach, reach), (0, 0)), precision=HIGHEST_PRECISION)
    gradient = lax.conv_general_dilated(backrows, kcol[None, None, None, :], (1, 1), ((0, 0), (reach, reach)), precision=HIGHEST_PRECISION)
    return (resid, gradient[0, 0])

def reference(observed, inverse_variance, sed, morph, foot_block, gamma, row_kernel, col_kernel):
    blocks = BPT * N_TX
    placed = (foot_block[:, :, None] == jnp.arange(blocks, dtype=jnp.int32)[None, None, :]).astype(jnp.float32)
    weighted = placed[:, :, None, :] * sed[:, :, :, None]

    def render(items):
        weighted_row, morph_row = items
        return jnp.einsum('kbj,krc->brjc', weighted_row, morph_row, precision=HIGHEST_PRECISION)
    model = lax.map(render, (weighted, morph))
    model = model.transpose(1, 0, 2, 3, 4).reshape(BANDS, N_TY * FOOT, blocks * FOOT)
    residual, gradient = lax.map(band_pass, (model, observed, inverse_variance, row_kernel, col_kernel))
    grid = gradient.reshape(BANDS, N_TY, FOOT, blocks, FOOT).transpose(1, 0, 2, 3, 4)

    def source_terms(items):
        weighted_row, placed_row, morph_row, grid_row = items
        morph_terms = jnp.einsum('kbj,brjc->krc', weighted_row, grid_row, precision=HIGHEST_PRECISION)
        raw_terms = jnp.einsum('krc,brjc->kbj', morph_row, grid_row, precision=HIGHEST_PRECISION)
        sed_terms = lax.optimization_barrier(jnp.sum(raw_terms * placed_row[:, None, :], axis=2))
        return (morph_terms, sed_terms)
    morph_grad, sed_grad = lax.map(source_terms, (weighted, placed, morph, grid))
    step_morph = gamma / lax.optimization_barrier(jnp.sum(sed * sed, axis=2))
    new_morph = jnp.maximum(morph + step_morph[:, :, None, None] * morph_grad, 0.0)
    step_sed = gamma / jnp.sqrt(lax.optimization_barrier(jnp.sum(morph * morph, axis=(2, 3))))
    new_sed = jnp.maximum(sed + step_sed[:, :, None] * sed_grad, 0.0)
    return (residual, new_morph, new_sed)
```

```python
import functools

import jax
import jax.numpy as jnp
from jax import lax
from jax.experimental import pallas as pl
from jax.experimental.pallas import tpu as pltpu
from jax.sharding import PartitionSpec as P

MESH = pl.DeviceIdType.MESH
F32 = jnp.float32
BF16 = jnp.bfloat16
HIGHEST = lax.Precision.HIGHEST
BOX = 128
HALO = 24
WIDE = 384
NAR = 256


def up8(n):
    return (n + 7) // 8 * 8


def iota(shape, dim):
    return lax.broadcasted_iota(jnp.int32, shape, dim)


def split(x):
    hi = x.astype(BF16)
    return hi, (x - hi.astype(F32)).astype(BF16)


def dot(a, b):
    return jnp.dot(a, b, preferred_element_type=F32)


def exact(a, b):
    return jnp.dot(a, b, preferred_element_type=F32, precision=HIGHEST)


def kernel(
    nty, ntx, bands, taps,
    obs_hbm, iv_hbm, sed_s, morph_hbm, foot_s, gamma_s, rk_hbm, ck_hbm,
    resid_hbm, nmorph_ref, nsed_ref,
    obs_e, iv_e, res_e, model_e, west1, east1, west2, east2, sw1, se1, sw2, se2,
    morph_v, ob1, ib1, ob2, ib2, ob3, ib3, ob4, ib4, sg_send, sg_in,
    slots, sinfo, nslots, sslots, ninfo, soinfo, grads, sgacc,
    wtab, mtab, rk_v, ck_v, ktab_c, ktab_r, tcol, trow1, trow2, ext_h, ext_l,
    loc_sem, send_sem, a2a_sem, obs_sem, sl_sem, st_sem,
):
    ti = lax.axis_index("ty")
    me = lax.axis_index("tx")
    reach = (taps - 1) // 2
    rows = BOX // ntx
    m1, m2, m4 = up8(rows + 1), 2 * rows, up8(rows)
    deep = 2 * HALO
    ext1, ext2 = BOX + 2 * deep, BOX + 2 * HALO
    north, south = lax.rem(ti + nty - 1, nty), lax.rem(ti + 1, nty)
    west, east = lax.rem(me + ntx - 1, ntx), lax.rem(me + 1, ntx)

    barrier = pltpu.get_barrier_semaphore()

    def greet(j, carry):
        pl.semaphore_signal(
            barrier, inc=1, device_id=(ti, lax.rem(me + j, ntx)), device_id_type=MESH
        )
        return carry

    lax.fori_loop(1, ntx, greet, 0)
    for yy in (north, south):
        for xx in (me, west, east):
            pl.semaphore_signal(barrier, inc=1, device_id=(yy, xx), device_id_type=MESH)

    load_morph = pltpu.make_async_copy(morph_hbm.at[0, 0], morph_v, loc_sem.at[0])
    load_rk = pltpu.make_async_copy(rk_hbm, rk_v, loc_sem.at[1])
    load_ck = pltpu.make_async_copy(ck_hbm, ck_v, loc_sem.at[2])
    load_obs = pltpu.make_async_copy(obs_hbm, obs_e.at[:, HALO : HALO + BOX, :], loc_sem.at[3])
    load_iv = pltpu.make_async_copy(iv_hbm, iv_e.at[:, HALO : HALO + BOX, :], loc_sem.at[4])
    load_morph.start()
    load_rk.start()
    load_ck.start()
    load_obs.start()
    load_iv.start()

    foot = foot_s[0, 0]
    tile = foot // 2
    box = foot - 2 * tile
    lane1 = iota((1, BOX), 1)
    info = jnp.zeros((1, BOX), F32)
    for b in range(bands):
        info = jnp.where(lane1 == b, sed_s[0, 0, b], info)
    info = jnp.where(lane1 == 6, tile.astype(F32), info)
    info = jnp.where(lane1 == 7, box.astype(F32), info)
    ob1[...] = jnp.zeros_like(ob1)
    ob4[...] = jnp.zeros_like(ob4)
    ob1[pl.ds(rows, ntx, stride=m1), :] = jnp.broadcast_to(info, (ntx, BOX))
    load_morph.wait()
    for r in range(rows):
        ob1[pl.ds(r, ntx, stride=m1), :] = morph_v[pl.ds(r, ntx, stride=rows), :]

    def exchange(out, arrived, m, phase):
        def step(j, carry):
            p = lax.rem(me + j, ntx)
            pltpu.make_async_remote_copy(
                out.at[pl.ds(pl.multiple_of(p * m, 8), m)],
                arrived.at[pl.ds(pl.multiple_of(me * m, 8), m)],
                send_sem.at[phase], a2a_sem.at[phase],
                device_id=(ti, p), device_id_type=MESH,
            ).start()
            return carry

        lax.fori_loop(1, ntx, step, 0)
        mine = pl.ds(pl.multiple_of(me * m, 8), m)
        arrived[mine, :] = out[mine, :]

    def whole(out, arrived, m, phase):
        part = pl.ds(0, (ntx - 1) * m)
        return pltpu.make_async_remote_copy(
            out.at[part], arrived.at[part], send_sem.at[phase], a2a_sem.at[phase],
            device_id=(ti, east), device_id_type=MESH,
        )

    pl.semaphore_wait(barrier, ntx - 1 + 6)
    exchange(ob1, ib1, m1, 0)

    def send(src, dst, s_sem, r_sem, yy, xx):
        copy = pltpu.make_async_remote_copy(
            src, dst, s_sem, r_sem, device_id=(yy, xx), device_id_type=MESH
        )
        copy.start()
        return copy

    low, high = slice(0, HALO), slice(BOX - HALO, BOX)
    far = slice(HALO + BOX, ext2)
    images = []
    for n, (src, dst) in enumerate(((obs_hbm, obs_e), (iv_hbm, iv_e))):
        images.append(send(src.at[:, high, :], dst.at[:, low, :], obs_sem.at[0, 2 * n], obs_sem.at[1, 2 * n], south, me))
        images.append(send(src.at[:, low, :], dst.at[:, far, :], obs_sem.at[0, 2 * n + 1], obs_sem.at[1, 2 * n + 1], north, me))

    load_rk.wait()
    load_ck.wait()
    flip = (iota((BOX, BOX), 0) + iota((BOX, BOX), 1) == taps - 1).astype(F32)

    for table, values, forward in ((ktab_c, ck_v, 0), (ktab_r, rk_v, 1)):
        table[...] = jnp.zeros_like(table)
        table[forward, 0, 0:bands, 0:taps] = values[...]
        plain = table[forward, 0, :, 0:BOX]
        table[1 - forward, 0, :, 0:BOX] = exact(plain, flip)
        for st in range(2):
            full = table[st, 0, :, 0:BOX]
            hi = full.astype(BF16).astype(F32)
            table[st, 0, :, 0:BOX] = hi
            table[st, 1, :, 0:BOX] = full - hi

    def band_tables(st, b):
        strip_row = iota((BOX, NAR), 0)
        inside = (strip_row >= reach * b) & (strip_row < reach * b + reach)
        for part in range(2):
            spread = jnp.broadcast_to(ktab_c[st, part, pl.ds(b, 1), :], (BOX, WIDE))
            skew = pltpu.roll(spread, 0, 1, stride=1, stride_axis=0)
            for n in range(2):
                own = pltpu.roll(skew, (WIDE - reach + n * BOX) % WIDE, 1)[:, 0:NAR]
                tcol[st, b, part, n * BOX : (n + 1) * BOX, :] = own.astype(BF16)
            for n, shift in enumerate((WIDE - 2 * reach, NAR - reach)):
                side = pltpu.roll(skew, shift - reach * b, 1)[:, 0:NAR]
                side = jnp.where(inside, side, 0.0).astype(BF16)
                tcol[st, b, part, NAR + n * BOX : NAR + (n + 1) * BOX, :] = side
            spread = jnp.broadcast_to(ktab_r[st, part, pl.ds(b, 1), :], (BOX, NAR))
            skew = pltpu.roll(spread, 0, 1, stride=1, stride_axis=0)
            out, trow = ((ext2, trow1), (BOX, trow2))[st]
            for n in range(0, out, BOX):
                count = min(BOX, out - n)
                own = pltpu.roll(skew, (HALO - reach + n) % NAR, 1)
                trow[b, part, n : n + count] = own[0:count, 0 : trow.shape[3]].astype(BF16)

    for b in range(bands):
        band_tables(0, b)

    whole(ob1, ib1, m1, 0).wait_recv()
    infos = ib1[pl.ds(rows, ntx, stride=m1), :]
    wide = (ntx, BOX)
    row_i, lane_i = iota(wide, 0), iota(wide, 1)
    tile_col = jnp.broadcast_to(infos[:, 6:7], wide)
    tile_row = jnp.sum(jnp.where(row_i == lane_i, tile_col, 0.0), axis=0, keepdims=True)
    tile_row = jnp.broadcast_to(jnp.where(lane1 < ntx, tile_row, -1.0), wide)
    same = tile_col == tile_row
    slot_row = jnp.sum(jnp.where(same & (row_i < lane_i), 1.0, 0.0), axis=0, keepdims=True)
    slot_row = jnp.broadcast_to(slot_row, wide)
    slot_col = jnp.sum(jnp.where(same & (lane_i < row_i), 1.0, 0.0), axis=1, keepdims=True)
    slot_col = jnp.broadcast_to(slot_col, wide)
    target = row_i.astype(F32)
    pick = [
        jnp.where((tile_row == target) & (slot_row == float(s)), 1.0, 0.0)[:, 0:ntx]
        for s in range(2)
    ]
    pieces = jnp.concatenate([ib1[pl.ds(r, ntx, stride=m1), :] for r in range(rows)], axis=1)
    chosen = exact(jnp.concatenate(pick, axis=0), pieces)
    for s in range(2):
        for r in range(rows):
            ob2[pl.ds(s * rows + r, ntx, stride=m2), :] = chosen[
                s * ntx : (s + 1) * ntx, r * BOX : (r + 1) * BOX
            ]
    exchange(ob2, ib2, m2, 1)

    here = me.astype(F32)
    for s in range(2):
        mine = (tile_col == here) & (slot_col == float(s))
        sinfo[pl.ds(s, 1), :] = jnp.sum(jnp.where(mine, infos, 0.0), axis=0, keepdims=True)
    sinfo[2:8, :] = jnp.zeros((6, BOX), F32)
    lane_f = lane_i.astype(F32)
    give = jnp.concatenate(
        [
            jnp.where((tile_col == lane_f) & (slot_col == float(s)), 1.0, 0.0)[:, 0:ntx]
            for s in range(2)
        ],
        axis=1,
    )
    own_tile = tile.astype(F32)
    own_slot = jnp.sum(
        jnp.where(row_i[:, 0:1] == me, slot_col[:, 0:1], 0.0), axis=0, keepdims=True
    )

    eye8 = iota((8, BOX), 0) == iota((8, BOX), 1)

    def tables(which, ref, live):
        for s in range(2):
            line = jnp.broadcast_to(ref[pl.ds(s, 1), :], (8, BOX))
            column = jnp.sum(jnp.where(eye8, line, 0.0), axis=1, keepdims=True)
            table = jnp.broadcast_to(column, (8, BOX)) * live
            boxes = jnp.broadcast_to(column[7:8], (8, BOX))
            for j in range(2):
                wtab[which, s, j] = jnp.where(boxes == float(j), table, 0.0)
                if which == 1:
                    mtab[s, j] = jnp.where(boxes == float(j), 1.0, 0.0)

    tables(1, sinfo, 1.0)
    for b in range(bands):
        band_tables(1, b)

    whole(ob2, ib2, m2, 1).wait_recv()
    for s in range(2):
        for r in range(rows):
            slots[s, pl.ds(r, ntx, stride=rows), :] = ib2[pl.ds(s * rows + r, ntx, stride=m2), :]

    waits = []
    for n, (src, dst, yy) in enumerate(
        (
            (slots.at[:, BOX - deep : BOX, :], nslots, south),
            (slots.at[:, 0:deep, :], sslots, north),
            (sinfo, ninfo, south),
            (sinfo, soinfo, north),
        )
    ):
        waits.append(send(src, dst, sl_sem.at[0, n], sl_sem.at[1, n], yy, me))

    sw1[...] = jnp.zeros_like(sw1)
    se1[...] = jnp.zeros_like(se1)
    tile_lane = iota((BOX, BOX), 1)
    for b in range(bands):
        for j in range(2):
            part = sum(wtab[1, s, j, pl.ds(b, 1), :] * slots[s] for s in range(2))
            model_e[b, deep : deep + BOX, j * BOX : (j + 1) * BOX] = part
            keep = (tile_lane >= reach * b) & (tile_lane < reach * b + reach)
            shift = (reach * b) if j == 0 else (reach * b + reach) % BOX
            moved = pltpu.roll(part, shift, 1) if shift else part
            ref = (sw1, se1)[j]
            ref[...] = jnp.where(keep, moved, ref[...])
    for n, (src, dst, yy, xx) in enumerate(
        (
            (se1, west1.at[deep : deep + BOX], ti, east),
            (sw1, east1.at[deep : deep + BOX], ti, west),
            (se1.at[BOX - deep : BOX], west1.at[0:deep], south, east),
            (sw1.at[BOX - deep : BOX], east1.at[0:deep], south, west),
            (se1.at[0:deep], west1.at[deep + BOX : ext1], north, east),
            (sw1.at[0:deep], east1.at[deep + BOX : ext1], north, west),
        )
    ):
        waits.append(send(src, dst, sl_sem.at[0, 4 + n], sl_sem.at[1, 4 + n], yy, xx))

    for copy in waits[0:4]:
        copy.wait_recv()
    tables(0, ninfo, jnp.where(ti > 0, 1.0, 0.0))
    tables(2, soinfo, jnp.where(ti < nty - 1, 1.0, 0.0))

    for b in range(bands):
        for which, ref, start in ((0, nslots, 0), (2, sslots, deep + BOX)):
            for j in range(2):
                part = sum(wtab[which, s, j, pl.ds(b, 1), :] * ref[s] for s in range(2))
                model_e[b, start : start + deep, j * BOX : (j + 1) * BOX] = part

    load_obs.wait()
    load_iv.wait()
    for copy in images:
        copy.wait_recv()
    for copy in waits[4:]:
        copy.wait_recv()

    def halo_parts(left, right, count, edge):
        row = iota((count, BOX), 0)
        inner = ((row >= edge) | (ti > 0)) & ((row < count - edge) | (ti < nty - 1))
        for n, (ref, ok) in enumerate(((left, me > 0), (right, me < ntx - 1))):
            hi, lo = split(jnp.where(inner & ok, ref[...], 0.0))
            ext_h[0:count, n * BOX : (n + 1) * BOX] = hi
            ext_l[0:count, n * BOX : (n + 1) * BOX] = lo

    def passes(st, b, image, count, trow):
        hi, lo = split(image)
        hi = jnp.concatenate([hi, ext_h[0:count, :]], axis=1)
        lo = jnp.concatenate([lo, ext_l[0:count, :]], axis=1)
        mixed = dot(hi, tcol[st, b, 0]) + (dot(hi, tcol[st, b, 1]) + dot(lo, tcol[st, b, 0]))
        hi, lo = split(mixed)
        return dot(trow[b, 0], hi) + (dot(trow[b, 0], lo) + dot(trow[b, 1], hi))

    halo_parts(west1, east1, ext1, deep)
    sw2[...] = jnp.zeros_like(sw2)
    se2[...] = jnp.zeros_like(se2)
    row = iota((ext2, 2 * BOX), 0)
    inside = ((row >= HALO) | (ti > 0)) & ((row < HALO + BOX) | (ti < nty - 1))
    lane = iota((ext2, BOX), 1)

    def first(b, carry):
        predicted = passes(0, b, model_e[b], ext1, trow1)
        residual = jnp.where(inside, iv_e[b] * (obs_e[b] - predicted), 0.0)
        res_e[b] = residual
        keep = (lane >= reach * b) & (lane < reach * b + reach)
        moved = pltpu.roll(residual[:, 0:BOX], reach * b, 1)
        sw2[...] = jnp.where(keep, moved, sw2[...])
        moved = pltpu.roll(residual[:, BOX:], lax.rem(reach * b + reach, BOX), 1)
        se2[...] = jnp.where(keep, moved, se2[...])
        return carry

    lax.fori_loop(0, bands, first, 0)
    strips = [
        send(se2, west2, st_sem.at[0, 0], st_sem.at[1, 0], ti, east),
        send(sw2, east2, st_sem.at[0, 1], st_sem.at[1, 1], ti, west),
    ]
    store = pltpu.make_async_copy(res_e.at[:, HALO : HALO + BOX, :], resid_hbm, loc_sem.at[5])
    store.start()
    grads[...] = jnp.zeros_like(grads)
    sgacc[...] = jnp.zeros_like(sgacc)
    for copy in strips:
        copy.wait_recv()
    halo_parts(west2, east2, ext2, HALO)

    def second(b, carry):
        gradient = passes(1, b, res_e[b], ext2, trow2)
        halves = (gradient[:, 0:BOX], gradient[:, BOX:])
        for s in range(2):
            grads[s] += sum(wtab[1, s, j, pl.ds(b, 1), :] * halves[j] for j in range(2))
            under = sum(mtab[s, j, pl.ds(b, 1), :] * halves[j] for j in range(2))
            sgacc[s, pl.ds(b, 1), :] = jnp.sum(slots[s] * under, axis=0, keepdims=True)
        return carry

    lax.fori_loop(0, bands, second, 0)

    for s in range(2):
        for r in range(rows):
            ob3[pl.ds(s * rows + r, ntx, stride=m2), :] = grads[s, pl.ds(r, ntx, stride=rows), :]
    exchange(ob3, ib3, m2, 2)
    line = jnp.zeros((1, BOX), F32)
    for s in range(2):
        column = jnp.broadcast_to(jnp.sum(sgacc[s], axis=1, keepdims=True), (8, BOX))
        mark = iota((8, BOX), 1) == iota((8, BOX), 0) + 8 * s
        line = line + jnp.sum(jnp.where(mark, column, 0.0), axis=0, keepdims=True)
    sg_send[0] = line
    sg_in[me] = line

    def spread_sed(j, carry):
        p = lax.rem(me + j, ntx)
        pltpu.make_async_remote_copy(
            sg_send.at[0], sg_in.at[me], send_sem.at[4], a2a_sem.at[4],
            device_id=(ti, p), device_id_type=MESH,
        ).start()
        return carry

    lax.fori_loop(1, ntx, spread_sed, 0)

    whole(ob3, ib3, m2, 2).wait_recv()
    pieces = jnp.concatenate(
        [
            jnp.concatenate(
                [ib3[pl.ds(s * rows + r, ntx, stride=m2), :] for r in range(rows)], axis=1
            )
            for s in range(2)
        ],
        axis=0,
    )
    chosen = exact(give, pieces)
    for r in range(rows):
        ob4[pl.ds(r, ntx, stride=m4), :] = chosen[:, r * BOX : (r + 1) * BOX]
    exchange(ob4, ib4, m4, 3)

    square = jnp.sum(jnp.where(lane1 < bands, info * info, 0.0), axis=1, keepdims=True)
    step_morph = gamma_s[0, 0] / square
    full = morph_v[...]
    norm = jnp.sum(jnp.sum(full * full, axis=0, keepdims=True), axis=1, keepdims=True)
    step_sed = gamma_s[0, 0] / jnp.sqrt(norm)

    part = pl.ds(0, ntx - 1)
    seds = pltpu.make_async_remote_copy(
        sg_in.at[part], sg_in.at[part], send_sem.at[4], a2a_sem.at[4],
        device_id=(ti, east), device_id_type=MESH,
    )
    seds.wait_recv()
    terms = jnp.zeros((1, BOX), F32)
    for d in range(ntx):
        terms = terms + jnp.where(own_tile == float(d), sg_in[d], 0.0)
    terms = jnp.where(own_slot == 0.0, terms, pltpu.roll(terms, BOX - 8, 1))
    nsed_ref[0] = jnp.maximum(info + step_sed * terms, 0.0)[:, 0:bands]

    whole(ob4, ib4, m4, 3).wait_recv()
    for r in range(rows):
        at = pl.ds(r, ntx, stride=rows)
        update = step_morph * ib4[pl.ds(r, ntx, stride=m4), :]
        nmorph_ref[0, 0, at, :] = jnp.maximum(morph_v[at, :] + update, 0.0)

    whole(ob1, ib1, m1, 0).wait_send()
    whole(ob2, ib2, m2, 1).wait_send()
    whole(ob3, ib3, m2, 2).wait_send()
    whole(ob4, ib4, m4, 3).wait_send()
    seds.wait_send()
    for copy in images + waits + strips:
        copy.wait_send()
    store.wait()


def solution(mesh):
    nty, ntx = mesh.shape["ty"], mesh.shape["tx"]

    def body(observed, inverse_variance, sed, morph, foot_block, gamma, row_kernel, col_kernel):
        bands, height, width = observed.shape
        taps = row_kernel.shape[1]
        rows = BOX // ntx
        m1, m2, m4 = up8(rows + 1), 2 * rows, up8(rows)
        deep = 2 * HALO
        ext1, ext2 = height + 2 * deep, height + 2 * HALO

        def vmem(*shape, dtype=F32):
            return pltpu.VMEM(shape, dtype)

        scratch = [
            vmem(bands, ext2, width), vmem(bands, ext2, width), vmem(bands, ext2, width),
            vmem(bands, ext1, width),
            vmem(ext1, BOX), vmem(ext1, BOX), vmem(ext2, BOX), vmem(ext2, BOX),
            vmem(BOX, BOX), vmem(BOX, BOX), vmem(ext2, BOX), vmem(ext2, BOX),
            vmem(BOX, BOX),
            vmem(ntx * m1, BOX), vmem(ntx * m1, BOX), vmem(ntx * m2, BOX), vmem(ntx * m2, BOX),
            vmem(ntx * m2, BOX), vmem(ntx * m2, BOX), vmem(ntx * m4, BOX), vmem(ntx * m4, BOX),
            vmem(1, 1, BOX), vmem(ntx, 1, BOX),
            vmem(2, BOX, BOX), vmem(8, BOX), vmem(2, deep, BOX), vmem(2, deep, BOX),
            vmem(8, BOX), vmem(8, BOX), vmem(2, BOX, BOX), vmem(2, 8, BOX),
            vmem(3, 2, 2, 8, BOX), vmem(2, 2, 8, BOX),
            vmem(bands, taps), vmem(bands, taps),
            vmem(2, 2, 8, WIDE), vmem(2, 2, 8, NAR),
            vmem(2, bands, 2, 2 * NAR, NAR, dtype=BF16),
            vmem(bands, 2, ext2, ext1, dtype=BF16), vmem(bands, 2, BOX, ext2, dtype=BF16),
            vmem(ext1, NAR, dtype=BF16), vmem(ext1, NAR, dtype=BF16),
            pltpu.SemaphoreType.DMA((6,)), pltpu.SemaphoreType.DMA((5,)),
            pltpu.SemaphoreType.DMA((5,)), pltpu.SemaphoreType.DMA((2, 4)),
            pltpu.SemaphoreType.DMA((2, 10)), pltpu.SemaphoreType.DMA((2, 2)),
        ]
        anywhere = pl.BlockSpec(memory_space=pl.ANY)
        scalars = pl.BlockSpec(memory_space=pltpu.SMEM)
        vector = pl.BlockSpec(memory_space=pltpu.VMEM)
        return pl.pallas_call(
            functools.partial(kernel, nty, ntx, bands, taps),
            out_shape=(
                jax.ShapeDtypeStruct(observed.shape, F32),
                jax.ShapeDtypeStruct(morph.shape, F32),
                jax.ShapeDtypeStruct(sed.shape, F32),
            ),
            in_specs=[anywhere, anywhere, scalars, anywhere, scalars, scalars, anywhere, anywhere],
            out_specs=(anywhere, vector, vector),
            scratch_shapes=scratch,
            compiler_params=pltpu.CompilerParams(collective_id=0, has_side_effects=True),
        )(observed, inverse_variance, sed, morph, foot_block, gamma, row_kernel, col_kernel)

    in_specs = (
        P(None, "ty", "tx"),
        P(None, "ty", "tx"),
        P("ty", "tx", None),
        P("ty", "tx", None, None),
        P("ty", "tx"),
        P("ty", "tx"),
        P(),
        P(),
    )
    out_specs = (P(None, "ty", "tx"), P("ty", "tx", None, None), P("ty", "tx", None))
    return jax.shard_map(body, mesh=mesh, in_specs=in_specs, out_specs=out_specs, check_vma=False)
```

```python
import functools

import jax
import jax.numpy as jnp
from jax import lax
from jax.experimental import pallas as pl
from jax.experimental.pallas import tpu as pltpu
from jax.sharding import PartitionSpec as P

MESH = pl.DeviceIdType.MESH
F32 = jnp.float32
BF16 = jnp.bfloat16
HIGHEST = lax.Precision.HIGHEST
BOX = 128
HALO = 24
WIDE = 384
NAR = 256


def up8(n):
    return (n + 7) // 8 * 8


def iota(shape, dim):
    return lax.broadcasted_iota(jnp.int32, shape, dim)


def split(x):
    hi = x.astype(BF16)
    return hi, (x - hi.astype(F32)).astype(BF16)


def dot(a, b):
    return jnp.dot(a, b, preferred_element_type=F32)


def exact(a, b):
    return jnp.dot(a, b, preferred_element_type=F32, precision=HIGHEST)


def kernel(
    nty, ntx, bands, taps,
    obs_hbm, iv_hbm, sed_hbm, morph_hbm, foot_hbm, gamma_hbm, rk_hbm, ck_hbm,
    resid_hbm, nmorph_ref, nsed_ref,
    obs_e, iv_e, res_e, model_e, mixed_e, back, grad,
    west1, east1, west2, east2, sw1, se1, sw2, se2, pack, edges,
    morph_v, sed_v, foot_v, gamma_v, info_v,
    ob1, ib1, ob2, ib2, ob3, ib3, ob4, ib4, sg_send, sg_in,
    slots, sinfo, nslots, sslots, ninfo, soinfo, grads, sgacc,
    wtab, mtab, rk_v, ck_v, ktab_c, ktab_r, tcol, trow1, trow2, diag, last, ext_h, ext_l,
    loc_sem, send_sem, a2a_sem, obs_sem, sl_sem, st_sem,
):
    ti = lax.axis_index("ty")
    me = lax.axis_index("tx")
    reach = (taps - 1) // 2
    rows = BOX // ntx
    m1, m2, m4 = up8(rows + 1), 2 * rows, up8(rows)
    deep = 2 * HALO
    ext1, ext2 = BOX + 2 * deep, BOX + 2 * HALO
    north, south = lax.rem(ti + nty - 1, nty), lax.rem(ti + 1, nty)
    west, east = lax.rem(me + ntx - 1, ntx), lax.rem(me + 1, ntx)

    barrier = pltpu.get_barrier_semaphore()

    def wrapped(j):
        p = me + j
        return jnp.where(p >= ntx, p - ntx, p)

    order = sorted(range(1, ntx), key=lambda j: -min(j, ntx - j))
    for j in order:
        pl.semaphore_signal(barrier, inc=1, device_id=(ti, wrapped(j)), device_id_type=MESH)
    for yy in (north, south):
        for xx in (me, west, east):
            pl.semaphore_signal(barrier, inc=1, device_id=(yy, xx), device_id_type=MESH)

    load_morph = pltpu.make_async_copy(morph_hbm.at[0, 0], morph_v, loc_sem.at[0])
    load_rk = pltpu.make_async_copy(rk_hbm, rk_v, loc_sem.at[1])
    load_ck = pltpu.make_async_copy(ck_hbm, ck_v, loc_sem.at[2])
    load_obs = pltpu.make_async_copy(obs_hbm, obs_e.at[:, HALO : HALO + BOX, :], loc_sem.at[3])
    load_iv = pltpu.make_async_copy(iv_hbm, iv_e.at[:, HALO : HALO + BOX, :], loc_sem.at[4])
    scalars = [
        pltpu.make_async_copy(src, dst, loc_sem.at[6 + n])
        for n, (src, dst) in enumerate(((sed_hbm, sed_v), (foot_hbm, foot_v), (gamma_hbm, gamma_v)))
    ]
    for copy in scalars:
        copy.start()
    load_morph.start()
    load_rk.start()
    load_ck.start()
    load_obs.start()
    load_iv.start()

    ob1[...] = jnp.zeros_like(ob1)
    ob4[...] = jnp.zeros_like(ob4)
    lane1 = iota((1, BOX), 1)
    info_v[...] = jnp.zeros_like(info_v)
    for copy in scalars:
        copy.wait()
    tile = foot_v[...] // 2
    box = foot_v[...] - 2 * tile
    info_v[0:1, 0:bands] = sed_v[0]
    info = info_v[0:1, :]
    own_tile = tile.astype(F32)
    info = jnp.where(lane1 == 6, own_tile, info)
    info = jnp.where(lane1 == 7, box.astype(F32), info)
    ob1[pl.ds(rows, ntx, stride=m1), :] = jnp.broadcast_to(info, (ntx, BOX))
    load_morph.wait()
    for r in range(rows):
        ob1[pl.ds(r, ntx, stride=m1), :] = morph_v[pl.ds(r, ntx, stride=rows), :]

    def exchange(out, arrived, m, phase):
        for j in order:
            pltpu.make_async_remote_copy(
                out.at[pl.ds(pl.multiple_of(wrapped(j) * m, 8), m)],
                arrived.at[pl.ds(pl.multiple_of(me * m, 8), m)],
                send_sem.at[phase], a2a_sem.at[phase],
                device_id=(ti, wrapped(j)), device_id_type=MESH,
            ).start()
        mine = pl.ds(pl.multiple_of(me * m, 8), m)
        arrived[mine, :] = out[mine, :]

    def whole(out, arrived, m, phase):
        part = pl.ds(0, (ntx - 1) * m)
        return pltpu.make_async_remote_copy(
            out.at[part], arrived.at[part], send_sem.at[phase], a2a_sem.at[phase],
            device_id=(ti, east), device_id_type=MESH,
        )

    pl.semaphore_wait(barrier, ntx - 1 + 6)
    exchange(ob1, ib1, m1, 0)

    def send(src, dst, s_sem, r_sem, yy, xx):
        copy = pltpu.make_async_remote_copy(
            src, dst, s_sem, r_sem, device_id=(yy, xx), device_id_type=MESH
        )
        copy.start()
        return copy

    low, high = slice(0, HALO), slice(BOX - HALO, BOX)
    far = slice(HALO + BOX, ext2)
    images = []
    for n, (src, dst) in enumerate(((obs_hbm, obs_e), (iv_hbm, iv_e))):
        images.append(send(src.at[:, high, :], dst.at[:, low, :], obs_sem.at[0, 2 * n], obs_sem.at[1, 2 * n], south, me))
        images.append(send(src.at[:, low, :], dst.at[:, far, :], obs_sem.at[0, 2 * n + 1], obs_sem.at[1, 2 * n + 1], north, me))

    load_rk.wait()
    load_ck.wait()
    flip = (iota((BOX, BOX), 0) + iota((BOX, BOX), 1) == taps - 1).astype(F32)

    for table, values, forward in ((ktab_c, ck_v, 0), (ktab_r, rk_v, 1)):
        table[...] = jnp.zeros_like(table)
        table[forward, 0, 0:bands, 0:taps] = values[...]
        plain = table[forward, 0, :, 0:BOX]
        table[1 - forward, 0, :, 0:BOX] = exact(plain, flip)
        for st in range(2):
            full = table[st, 0, :, 0:BOX]
            hi = full.astype(BF16).astype(F32)
            table[st, 0, :, 0:BOX] = hi
            table[st, 1, :, 0:BOX] = full - hi

    def band_tables(st, b):
        for part in range(2):
            spread = jnp.broadcast_to(ktab_c[st, part, pl.ds(b, 1), :], (BOX, WIDE))
            skew = pltpu.roll(spread, 0, 1, stride=1, stride_axis=0)
            for n in range(2):
                own = pltpu.roll(skew, (WIDE - reach + n * BOX) % WIDE, 1)[:, 0:NAR]
                tcol[st, b, part, n * BOX : (n + 1) * BOX, :] = own.astype(BF16)
            spread = jnp.broadcast_to(ktab_r[st, part, pl.ds(b, 1), :], (BOX, NAR))
            skew = pltpu.roll(spread, 0, 1, stride=1, stride_axis=0)
            out, trow = ((ext2, trow1), (BOX, trow2))[st]
            for n in range(0, out, BOX):
                count = min(BOX, out - n)
                own = pltpu.roll(skew, (HALO - reach + n) % NAR, 1)
                trow[b, part, n : n + count] = own[0:count, 0 : trow.shape[3]].astype(BF16)

    tile_row_i, tile_lane = iota((BOX, BOX), 0), iota((BOX, BOX), 1)

    def of_band(index, b):
        return (index >= reach * b) & (index < reach * b + reach)

    def strip_tables(st):
        together = tile_row_i < 0
        for b in range(bands):
            together = together | (of_band(tile_row_i, b) & of_band(tile_lane, b))
        rows_i = iota((BOX, WIDE), 0)
        for part in range(2):
            spread = jnp.zeros((BOX, WIDE), F32)
            for b in range(bands):
                line = jnp.broadcast_to(ktab_c[st, part, b : b + 1, :], (BOX, WIDE))
                spread = jnp.where(of_band(rows_i, b), line, spread)
            skew = pltpu.roll(spread, 0, 1, stride=1, stride_axis=0)
            left = pltpu.roll(skew, WIDE - 2 * reach, 1)
            empty = jnp.zeros((BOX, BOX), BF16)
            for n, values in enumerate((left, skew)):
                block = jnp.where(together, values[:, 0:BOX], 0.0).astype(BF16)
                at = slice(n * BOX, (n + 1) * BOX)
                diag[st, part, at, at] = block
                diag[st, part, at, slice((1 - n) * BOX, (2 - n) * BOX)] = empty

    for b in range(bands):
        band_tables(0, b)
    strip_tables(0)

    whole(ob1, ib1, m1, 0).wait_recv()
    infos = ib1[pl.ds(rows, ntx, stride=m1), :]
    wide = (ntx, BOX)
    row_i, lane_i = iota(wide, 0), iota(wide, 1)
    tile_col = jnp.broadcast_to(infos[:, 6:7], wide)
    tile_row = jnp.sum(jnp.where(row_i == lane_i, tile_col, 0.0), axis=0, keepdims=True)
    tile_row = jnp.broadcast_to(jnp.where(lane1 < ntx, tile_row, -1.0), wide)
    same = tile_col == tile_row
    slot_row = jnp.sum(jnp.where(same & (row_i < lane_i), 1.0, 0.0), axis=0, keepdims=True)
    slot_row = jnp.broadcast_to(slot_row, wide)
    slot_col = jnp.sum(jnp.where(same & (lane_i < row_i), 1.0, 0.0), axis=1, keepdims=True)
    slot_col = jnp.broadcast_to(slot_col, wide)
    target = row_i.astype(F32)
    pick = [
        jnp.where((tile_row == target) & (slot_row == float(s)), 1.0, 0.0)[:, 0:ntx]
        for s in range(2)
    ]
    pieces = jnp.concatenate([ib1[pl.ds(r, ntx, stride=m1), :] for r in range(rows)], axis=1)
    chosen = exact(jnp.concatenate(pick, axis=0), pieces)
    for s in range(2):
        for r in range(rows):
            ob2[pl.ds(s * rows + r, ntx, stride=m2), :] = chosen[
                s * ntx : (s + 1) * ntx, r * BOX : (r + 1) * BOX
            ]
    exchange(ob2, ib2, m2, 1)

    here = me.astype(F32)
    for s in range(2):
        mine = (tile_col == here) & (slot_col == float(s))
        sinfo[pl.ds(s, 1), :] = jnp.sum(jnp.where(mine, infos, 0.0), axis=0, keepdims=True)
    sinfo[2:8, :] = jnp.zeros((6, BOX), F32)
    lane_f = lane_i.astype(F32)
    give = jnp.concatenate(
        [
            jnp.where((tile_col == lane_f) & (slot_col == float(s)), 1.0, 0.0)[:, 0:ntx]
            for s in range(2)
        ],
        axis=1,
    )
    own_slot = jnp.sum(
        jnp.where(row_i[:, 0:1] == me, slot_col[:, 0:1], 0.0), axis=0, keepdims=True
    )

    eye8 = iota((8, BOX), 0) == iota((8, BOX), 1)

    def tables(which, ref, live):
        for s in range(2):
            line = jnp.broadcast_to(ref[pl.ds(s, 1), :], (8, BOX))
            column = jnp.sum(jnp.where(eye8, line, 0.0), axis=1, keepdims=True)
            table = jnp.broadcast_to(column, (8, BOX)) * live
            boxes = jnp.broadcast_to(column[7:8], (8, BOX))
            for j in range(2):
                wtab[which, s, j] = jnp.where(boxes == float(j), table, 0.0)
                if which == 1:
                    mtab[s, j] = jnp.where(boxes == float(j), 1.0, 0.0)

    tables(1, sinfo, 1.0)
    for b in range(bands):
        band_tables(1, b)
    strip_tables(1)

    whole(ob2, ib2, m2, 1).wait_recv()
    for s in range(2):
        for r in range(rows):
            slots[s, pl.ds(r, ntx, stride=rows), :] = ib2[pl.ds(s * rows + r, ntx, stride=m2), :]

    waits = []
    for n, (src, dst, yy) in enumerate(
        (
            (slots.at[:, BOX - deep : BOX, :], nslots, south),
            (slots.at[:, 0:deep, :], sslots, north),
            (sinfo, ninfo, south),
            (sinfo, soinfo, north),
        )
    ):
        waits.append(send(src, dst, sl_sem.at[0, n], sl_sem.at[1, n], yy, me))

    sw1[...] = jnp.zeros_like(sw1)
    se1[...] = jnp.zeros_like(se1)
    for b in range(bands):
        for j in range(2):
            part = sum(wtab[1, s, j, pl.ds(b, 1), :] * slots[s] for s in range(2))
            model_e[b, deep : deep + BOX, j * BOX : (j + 1) * BOX] = part
            keep = of_band(tile_lane, b)
            shift = (reach * b) if j == 0 else (reach * b + reach) % BOX
            moved = pltpu.roll(part, shift, 1) if shift else part
            ref = (sw1, se1)[j]
            ref[...] = jnp.where(keep, moved, ref[...])
    for n, (src, dst, yy, xx) in enumerate(
        (
            (se1, west1.at[deep : deep + BOX], ti, east),
            (sw1, east1.at[deep : deep + BOX], ti, west),
            (se1.at[BOX - deep : BOX], west1.at[0:deep], south, east),
            (sw1.at[BOX - deep : BOX], east1.at[0:deep], south, west),
            (se1.at[0:deep], west1.at[deep + BOX : ext1], north, east),
            (sw1.at[0:deep], east1.at[deep + BOX : ext1], north, west),
        )
    ):
        waits.append(send(src, dst, sl_sem.at[0, 4 + n], sl_sem.at[1, 4 + n], yy, xx))

    def three(hi, lo, right_hi, right_lo):
        return dot(hi, right_hi) + (dot(hi, right_lo) + dot(lo, right_hi))

    def columns(st, b, image):
        hi, lo = split(image)
        return three(hi, lo, tcol[st, b, 0], tcol[st, b, 1])

    def along_rows(trow, b, image):
        hi, lo = split(image)
        return three(trow[b, 0], trow[b, 1], hi, lo)

    def own_columns(b, carry):
        mixed_e[b, deep : deep + BOX] = columns(0, b, model_e[b, deep : deep + BOX])
        return carry

    lax.fori_loop(0, bands, own_columns, 0)

    for copy in waits[0:4]:
        copy.wait_recv()
    tables(0, ninfo, jnp.where(ti > 0, 1.0, 0.0))
    tables(2, soinfo, jnp.where(ti < nty - 1, 1.0, 0.0))

    def outer_columns(b, carry):
        image = jnp.concatenate(
            [
                jnp.concatenate(
                    [
                        sum(wtab[which, s, j, pl.ds(b, 1), :] * ref[s] for s in range(2))
                        for j in range(2)
                    ],
                    axis=1,
                )
                for which, ref in ((0, nslots), (2, sslots))
            ],
            axis=0,
        )
        image = columns(0, b, image)
        mixed_e[b, 0:deep] = image[0:deep]
        mixed_e[b, deep + BOX : ext1] = image[deep:]
        return carry

    lax.fori_loop(0, bands, outer_columns, 0)

    load_obs.wait()
    load_iv.wait()
    for copy in images:
        copy.wait_recv()
    for copy in waits[4:]:
        copy.wait_recv()

    def halo_parts(left, right, count, edge):
        row = iota((count, BOX), 0)
        inner = ((row >= edge) | (ti > 0)) & ((row < count - edge) | (ti < nty - 1))
        for n, (ref, ok) in enumerate(((left, me > 0), (right, me < ntx - 1))):
            hi, lo = split(jnp.where(inner & ok, ref[...], 0.0))
            ext_h[0:count, n * BOX : (n + 1) * BOX] = hi
            ext_l[0:count, n * BOX : (n + 1) * BOX] = lo

    halo_parts(west1, east1, ext1, deep)
    pack[...] = three(ext_h[...], ext_l[...], diag[0, 0], diag[0, 1])
    sw2[...] = jnp.zeros_like(sw2)
    se2[...] = jnp.zeros_like(se2)
    row = iota((ext2, 2 * BOX), 0)
    inside = ((row >= HALO) | (ti > 0)) & ((row < HALO + BOX) | (ti < nty - 1))
    first_lanes = iota((ext1, BOX), 1) < reach
    last_lanes = iota((ext1, BOX), 1) >= BOX - reach

    def first(b, carry):
        left = pltpu.roll(pack[:, 0:BOX], lax.rem(BOX - reach * b, BOX), 1)
        left = mixed_e[b, :, 0:BOX] + jnp.where(first_lanes, left, 0.0)
        right = pltpu.roll(pack[:, BOX:], lax.rem(2 * BOX - reach - reach * b, BOX), 1)
        right = mixed_e[b, :, BOX:] + jnp.where(last_lanes, right, 0.0)
        predicted = along_rows(trow1, b, jnp.concatenate([left, right], axis=1))
        residual = jnp.where(inside, iv_e[b] * (obs_e[b] - predicted), 0.0)
        res_e[b] = residual
        image = along_rows(trow2, b, residual)
        back[b] = image
        keep = of_band(tile_lane, b)
        moved = pltpu.roll(image[:, 0:BOX], reach * b, 1)
        sw2[...] = jnp.where(keep, moved, sw2[...])
        moved = pltpu.roll(image[:, BOX:], lax.rem(reach * b + reach, BOX), 1)
        se2[...] = jnp.where(keep, moved, se2[...])
        return carry

    lax.fori_loop(0, bands, first, 0)
    strips = [
        send(se2, west2, st_sem.at[0, 0], st_sem.at[1, 0], ti, east),
        send(sw2, east2, st_sem.at[0, 1], st_sem.at[1, 1], ti, west),
    ]
    store = pltpu.make_async_copy(res_e.at[:, HALO : HALO + BOX, :], resid_hbm, loc_sem.at[5])
    store.start()

    for side in range(2):
        at = slice(side * BOX, (side + 1) * BOX)
        full = diag[1, 0, at, at].astype(F32) + diag[1, 1, at, at].astype(F32)
        fold = jnp.zeros((BOX, BOX), F32)
        for b in range(bands):
            here_lane = tile_lane if side == 0 else tile_lane - (BOX - reach)
            inside_lane = (here_lane >= 0) & (here_lane < reach)
            fold = jnp.where(inside_lane & (tile_row_i - reach * b == here_lane), 1.0, fold)
        fold = fold.astype(BF16)
        for s in range(2):
            weight = jnp.zeros((1, BOX), F32)
            for b in range(bands):
                weight = jnp.where(of_band(lane1, b), wtab[1, s, side, b : b + 1, :], weight)
            hi, lo = split(full * weight)
            hi, lo = split(dot(hi, fold) + dot(lo, fold))
            last[0, at, s * BOX : (s + 1) * BOX] = hi
            last[1, at, s * BOX : (s + 1) * BOX] = lo

    grads[...] = jnp.zeros_like(grads)

    def second(b, carry):
        gradient = columns(1, b, back[b])
        grad[b] = gradient
        halves = (gradient[:, 0:BOX], gradient[:, BOX:])
        for s in range(2):
            grads[s] += sum(wtab[1, s, j, pl.ds(b, 1), :] * halves[j] for j in range(2))
        return carry

    lax.fori_loop(0, bands, second, 0)
    for copy in strips:
        copy.wait_recv()
    for n, (ref, ok) in enumerate(((west2, me > 0), (east2, me < ntx - 1))):
        hi, lo = split(jnp.where(ok, ref[...], 0.0))
        ext_h[0:BOX, n * BOX : (n + 1) * BOX] = hi
        ext_l[0:BOX, n * BOX : (n + 1) * BOX] = lo
    share = three(ext_h[0:BOX], ext_l[0:BOX], last[0], last[1])
    for s in range(2):
        grads[s] += share[:, s * BOX : (s + 1) * BOX]

    for s in range(2):
        for r in range(rows):
            ob3[pl.ds(s * rows + r, ntx, stride=m2), :] = grads[s, pl.ds(r, ntx, stride=rows), :]
    exchange(ob3, ib3, m2, 2)
    edges[...] = three(ext_h[0:BOX], ext_l[0:BOX], diag[1, 0], diag[1, 1])
    sgacc[...] = jnp.zeros_like(sgacc)

    def spectra(b, carry):
        left = pltpu.roll(edges[:, 0:BOX], lax.rem(BOX - reach * b, BOX), 1)
        right = pltpu.roll(edges[:, BOX:], lax.rem(2 * BOX - reach - reach * b, BOX), 1)
        halves = (
            grad[b, :, 0:BOX] + jnp.where(tile_lane < reach, left, 0.0),
            grad[b, :, BOX:] + jnp.where(tile_lane >= BOX - reach, right, 0.0),
        )
        for s in range(2):
            under = sum(mtab[s, j, pl.ds(b, 1), :] * halves[j] for j in range(2))
            sgacc[s, pl.ds(b, 1), :] = jnp.sum(slots[s] * under, axis=0, keepdims=True)
        return carry

    lax.fori_loop(0, bands, spectra, 0)
    line = jnp.zeros((1, BOX), F32)
    for s in range(2):
        column = jnp.broadcast_to(jnp.sum(sgacc[s], axis=1, keepdims=True), (8, BOX))
        mark = iota((8, BOX), 1) == iota((8, BOX), 0) + 8 * s
        line = line + jnp.sum(jnp.where(mark, column, 0.0), axis=0, keepdims=True)
    sg_send[0] = line
    sg_in[me] = line

    for j in order:
        pltpu.make_async_remote_copy(
            sg_send.at[0], sg_in.at[me], send_sem.at[4], a2a_sem.at[4],
            device_id=(ti, wrapped(j)), device_id_type=MESH,
        ).start()

    whole(ob3, ib3, m2, 2).wait_recv()
    pieces = jnp.concatenate(
        [
            jnp.concatenate(
                [ib3[pl.ds(s * rows + r, ntx, stride=m2), :] for r in range(rows)], axis=1
            )
            for s in range(2)
        ],
        axis=0,
    )
    chosen = exact(give, pieces)
    for r in range(rows):
        ob4[pl.ds(r, ntx, stride=m4), :] = chosen[:, r * BOX : (r + 1) * BOX]
    exchange(ob4, ib4, m4, 3)

    square = jnp.sum(jnp.where(lane1 < bands, info * info, 0.0), axis=1, keepdims=True)
    step_morph = gamma_v[...] / square
    full = morph_v[...]
    norm = jnp.sum(jnp.sum(full * full, axis=0, keepdims=True), axis=1, keepdims=True)
    step_sed = gamma_v[...] / jnp.sqrt(norm)

    part = pl.ds(0, ntx - 1)
    seds = pltpu.make_async_remote_copy(
        sg_in.at[part], sg_in.at[part], send_sem.at[4], a2a_sem.at[4],
        device_id=(ti, east), device_id_type=MESH,
    )
    seds.wait_recv()
    terms = jnp.zeros((1, BOX), F32)
    for d in range(ntx):
        terms = terms + jnp.where(own_tile == float(d), sg_in[d], 0.0)
    terms = jnp.where(own_slot == 0.0, terms, pltpu.roll(terms, BOX - 8, 1))
    nsed_ref[0] = jnp.maximum(info + step_sed * terms, 0.0)[:, 0:bands]

    whole(ob4, ib4, m4, 3).wait_recv()
    for r in range(rows):
        at = pl.ds(r, ntx, stride=rows)
        update = step_morph * ib4[pl.ds(r, ntx, stride=m4), :]
        nmorph_ref[0, 0, at, :] = jnp.maximum(morph_v[at, :] + update, 0.0)

    whole(ob1, ib1, m1, 0).wait_send()
    whole(ob2, ib2, m2, 1).wait_send()
    whole(ob3, ib3, m2, 2).wait_send()
    whole(ob4, ib4, m4, 3).wait_send()
    seds.wait_send()
    for copy in images + waits + strips:
        copy.wait_send()
    store.wait()


def write_out(resid, morph, sed, resid_o, morph_o, sed_o, resid_v, morph_v, sed_v, in_sem, out_sem):
    bands = resid.shape[0]
    trips = [(resid.at[b], resid_v.at[b], resid_o.at[b]) for b in range(bands)]
    trips += [(morph, morph_v, morph_o), (sed, sed_v, sed_o)]
    loads = [pltpu.make_async_copy(a, v, in_sem.at[n]) for n, (a, v, _) in enumerate(trips)]
    stores = [pltpu.make_async_copy(v, o, out_sem.at[n]) for n, (_, v, o) in enumerate(trips)]
    for copy in loads:
        copy.start()
    for load, out in zip(loads, stores):
        load.wait()
        out.start()
    for copy in stores:
        copy.wait()


def solution(mesh):
    nty, ntx = mesh.shape["ty"], mesh.shape["tx"]

    def body(observed, inverse_variance, sed, morph, foot_block, gamma, row_kernel, col_kernel):
        bands, height, width = observed.shape
        taps = row_kernel.shape[1]
        rows = BOX // ntx
        m1, m2, m4 = up8(rows + 1), 2 * rows, up8(rows)
        deep = 2 * HALO
        ext1, ext2 = height + 2 * deep, height + 2 * HALO

        def vmem(*shape, dtype=F32):
            return pltpu.VMEM(shape, dtype)

        scratch = [
            vmem(bands, ext2, width), vmem(bands, ext2, width), vmem(bands, ext2, width),
            vmem(bands, ext1, width), vmem(bands, ext1, width),
            vmem(bands, height, width), vmem(bands, height, width),
            vmem(ext1, BOX), vmem(ext1, BOX), vmem(BOX, BOX), vmem(BOX, BOX),
            vmem(BOX, BOX), vmem(BOX, BOX), vmem(BOX, BOX), vmem(BOX, BOX),
            vmem(ext1, NAR), vmem(BOX, NAR),
            vmem(BOX, BOX), vmem(*sed.shape), vmem(1, 1, dtype=jnp.int32), vmem(1, 1), vmem(8, BOX),
            vmem(ntx * m1, BOX), vmem(ntx * m1, BOX), vmem(ntx * m2, BOX), vmem(ntx * m2, BOX),
            vmem(ntx * m2, BOX), vmem(ntx * m2, BOX), vmem(ntx * m4, BOX), vmem(ntx * m4, BOX),
            vmem(1, 1, BOX), vmem(ntx, 1, BOX),
            vmem(2, BOX, BOX), vmem(8, BOX), vmem(2, deep, BOX), vmem(2, deep, BOX),
            vmem(8, BOX), vmem(8, BOX), vmem(2, BOX, BOX), vmem(2, 8, BOX),
            vmem(3, 2, 2, 8, BOX), vmem(2, 2, 8, BOX),
            vmem(bands, taps), vmem(bands, taps),
            vmem(2, 2, 8, WIDE), vmem(2, 2, 8, NAR),
            vmem(2, bands, 2, NAR, NAR, dtype=BF16),
            vmem(bands, 2, ext2, ext1, dtype=BF16), vmem(bands, 2, BOX, ext2, dtype=BF16),
            vmem(2, 2, NAR, NAR, dtype=BF16), vmem(2, NAR, NAR, dtype=BF16),
            vmem(ext1, NAR, dtype=BF16), vmem(ext1, NAR, dtype=BF16),
            pltpu.SemaphoreType.DMA((9,)), pltpu.SemaphoreType.DMA((5,)),
            pltpu.SemaphoreType.DMA((5,)), pltpu.SemaphoreType.DMA((2, 4)),
            pltpu.SemaphoreType.DMA((2, 10)), pltpu.SemaphoreType.DMA((2, 2)),
        ]
        anywhere = pl.BlockSpec(memory_space=pl.ANY)
        vector = pl.BlockSpec(memory_space=pltpu.VMEM)
        shapes = tuple(
            jax.ShapeDtypeStruct(a.shape, F32) for a in (observed, morph, sed)
        )
        results = pl.pallas_call(
            functools.partial(kernel, nty, ntx, bands, taps),
            out_shape=shapes,
            in_specs=[pl.BlockSpec(memory_space=pltpu.HBM)] * 8,
            out_specs=(anywhere, vector, vector),
            scratch_shapes=scratch,
            compiler_params=pltpu.CompilerParams(collective_id=0, has_side_effects=True),
        )(observed, inverse_variance, sed, morph, foot_block, gamma, row_kernel, col_kernel)
        return pl.pallas_call(
            write_out,
            out_shape=shapes,
            in_specs=[anywhere] * 3,
            out_specs=(anywhere,) * 3,
            scratch_shapes=[
                vmem(bands, height, width), vmem(*morph.shape), vmem(*sed.shape),
                pltpu.SemaphoreType.DMA((bands + 2,)), pltpu.SemaphoreType.DMA((bands + 2,)),
            ],
        )(*results)

    in_specs = (
        P(None, "ty", "tx"),
        P(None, "ty", "tx"),
        P("ty", "tx", None),
        P("ty", "tx", None, None),
        P("ty", "tx"),
        P("ty", "tx"),
        P(),
        P(),
    )
    out_specs = (P(None, "ty", "tx"), P("ty", "tx", None, None), P("ty", "tx", None))
    return jax.shard_map(body, mesh=mesh, in_specs=in_specs, out_specs=out_specs, check_vma=False)
```

```python
import functools

import jax
import jax.numpy as jnp
from jax import lax
from jax.experimental import pallas as pl
from jax.experimental.pallas import tpu as pltpu
from jax.sharding import PartitionSpec as P

MESH = pl.DeviceIdType.MESH
F32 = jnp.float32
BF16 = jnp.bfloat16
HIGHEST = lax.Precision.HIGHEST
BOX = 128
HALO = 24
WIDE = 384
NAR = 256


def iota(shape, dim):
    return lax.broadcasted_iota(jnp.int32, shape, dim)


def split(x):
    hi = x.astype(BF16)
    return hi, (x - hi.astype(F32)).astype(BF16)


def dot(a, b):
    return jnp.dot(a, b, preferred_element_type=F32)


def exact(a, b):
    return jnp.dot(a, b, preferred_element_type=F32, precision=HIGHEST)


def kernel(
    nty, ntx, bands, taps,
    obs_hbm, iv_hbm, sed_hbm, morph_hbm, foot_hbm, gamma_hbm, rk_hbm, ck_hbm,
    resid_ref, nmorph_ref, nsed_ref,
    obs_e, iv_e, model_e, mixed_e, back, grad,
    west1, east1, west2, east2, sw1, se1, sw2, se2, pack, edges,
    morph_v, sed_v, foot_v, gamma_v, info_v, info_send, info_in,
    ob1, ib1, ob2, ib2, ob3, ib3, ob4, ib4, sg_send, sg_in,
    slots, sinfo, nslots, sslots, ninfo, soinfo, grads, sgacc,
    wtab, mtab, rk_v, ck_v, ktab_c, ktab_r, tcol, trow1, trow2, diag, last, ext_h, ext_l,
    loc_sem, send_sem, a2a_sem, obs_sem, sl_sem, st_sem,
):
    ti = lax.axis_index("ty")
    me = lax.axis_index("tx")
    reach = (taps - 1) // 2
    rows = BOX // ntx
    deep = 2 * HALO
    ext1, ext2 = BOX + 2 * deep, BOX + 2 * HALO
    north, south = lax.rem(ti + nty - 1, nty), lax.rem(ti + 1, nty)
    west, east = lax.rem(me + ntx - 1, ntx), lax.rem(me + 1, ntx)

    barrier = pltpu.get_barrier_semaphore()

    def wrapped(j):
        p = me + j
        return jnp.where(p >= ntx, p - ntx, p)

    order = sorted(range(1, ntx), key=lambda j: -min(j, ntx - j))
    for j in order:
        pl.semaphore_signal(barrier, inc=1, device_id=(ti, wrapped(j)), device_id_type=MESH)
    for yy in (north, south):
        for xx in (me, west, east):
            pl.semaphore_signal(barrier, inc=1, device_id=(yy, xx), device_id_type=MESH)

    load_morph = pltpu.make_async_copy(morph_hbm.at[0, 0], morph_v, loc_sem.at[0])
    load_rk = pltpu.make_async_copy(rk_hbm, rk_v, loc_sem.at[1])
    load_ck = pltpu.make_async_copy(ck_hbm, ck_v, loc_sem.at[2])
    load_obs = pltpu.make_async_copy(obs_hbm, obs_e.at[:, HALO : HALO + BOX, :], loc_sem.at[3])
    load_iv = pltpu.make_async_copy(iv_hbm, iv_e.at[:, HALO : HALO + BOX, :], loc_sem.at[4])
    scalars = [
        pltpu.make_async_copy(src, dst, loc_sem.at[6 + n])
        for n, (src, dst) in enumerate(((sed_hbm, sed_v), (foot_hbm, foot_v), (gamma_hbm, gamma_v)))
    ]
    for copy in scalars:
        copy.start()
    load_morph.start()
    load_rk.start()
    load_ck.start()
    load_obs.start()
    load_iv.start()

    lane1 = iota((1, BOX), 1)
    info_v[...] = jnp.zeros_like(info_v)
    for copy in scalars:
        copy.wait()
    tile = foot_v[...] // 2
    box = foot_v[...] - 2 * tile
    info_v[0:1, 0:bands] = sed_v[0]
    info = info_v[0:1, :]
    own_tile = tile.astype(F32)
    info = jnp.where(lane1 == 6, own_tile, info)
    info = jnp.where(lane1 == 7, box.astype(F32), info)
    info_send[0] = info
    load_morph.wait()
    for r in range(rows):
        ob1[:, r, :] = morph_v[pl.ds(r, ntx, stride=rows), :]

    def copy_to(src, dst, phase, p):
        return pltpu.make_async_remote_copy(
            src, dst, send_sem.at[phase], a2a_sem.at[phase],
            device_id=(ti, p), device_id_type=MESH,
        )

    def exchange(out, arrived, phase):
        for j in order:
            copy_to(out.at[wrapped(j)], arrived.at[me], phase, wrapped(j)).start()
        arrived[me] = out[me]

    def spread(out, arrived, phase):
        for j in order:
            copy_to(out.at[0], arrived.at[me], phase, wrapped(j)).start()
        arrived[me] = out[0]

    def whole(arrived, phase):
        part = arrived.at[pl.ds(0, ntx - 1)]
        return copy_to(part, part, phase, east)

    pl.semaphore_wait(barrier, ntx - 1 + 6)
    spread(info_send, info_in, 5)
    exchange(ob1, ib1, 0)

    def send(src, dst, s_sem, r_sem, yy, xx):
        copy = pltpu.make_async_remote_copy(
            src, dst, s_sem, r_sem, device_id=(yy, xx), device_id_type=MESH
        )
        copy.start()
        return copy

    low, high = slice(0, HALO), slice(BOX - HALO, BOX)
    far = slice(HALO + BOX, ext2)
    images = []
    for n, (src, dst) in enumerate(((obs_hbm, obs_e), (iv_hbm, iv_e))):
        images.append(send(src.at[:, high, :], dst.at[:, low, :], obs_sem.at[0, 2 * n], obs_sem.at[1, 2 * n], south, me))
        images.append(send(src.at[:, low, :], dst.at[:, far, :], obs_sem.at[0, 2 * n + 1], obs_sem.at[1, 2 * n + 1], north, me))

    load_rk.wait()
    load_ck.wait()
    flip = (iota((BOX, BOX), 0) + iota((BOX, BOX), 1) == taps - 1).astype(F32)

    for table, values, forward in ((ktab_c, ck_v, 0), (ktab_r, rk_v, 1)):
        table[...] = jnp.zeros_like(table)
        table[forward, 0, 0:bands, 0:taps] = values[...]
        plain = table[forward, 0, :, 0:BOX]
        table[1 - forward, 0, :, 0:BOX] = exact(plain, flip)
        for st in range(2):
            full = table[st, 0, :, 0:BOX]
            hi = full.astype(BF16).astype(F32)
            table[st, 0, :, 0:BOX] = hi
            table[st, 1, :, 0:BOX] = full - hi

    def band_tables(st, b):
        for part in range(2):
            spread = jnp.broadcast_to(ktab_c[st, part, pl.ds(b, 1), :], (BOX, WIDE))
            skew = pltpu.roll(spread, 0, 1, stride=1, stride_axis=0)
            for n in range(2):
                own = pltpu.roll(skew, (WIDE - reach + n * BOX) % WIDE, 1)[:, 0:NAR]
                tcol[st, b, part, n * BOX : (n + 1) * BOX, :] = own.astype(BF16)
            spread = jnp.broadcast_to(ktab_r[st, part, pl.ds(b, 1), :], (BOX, NAR))
            skew = pltpu.roll(spread, 0, 1, stride=1, stride_axis=0)
            out, trow = ((ext2, trow1), (BOX, trow2))[st]
            for n in range(0, out, BOX):
                count = min(BOX, out - n)
                own = pltpu.roll(skew, (HALO - reach + n) % NAR, 1)
                trow[b, part, n : n + count] = own[0:count, 0 : trow.shape[3]].astype(BF16)

    tile_row_i, tile_lane = iota((BOX, BOX), 0), iota((BOX, BOX), 1)

    def of_band(index, b):
        return (index >= reach * b) & (index < reach * b + reach)

    def strip_tables(st):
        together = tile_row_i < 0
        for b in range(bands):
            together = together | (of_band(tile_row_i, b) & of_band(tile_lane, b))
        rows_i = iota((BOX, WIDE), 0)
        for part in range(2):
            spread = jnp.zeros((BOX, WIDE), F32)
            for b in range(bands):
                line = jnp.broadcast_to(ktab_c[st, part, b : b + 1, :], (BOX, WIDE))
                spread = jnp.where(of_band(rows_i, b), line, spread)
            skew = pltpu.roll(spread, 0, 1, stride=1, stride_axis=0)
            left = pltpu.roll(skew, WIDE - 2 * reach, 1)
            empty = jnp.zeros((BOX, BOX), BF16)
            for n, values in enumerate((left, skew)):
                block = jnp.where(together, values[:, 0:BOX], 0.0).astype(BF16)
                at = slice(n * BOX, (n + 1) * BOX)
                diag[st, part, at, at] = block
                diag[st, part, at, slice((1 - n) * BOX, (2 - n) * BOX)] = empty

    for b in range(bands):
        band_tables(0, b)
    strip_tables(0)

    whole(info_in, 5).wait_recv()
    whole(ib1, 0).wait_recv()
    infos = info_in[:, 0, :]
    wide = (ntx, BOX)
    row_i, lane_i = iota(wide, 0), iota(wide, 1)
    tile_col = jnp.broadcast_to(infos[:, 6:7], wide)
    tile_row = jnp.sum(jnp.where(row_i == lane_i, tile_col, 0.0), axis=0, keepdims=True)
    tile_row = jnp.broadcast_to(jnp.where(lane1 < ntx, tile_row, -1.0), wide)
    same = tile_col == tile_row
    slot_row = jnp.sum(jnp.where(same & (row_i < lane_i), 1.0, 0.0), axis=0, keepdims=True)
    slot_row = jnp.broadcast_to(slot_row, wide)
    slot_col = jnp.sum(jnp.where(same & (lane_i < row_i), 1.0, 0.0), axis=1, keepdims=True)
    slot_col = jnp.broadcast_to(slot_col, wide)
    target = row_i.astype(F32)
    pick = [
        jnp.where((tile_row == target) & (slot_row == float(s)), 1.0, 0.0)[:, 0:ntx]
        for s in range(2)
    ]
    pieces = jnp.concatenate([ib1[:, r, :] for r in range(rows)], axis=1)
    chosen = exact(jnp.concatenate(pick, axis=0), pieces)
    for s in range(2):
        for r in range(rows):
            ob2[:, s * rows + r, :] = chosen[
                s * ntx : (s + 1) * ntx, r * BOX : (r + 1) * BOX
            ]
    exchange(ob2, ib2, 1)

    here = me.astype(F32)
    for s in range(2):
        mine = (tile_col == here) & (slot_col == float(s))
        sinfo[pl.ds(s, 1), :] = jnp.sum(jnp.where(mine, infos, 0.0), axis=0, keepdims=True)
    sinfo[2:8, :] = jnp.zeros((6, BOX), F32)
    lane_f = lane_i.astype(F32)
    give = jnp.concatenate(
        [
            jnp.where((tile_col == lane_f) & (slot_col == float(s)), 1.0, 0.0)[:, 0:ntx]
            for s in range(2)
        ],
        axis=1,
    )
    own_slot = jnp.sum(
        jnp.where(row_i[:, 0:1] == me, slot_col[:, 0:1], 0.0), axis=0, keepdims=True
    )

    eye8 = iota((8, BOX), 0) == iota((8, BOX), 1)

    def tables(which, ref, live):
        for s in range(2):
            line = jnp.broadcast_to(ref[pl.ds(s, 1), :], (8, BOX))
            column = jnp.sum(jnp.where(eye8, line, 0.0), axis=1, keepdims=True)
            table = jnp.broadcast_to(column, (8, BOX)) * live
            boxes = jnp.broadcast_to(column[7:8], (8, BOX))
            for j in range(2):
                wtab[which, s, j] = jnp.where(boxes == float(j), table, 0.0)
                if which == 1:
                    mtab[s, j] = jnp.where(boxes == float(j), 1.0, 0.0)

    tables(1, sinfo, 1.0)
    for b in range(bands):
        band_tables(1, b)
    strip_tables(1)

    whole(ib2, 1).wait_recv()
    for s in range(2):
        for r in range(rows):
            slots[s, pl.ds(r, ntx, stride=rows), :] = ib2[:, s * rows + r, :]

    waits = []
    for n, (src, dst, yy) in enumerate(
        (
            (slots.at[:, BOX - deep : BOX, :], nslots, south),
            (slots.at[:, 0:deep, :], sslots, north),
            (sinfo, ninfo, south),
            (sinfo, soinfo, north),
        )
    ):
        waits.append(send(src, dst, sl_sem.at[0, n], sl_sem.at[1, n], yy, me))

    sw1[...] = jnp.zeros_like(sw1)
    se1[...] = jnp.zeros_like(se1)
    for b in range(bands):
        for j in range(2):
            part = sum(wtab[1, s, j, pl.ds(b, 1), :] * slots[s] for s in range(2))
            model_e[b, deep : deep + BOX, j * BOX : (j + 1) * BOX] = part
            keep = of_band(tile_lane, b)
            shift = (reach * b) if j == 0 else (reach * b + reach) % BOX
            moved = pltpu.roll(part, shift, 1) if shift else part
            ref = (sw1, se1)[j]
            ref[...] = jnp.where(keep, moved, ref[...])
    for n, (src, dst, yy, xx) in enumerate(
        (
            (se1, west1.at[deep : deep + BOX], ti, east),
            (sw1, east1.at[deep : deep + BOX], ti, west),
            (se1.at[BOX - deep : BOX], west1.at[0:deep], south, east),
            (sw1.at[BOX - deep : BOX], east1.at[0:deep], south, west),
            (se1.at[0:deep], west1.at[deep + BOX : ext1], north, east),
            (sw1.at[0:deep], east1.at[deep + BOX : ext1], north, west),
        )
    ):
        waits.append(send(src, dst, sl_sem.at[0, 4 + n], sl_sem.at[1, 4 + n], yy, xx))

    def three(hi, lo, right_hi, right_lo):
        return dot(hi, right_hi) + (dot(hi, right_lo) + dot(lo, right_hi))

    def columns(st, b, image):
        hi, lo = split(image)
        return three(hi, lo, tcol[st, b, 0], tcol[st, b, 1])

    def along_rows(trow, b, image):
        hi, lo = split(image)
        count, depth = trow.shape[2:]
        both = dot(trow[b].reshape(2 * count, depth), hi)
        return both[:count] + (both[count:] + dot(trow[b, 0], lo))

    for b in range(bands):
        mixed_e[b, deep : deep + BOX] = columns(0, b, model_e[b, deep : deep + BOX])

    for copy in waits[0:4]:
        copy.wait_recv()
    tables(0, ninfo, jnp.where(ti > 0, 1.0, 0.0))
    tables(2, soinfo, jnp.where(ti < nty - 1, 1.0, 0.0))

    for b in range(bands):
        image = jnp.concatenate(
            [
                jnp.concatenate(
                    [
                        sum(wtab[which, s, j, pl.ds(b, 1), :] * ref[s] for s in range(2))
                        for j in range(2)
                    ],
                    axis=1,
                )
                for which, ref in ((0, nslots), (2, sslots))
            ],
            axis=0,
        )
        image = columns(0, b, image)
        mixed_e[b, 0:deep] = image[0:deep]
        mixed_e[b, deep + BOX : ext1] = image[deep:]

    load_obs.wait()
    load_iv.wait()
    for copy in images:
        copy.wait_recv()
    for copy in waits[4:]:
        copy.wait_recv()

    def halo_parts(left, right, count, edge):
        row = iota((count, BOX), 0)
        inner = ((row >= edge) | (ti > 0)) & ((row < count - edge) | (ti < nty - 1))
        for n, (ref, ok) in enumerate(((left, me > 0), (right, me < ntx - 1))):
            hi, lo = split(jnp.where(inner & ok, ref[...], 0.0))
            ext_h[0:count, n * BOX : (n + 1) * BOX] = hi
            ext_l[0:count, n * BOX : (n + 1) * BOX] = lo

    halo_parts(west1, east1, ext1, deep)
    pack[...] = three(ext_h[...], ext_l[...], diag[0, 0], diag[0, 1])
    row = iota((ext2, 2 * BOX), 0)
    inside = ((row >= HALO) | (ti > 0)) & ((row < HALO + BOX) | (ti < nty - 1))
    first_lanes = iota((ext1, BOX), 1) < reach
    last_lanes = iota((ext1, BOX), 1) >= BOX - reach

    to_west = to_east = jnp.zeros((BOX, BOX), F32)
    for b in range(bands):
        left = pltpu.roll(pack[:, 0:BOX], (BOX - reach * b) % BOX, 1)
        left = mixed_e[b, :, 0:BOX] + jnp.where(first_lanes, left, 0.0)
        right = pltpu.roll(pack[:, BOX:], (2 * BOX - reach - reach * b) % BOX, 1)
        right = mixed_e[b, :, BOX:] + jnp.where(last_lanes, right, 0.0)
        predicted = along_rows(trow1, b, jnp.concatenate([left, right], axis=1))
        residual = jnp.where(inside, iv_e[b] * (obs_e[b] - predicted), 0.0)
        resid_ref[b] = residual[HALO : HALO + BOX]
        image = along_rows(trow2, b, residual)
        back[b] = image
        keep = of_band(tile_lane, b)
        to_west = jnp.where(keep, pltpu.roll(image[:, 0:BOX], reach * b, 1), to_west)
        moved = pltpu.roll(image[:, BOX:], (reach * b + reach) % BOX, 1)
        to_east = jnp.where(keep, moved, to_east)
    sw2[...] = to_west
    se2[...] = to_east
    strips = [
        send(se2, west2, st_sem.at[0, 0], st_sem.at[1, 0], ti, east),
        send(sw2, east2, st_sem.at[0, 1], st_sem.at[1, 1], ti, west),
    ]
    for side in range(2):
        at = slice(side * BOX, (side + 1) * BOX)
        full = diag[1, 0, at, at].astype(F32) + diag[1, 1, at, at].astype(F32)
        fold = jnp.zeros((BOX, BOX), F32)
        for b in range(bands):
            here_lane = tile_lane if side == 0 else tile_lane - (BOX - reach)
            inside_lane = (here_lane >= 0) & (here_lane < reach)
            fold = jnp.where(inside_lane & (tile_row_i - reach * b == here_lane), 1.0, fold)
        fold = fold.astype(BF16)
        for s in range(2):
            weight = jnp.zeros((1, BOX), F32)
            for b in range(bands):
                weight = jnp.where(of_band(lane1, b), wtab[1, s, side, b : b + 1, :], weight)
            hi, lo = split(full * weight)
            hi, lo = split(dot(hi, fold) + dot(lo, fold))
            last[0, at, s * BOX : (s + 1) * BOX] = hi
            last[1, at, s * BOX : (s + 1) * BOX] = lo

    totals = [jnp.zeros((BOX, BOX), F32) for _ in range(2)]
    for b in range(bands):
        gradient = columns(1, b, back[b])
        grad[b] = gradient
        halves = (gradient[:, 0:BOX], gradient[:, BOX:])
        for s in range(2):
            for j in range(2):
                totals[s] = totals[s] + wtab[1, s, j, b : b + 1, :] * halves[j]
    for s in range(2):
        grads[s] = totals[s]
    for copy in strips:
        copy.wait_recv()
    for n, (ref, ok) in enumerate(((west2, me > 0), (east2, me < ntx - 1))):
        hi, lo = split(jnp.where(ok, ref[...], 0.0))
        ext_h[0:BOX, n * BOX : (n + 1) * BOX] = hi
        ext_l[0:BOX, n * BOX : (n + 1) * BOX] = lo
    share = three(ext_h[0:BOX], ext_l[0:BOX], last[0], last[1])
    for s in range(2):
        grads[s] += share[:, s * BOX : (s + 1) * BOX]

    for s in range(2):
        for r in range(rows):
            ob3[:, s * rows + r, :] = grads[s, pl.ds(r, ntx, stride=rows), :]
    exchange(ob3, ib3, 2)
    edges[...] = three(ext_h[0:BOX], ext_l[0:BOX], diag[1, 0], diag[1, 1])
    sgacc[...] = jnp.zeros_like(sgacc)

    def spectra(b, carry):
        left = pltpu.roll(edges[:, 0:BOX], lax.rem(BOX - reach * b, BOX), 1)
        right = pltpu.roll(edges[:, BOX:], lax.rem(2 * BOX - reach - reach * b, BOX), 1)
        halves = (
            grad[b, :, 0:BOX] + jnp.where(tile_lane < reach, left, 0.0),
            grad[b, :, BOX:] + jnp.where(tile_lane >= BOX - reach, right, 0.0),
        )
        for s in range(2):
            under = sum(mtab[s, j, pl.ds(b, 1), :] * halves[j] for j in range(2))
            sgacc[s, pl.ds(b, 1), :] = jnp.sum(slots[s] * under, axis=0, keepdims=True)
        return carry

    lax.fori_loop(0, bands, spectra, 0)
    line = jnp.zeros((1, BOX), F32)
    for s in range(2):
        column = jnp.broadcast_to(jnp.sum(sgacc[s], axis=1, keepdims=True), (8, BOX))
        mark = iota((8, BOX), 1) == iota((8, BOX), 0) + 8 * s
        line = line + jnp.sum(jnp.where(mark, column, 0.0), axis=0, keepdims=True)
    sg_send[0] = line
    spread(sg_send, sg_in, 4)

    whole(ib3, 2).wait_recv()
    pieces = jnp.concatenate(
        [
            jnp.concatenate(
                [ib3[:, s * rows + r, :] for r in range(rows)], axis=1
            )
            for s in range(2)
        ],
        axis=0,
    )
    chosen = exact(give, pieces)
    for r in range(rows):
        ob4[:, r, :] = chosen[:, r * BOX : (r + 1) * BOX]
    exchange(ob4, ib4, 3)

    square = jnp.sum(jnp.where(lane1 < bands, info * info, 0.0), axis=1, keepdims=True)
    step_morph = gamma_v[...] / square
    full = morph_v[...]
    norm = jnp.sum(jnp.sum(full * full, axis=0, keepdims=True), axis=1, keepdims=True)
    step_sed = gamma_v[...] / jnp.sqrt(norm)

    whole(sg_in, 4).wait_recv()
    terms = jnp.zeros((1, BOX), F32)
    for d in range(ntx):
        terms = terms + jnp.where(own_tile == float(d), sg_in[d], 0.0)
    terms = jnp.where(own_slot == 0.0, terms, pltpu.roll(terms, BOX - 8, 1))
    nsed_ref[0] = jnp.maximum(info + step_sed * terms, 0.0)[:, 0:bands]

    whole(ib4, 3).wait_recv()
    for r in range(rows):
        at = pl.ds(r, ntx, stride=rows)
        update = step_morph * ib4[:, r, :]
        nmorph_ref[0, 0, at, :] = jnp.maximum(morph_v[at, :] + update, 0.0)

    for phase, arrived in enumerate((ib1, ib2, ib3, ib4, sg_in, info_in)):
        whole(arrived, phase).wait_send()
    for copy in images + waits + strips:
        copy.wait_send()


def write_out(resid, morph, sed, resid_o, morph_o, sed_o, sem):
    pairs = ((resid, resid_o), (morph, morph_o), (sed, sed_o))
    stores = [pltpu.make_async_copy(a, o, sem.at[n]) for n, (a, o) in enumerate(pairs)]
    for copy in stores:
        copy.start()
    for copy in stores:
        copy.wait()


def solution(mesh):
    nty, ntx = mesh.shape["ty"], mesh.shape["tx"]

    def body(observed, inverse_variance, sed, morph, foot_block, gamma, row_kernel, col_kernel):
        bands, height, width = observed.shape
        taps = row_kernel.shape[1]
        rows = BOX // ntx
        deep = 2 * HALO
        ext1, ext2 = height + 2 * deep, height + 2 * HALO

        def vmem(*shape, dtype=F32):
            return pltpu.VMEM(shape, dtype)

        scratch = [
            vmem(bands, ext2, width), vmem(bands, ext2, width),
            vmem(bands, ext1, width), vmem(bands, ext1, width),
            vmem(bands, height, width), vmem(bands, height, width),
            vmem(ext1, BOX), vmem(ext1, BOX), vmem(BOX, BOX), vmem(BOX, BOX),
            vmem(BOX, BOX), vmem(BOX, BOX), vmem(BOX, BOX), vmem(BOX, BOX),
            vmem(ext1, NAR), vmem(BOX, NAR),
            vmem(BOX, BOX), vmem(*sed.shape), vmem(1, 1, dtype=jnp.int32), vmem(1, 1), vmem(8, BOX),
            vmem(1, 1, BOX), vmem(ntx, 1, BOX),
            vmem(ntx, rows, BOX), vmem(ntx, rows, BOX),
            vmem(ntx, 2 * rows, BOX), vmem(ntx, 2 * rows, BOX),
            vmem(ntx, 2 * rows, BOX), vmem(ntx, 2 * rows, BOX),
            vmem(ntx, rows, BOX), vmem(ntx, rows, BOX),
            vmem(1, 1, BOX), vmem(ntx, 1, BOX),
            vmem(2, BOX, BOX), vmem(8, BOX), vmem(2, deep, BOX), vmem(2, deep, BOX),
            vmem(8, BOX), vmem(8, BOX), vmem(2, BOX, BOX), vmem(2, 8, BOX),
            vmem(3, 2, 2, 8, BOX), vmem(2, 2, 8, BOX),
            vmem(bands, taps), vmem(bands, taps),
            vmem(2, 2, 8, WIDE), vmem(2, 2, 8, NAR),
            vmem(2, bands, 2, NAR, NAR, dtype=BF16),
            vmem(bands, 2, ext2, ext1, dtype=BF16), vmem(bands, 2, BOX, ext2, dtype=BF16),
            vmem(2, 2, NAR, NAR, dtype=BF16), vmem(2, NAR, NAR, dtype=BF16),
            vmem(ext1, NAR, dtype=BF16), vmem(ext1, NAR, dtype=BF16),
            pltpu.SemaphoreType.DMA((9,)), pltpu.SemaphoreType.DMA((6,)),
            pltpu.SemaphoreType.DMA((6,)), pltpu.SemaphoreType.DMA((2, 4)),
            pltpu.SemaphoreType.DMA((2, 10)), pltpu.SemaphoreType.DMA((2, 2)),
        ]
        anywhere = pl.BlockSpec(memory_space=pl.ANY)
        vector = pl.BlockSpec(memory_space=pltpu.VMEM)
        shapes = tuple(
            jax.ShapeDtypeStruct(a.shape, F32) for a in (observed, morph, sed)
        )
        operands = (
            observed, inverse_variance, sed, morph, foot_block, gamma, row_kernel, col_kernel
        )
        results = pl.pallas_call(
            functools.partial(kernel, nty, ntx, bands, taps),
            out_shape=shapes,
            in_specs=[pl.BlockSpec(memory_space=pltpu.HBM)] * 8,
            out_specs=(vector, vector, vector),
            scratch_shapes=scratch,
            compiler_params=pltpu.CompilerParams(
                collective_id=0, has_side_effects=True, vmem_limit_bytes=40 * 2**20
            ),
        )(*(a if a.size == 1 else pltpu.with_memory_space_constraint(a, pltpu.HBM) for a in operands))
        return pl.pallas_call(
            write_out,
            out_shape=shapes,
            in_specs=[vector] * 3,
            out_specs=(anywhere,) * 3,
            scratch_shapes=[pltpu.SemaphoreType.DMA((3,))],
            compiler_params=pltpu.CompilerParams(vmem_limit_bytes=8 * 2**20),
        )(*results)

    in_specs = (
        P(None, "ty", "tx"),
        P(None, "ty", "tx"),
        P("ty", "tx", None),
        P("ty", "tx", None, None),
        P("ty", "tx"),
        P("ty", "tx"),
        P(),
        P(),
    )
    out_specs = (P(None, "ty", "tx"), P("ty", "tx", None, None), P("ty", "tx", None))
    return jax.shard_map(body, mesh=mesh, in_specs=in_specs, out_specs=out_specs, check_vma=False)
```

```python
import functools

import jax
import jax.numpy as jnp
from jax import lax
from jax.experimental import pallas as pl
from jax.experimental.pallas import tpu as pltpu
from jax.sharding import PartitionSpec as P

MESH = pl.DeviceIdType.MESH
F32 = jnp.float32
BF16 = jnp.bfloat16
HIGHEST = lax.Precision.HIGHEST
BOX = 128
HALO = 24
WIDE = 384
NAR = 256


def iota(shape, dim):
    return lax.broadcasted_iota(jnp.int32, shape, dim)


def split(x):
    hi = x.astype(BF16)
    return hi, (x - hi.astype(F32)).astype(BF16)


def dot(a, b):
    return jnp.dot(a, b, preferred_element_type=F32)


def exact(a, b):
    return jnp.dot(a, b, preferred_element_type=F32, precision=HIGHEST)


def gather(pick, x):
    hi = x.astype(BF16)
    rest = x - hi.astype(F32)
    mid = rest.astype(BF16)
    low = (rest - mid.astype(F32)).astype(BF16)
    pick = pick.astype(BF16)
    return (dot(pick, hi) + dot(pick, mid)) + dot(pick, low)


def kernel(
    nty, ntx, bands, taps,
    obs_hbm, iv_hbm, sed_hbm, morph_hbm, foot_hbm, gamma_hbm, rk_hbm, ck_hbm,
    resid_ref, nmorph_ref, nsed_ref,
    obs_e, iv_e, model_e, mixed_e, back, grad,
    west1, east1, west2, east2, sw1, se1, sw2, se2, pack, edges,
    morph_v, sed_v, foot_v, gamma_v, info_v, info_send, info_in,
    ob1, ib1, ob2, ib2, ob3, ib3, ob4, ib4, sg_send, sg_in,
    slots, sinfo, nslots, sslots, ninfo, soinfo, grads, sgacc,
    wtab, mtab, rk_v, ck_v, ktab_c, ktab_r, tcol, trow1, trow2, diag, last, ext_h, ext_l,
    loc_sem, send_sem, a2a_sem, obs_sem, sl_sem, st_sem,
):
    ti = lax.axis_index("ty")
    me = lax.axis_index("tx")
    reach = (taps - 1) // 2
    rows = BOX // ntx
    deep = 2 * HALO
    ext1, ext2 = BOX + 2 * deep, BOX + 2 * HALO
    north, south = lax.rem(ti + nty - 1, nty), lax.rem(ti + 1, nty)
    west, east = lax.rem(me + ntx - 1, ntx), lax.rem(me + 1, ntx)

    barrier = pltpu.get_barrier_semaphore()

    def wrapped(j):
        p = me + j
        return jnp.where(p >= ntx, p - ntx, p)

    order = sorted(range(1, ntx), key=lambda j: -min(j, ntx - j))
    for j in order:
        pl.semaphore_signal(barrier, inc=1, device_id=(ti, wrapped(j)), device_id_type=MESH)
    for yy in (north, south):
        for xx in (me, west, east):
            pl.semaphore_signal(barrier, inc=1, device_id=(yy, xx), device_id_type=MESH)

    load_morph = pltpu.make_async_copy(morph_hbm.at[0, 0], morph_v, loc_sem.at[0])
    load_rk = pltpu.make_async_copy(rk_hbm, rk_v, loc_sem.at[1])
    load_ck = pltpu.make_async_copy(ck_hbm, ck_v, loc_sem.at[2])
    load_obs = pltpu.make_async_copy(obs_hbm, obs_e.at[:, HALO : HALO + BOX, :], loc_sem.at[3])
    load_iv = pltpu.make_async_copy(iv_hbm, iv_e.at[:, HALO : HALO + BOX, :], loc_sem.at[4])
    scalars = [
        pltpu.make_async_copy(src, dst, loc_sem.at[6 + n])
        for n, (src, dst) in enumerate(((sed_hbm, sed_v), (foot_hbm, foot_v), (gamma_hbm, gamma_v)))
    ]
    for copy in scalars:
        copy.start()
    load_morph.start()
    load_rk.start()
    load_ck.start()
    load_obs.start()
    load_iv.start()

    lane1 = iota((1, BOX), 1)
    info_v[...] = jnp.zeros_like(info_v)
    for copy in scalars:
        copy.wait()
    tile = foot_v[...] // 2
    box = foot_v[...] - 2 * tile
    info_v[0:1, 0:bands] = sed_v[0]
    info = info_v[0:1, :]
    own_tile = tile.astype(F32)
    info = jnp.where(lane1 == 6, own_tile, info)
    info = jnp.where(lane1 == 7, box.astype(F32), info)
    info_send[0] = info
    load_morph.wait()
    for r in range(rows):
        ob1[:, r, :] = morph_v[pl.ds(r, ntx, stride=rows), :]

    def copy_to(src, dst, phase, p):
        return pltpu.make_async_remote_copy(
            src, dst, send_sem.at[phase], a2a_sem.at[phase],
            device_id=(ti, p), device_id_type=MESH,
        )

    def exchange(out, arrived, phase):
        for j in order:
            copy_to(out.at[wrapped(j)], arrived.at[me], phase, wrapped(j)).start()
        arrived[me] = out[me]

    def spread(out, arrived, phase):
        for j in order:
            copy_to(out.at[0], arrived.at[me], phase, wrapped(j)).start()
        arrived[me] = out[0]

    def whole(arrived, phase):
        part = arrived.at[pl.ds(0, ntx - 1)]
        return copy_to(part, part, phase, east)

    pl.semaphore_wait(barrier, ntx - 1 + 6)
    spread(info_send, info_in, 5)
    exchange(ob1, ib1, 0)

    def send(src, dst, s_sem, r_sem, yy, xx):
        copy = pltpu.make_async_remote_copy(
            src, dst, s_sem, r_sem, device_id=(yy, xx), device_id_type=MESH
        )
        copy.start()
        return copy

    low, high = slice(0, HALO), slice(BOX - HALO, BOX)
    far = slice(HALO + BOX, ext2)
    images = []
    for n, (src, dst) in enumerate(((obs_hbm, obs_e), (iv_hbm, iv_e))):
        images.append(send(src.at[:, high, :], dst.at[:, low, :], obs_sem.at[0, 2 * n], obs_sem.at[1, 2 * n], south, me))
        images.append(send(src.at[:, low, :], dst.at[:, far, :], obs_sem.at[0, 2 * n + 1], obs_sem.at[1, 2 * n + 1], north, me))

    load_rk.wait()
    load_ck.wait()
    flip = (iota((BOX, BOX), 0) + iota((BOX, BOX), 1) == taps - 1).astype(F32)

    for table, values, forward in ((ktab_c, ck_v, 0), (ktab_r, rk_v, 1)):
        table[...] = jnp.zeros_like(table)
        table[forward, 0, 0:bands, 0:taps] = values[...]
        plain = table[forward, 0, :, 0:BOX]
        table[1 - forward, 0, :, 0:BOX] = exact(plain, flip)
        for st in range(2):
            full = table[st, 0, :, 0:BOX]
            hi = full.astype(BF16).astype(F32)
            table[st, 0, :, 0:BOX] = hi
            table[st, 1, :, 0:BOX] = full - hi

    def band_tables(st, b):
        for part in range(2):
            spread = jnp.broadcast_to(ktab_c[st, part, pl.ds(b, 1), :], (BOX, WIDE))
            skew = pltpu.roll(spread, 0, 1, stride=1, stride_axis=0)
            for n in range(2):
                own = pltpu.roll(skew, (WIDE - reach + n * BOX) % WIDE, 1)[:, 0:NAR]
                tcol[st, b, part, n * BOX : (n + 1) * BOX, :] = own.astype(BF16)
            spread = jnp.broadcast_to(ktab_r[st, part, pl.ds(b, 1), :], (BOX, NAR))
            skew = pltpu.roll(spread, 0, 1, stride=1, stride_axis=0)
            out, trow = ((ext2, trow1), (BOX, trow2))[st]
            for n in range(0, out, BOX):
                count = min(BOX, out - n)
                own = pltpu.roll(skew, (HALO - reach + n) % NAR, 1)
                trow[b, part, n : n + count] = own[0:count, 0 : trow.shape[3]].astype(BF16)

    tile_row_i, tile_lane = iota((BOX, BOX), 0), iota((BOX, BOX), 1)

    def of_band(index, b):
        return (index >= reach * b) & (index < reach * b + reach)

    def strip_tables(st):
        together = tile_row_i < 0
        for b in range(bands):
            together = together | (of_band(tile_row_i, b) & of_band(tile_lane, b))
        rows_i = iota((BOX, WIDE), 0)
        for part in range(2):
            spread = jnp.zeros((BOX, WIDE), F32)
            for b in range(bands):
                line = jnp.broadcast_to(ktab_c[st, part, b : b + 1, :], (BOX, WIDE))
                spread = jnp.where(of_band(rows_i, b), line, spread)
            skew = pltpu.roll(spread, 0, 1, stride=1, stride_axis=0)
            left = pltpu.roll(skew, WIDE - 2 * reach, 1)
            empty = jnp.zeros((BOX, BOX), BF16)
            for n, values in enumerate((left, skew)):
                block = jnp.where(together, values[:, 0:BOX], 0.0).astype(BF16)
                at = slice(n * BOX, (n + 1) * BOX)
                diag[st, part, at, at] = block
                diag[st, part, at, slice((1 - n) * BOX, (2 - n) * BOX)] = empty

    for b in range(bands):
        band_tables(0, b)
    strip_tables(0)

    whole(info_in, 5).wait_recv()
    infos = info_in[:, 0, :]
    wide = (ntx, BOX)
    row_i, lane_i = iota(wide, 0), iota(wide, 1)
    tile_col = jnp.broadcast_to(infos[:, 6:7], wide)
    tile_row = jnp.sum(jnp.where(row_i == lane_i, tile_col, 0.0), axis=0, keepdims=True)
    tile_row = jnp.broadcast_to(jnp.where(lane1 < ntx, tile_row, -1.0), wide)
    same = tile_col == tile_row
    slot_row = jnp.sum(jnp.where(same & (row_i < lane_i), 1.0, 0.0), axis=0, keepdims=True)
    slot_row = jnp.broadcast_to(slot_row, wide)
    slot_col = jnp.sum(jnp.where(same & (lane_i < row_i), 1.0, 0.0), axis=1, keepdims=True)
    slot_col = jnp.broadcast_to(slot_col, wide)
    target = row_i.astype(F32)
    pick = [
        jnp.where((tile_row == target) & (slot_row == float(s)), 1.0, 0.0)[:, 0:ntx]
        for s in range(2)
    ]
    whole(ib1, 0).wait_recv()
    pieces = jnp.concatenate([ib1[:, r, :] for r in range(rows)], axis=1)
    chosen = gather(jnp.concatenate(pick, axis=0), pieces)
    for s in range(2):
        for r in range(rows):
            ob2[:, s * rows + r, :] = chosen[
                s * ntx : (s + 1) * ntx, r * BOX : (r + 1) * BOX
            ]
    exchange(ob2, ib2, 1)

    here = me.astype(F32)
    for s in range(2):
        mine = (tile_col == here) & (slot_col == float(s))
        sinfo[pl.ds(s, 1), :] = jnp.sum(jnp.where(mine, infos, 0.0), axis=0, keepdims=True)
    sinfo[2:8, :] = jnp.zeros((6, BOX), F32)
    lane_f = lane_i.astype(F32)
    give = jnp.concatenate(
        [
            jnp.where((tile_col == lane_f) & (slot_col == float(s)), 1.0, 0.0)[:, 0:ntx]
            for s in range(2)
        ],
        axis=1,
    )
    own_slot = jnp.sum(
        jnp.where(row_i[:, 0:1] == me, slot_col[:, 0:1], 0.0), axis=0, keepdims=True
    )

    eye8 = iota((8, BOX), 0) == iota((8, BOX), 1)

    def tables(which, ref, live):
        for s in range(2):
            line = jnp.broadcast_to(ref[pl.ds(s, 1), :], (8, BOX))
            column = jnp.sum(jnp.where(eye8, line, 0.0), axis=1, keepdims=True)
            table = jnp.broadcast_to(column, (8, BOX)) * live
            boxes = jnp.broadcast_to(column[7:8], (8, BOX))
            for j in range(2):
                wtab[which, s, j] = jnp.where(boxes == float(j), table, 0.0)
                if which == 1:
                    mtab[s, j] = jnp.where(boxes == float(j), 1.0, 0.0)

    tables(1, sinfo, 1.0)
    for b in range(bands):
        band_tables(1, b)
    strip_tables(1)

    whole(ib2, 1).wait_recv()
    for s in range(2):
        for r in range(rows):
            slots[s, pl.ds(r, ntx, stride=rows), :] = ib2[:, s * rows + r, :]

    waits = []
    for n, (src, dst, yy) in enumerate(
        (
            (slots.at[:, BOX - deep : BOX, :], nslots, south),
            (slots.at[:, 0:deep, :], sslots, north),
            (sinfo, ninfo, south),
            (sinfo, soinfo, north),
        )
    ):
        waits.append(send(src, dst, sl_sem.at[0, n], sl_sem.at[1, n], yy, me))

    sw1[...] = jnp.zeros_like(sw1)
    se1[...] = jnp.zeros_like(se1)
    for b in range(bands):
        for j in range(2):
            part = sum(wtab[1, s, j, pl.ds(b, 1), :] * slots[s] for s in range(2))
            model_e[b, deep : deep + BOX, j * BOX : (j + 1) * BOX] = part
            keep = of_band(tile_lane, b)
            shift = (reach * b) if j == 0 else (reach * b + reach) % BOX
            moved = pltpu.roll(part, shift, 1) if shift else part
            ref = (sw1, se1)[j]
            ref[...] = jnp.where(keep, moved, ref[...])
    for n, (src, dst, yy, xx) in enumerate(
        (
            (se1, west1.at[deep : deep + BOX], ti, east),
            (sw1, east1.at[deep : deep + BOX], ti, west),
            (se1.at[BOX - deep : BOX], west1.at[0:deep], south, east),
            (sw1.at[BOX - deep : BOX], east1.at[0:deep], south, west),
            (se1.at[0:deep], west1.at[deep + BOX : ext1], north, east),
            (sw1.at[0:deep], east1.at[deep + BOX : ext1], north, west),
        )
    ):
        waits.append(send(src, dst, sl_sem.at[0, 4 + n], sl_sem.at[1, 4 + n], yy, xx))

    def three(hi, lo, right_hi, right_lo):
        return dot(hi, right_hi) + (dot(hi, right_lo) + dot(lo, right_hi))

    def columns(st, b, image):
        hi, lo = split(image)
        return three(hi, lo, tcol[st, b, 0], tcol[st, b, 1])

    def along_rows(trow, b, image):
        hi, lo = split(image)
        both = dot(trow[b, 0], jnp.concatenate([hi, lo], axis=1))
        return both[:, 0:BOX] + (both[:, BOX:] + dot(trow[b, 1], hi))

    for b in range(bands):
        mixed_e[b, deep : deep + BOX] = columns(0, b, model_e[b, deep : deep + BOX])

    for copy in waits[0:4]:
        copy.wait_recv()
    tables(0, ninfo, jnp.where(ti > 0, 1.0, 0.0))
    tables(2, soinfo, jnp.where(ti < nty - 1, 1.0, 0.0))

    for b in range(bands):
        image = jnp.concatenate(
            [
                jnp.concatenate(
                    [
                        sum(wtab[which, s, j, pl.ds(b, 1), :] * ref[s] for s in range(2))
                        for j in range(2)
                    ],
                    axis=1,
                )
                for which, ref in ((0, nslots), (2, sslots))
            ],
            axis=0,
        )
        image = columns(0, b, image)
        mixed_e[b, 0:deep] = image[0:deep]
        mixed_e[b, deep + BOX : ext1] = image[deep:]

    load_obs.wait()
    load_iv.wait()
    for copy in images:
        copy.wait_recv()

    half = BOX // 2
    row, lane = iota((ext2, BOX), 0), iota((ext2, BOX), 1)
    inside = ((row >= HALO) | (ti > 0)) & ((row < HALO + BOX) | (ti < nty - 1))
    near = iota((ext1, BOX), 1) < half

    def residual_of(b, mixed, flipped):
        predicted = along_rows(trow1, b, mixed)
        first = (lane < half) != flipped
        seen = jnp.where(first, obs_e[b, :, 0:BOX], obs_e[b, :, BOX:])
        weights = jnp.where(first, iv_e[b, :, 0:BOX], iv_e[b, :, BOX:])
        residual = jnp.where(inside, weights * (seen - predicted), 0.0)
        image = along_rows(trow2, b, residual)
        middle = residual[HALO : HALO + BOX]
        low = slice(BOX, BOX + half) if flipped else slice(0, half)
        high = slice(half, BOX) if flipped else slice(BOX + half, 2 * BOX)
        for ref, values in ((resid_ref, middle), (back, image)):
            ref[b, :, low] = values[:, 0:half]
            ref[b, :, high] = values[:, half:]
        return image

    for b in range(bands):
        residual_of(b, jnp.where(near, mixed_e[b, :, BOX:], mixed_e[b, :, 0:BOX]), True)

    for copy in waits[4:]:
        copy.wait_recv()

    def halo_parts(left, right, count, edge):
        row = iota((count, BOX), 0)
        inner = ((row >= edge) | (ti > 0)) & ((row < count - edge) | (ti < nty - 1))
        for n, (ref, ok) in enumerate(((left, me > 0), (right, me < ntx - 1))):
            hi, lo = split(jnp.where(inner & ok, ref[...], 0.0))
            ext_h[0:count, n * BOX : (n + 1) * BOX] = hi
            ext_l[0:count, n * BOX : (n + 1) * BOX] = lo

    halo_parts(west1, east1, ext1, deep)
    pack[...] = three(ext_h[...], ext_l[...], diag[0, 0], diag[0, 1])
    first_lanes = iota((ext1, BOX), 1) < reach
    last_lanes = iota((ext1, BOX), 1) >= BOX - reach
    to_west = to_east = jnp.zeros((BOX, BOX), F32)
    for b in range(bands):
        left = pltpu.roll(pack[:, 0:BOX], (BOX - reach * b) % BOX, 1)
        right = pltpu.roll(pack[:, BOX:], (2 * BOX - reach - reach * b) % BOX, 1)
        mixed = jnp.where(near, mixed_e[b, :, 0:BOX], mixed_e[b, :, BOX:])
        mixed = mixed + jnp.where(first_lanes, left, jnp.where(last_lanes, right, 0.0))
        image = residual_of(b, mixed, False)
        keep = of_band(tile_lane, b)
        to_west = jnp.where(keep, pltpu.roll(image, reach * b, 1), to_west)
        to_east = jnp.where(keep, pltpu.roll(image, (reach * b + reach) % BOX, 1), to_east)
    sw2[...] = to_west
    se2[...] = to_east
    strips = [
        send(se2, west2, st_sem.at[0, 0], st_sem.at[1, 0], ti, east),
        send(sw2, east2, st_sem.at[0, 1], st_sem.at[1, 1], ti, west),
    ]
    for side in range(2):
        at = slice(side * BOX, (side + 1) * BOX)
        full = diag[1, 0, at, at].astype(F32) + diag[1, 1, at, at].astype(F32)
        fold = jnp.zeros((BOX, BOX), F32)
        for b in range(bands):
            here_lane = tile_lane if side == 0 else tile_lane - (BOX - reach)
            inside_lane = (here_lane >= 0) & (here_lane < reach)
            fold = jnp.where(inside_lane & (tile_row_i - reach * b == here_lane), 1.0, fold)
        fold = fold.astype(BF16)
        for s in range(2):
            weight = jnp.zeros((1, BOX), F32)
            for b in range(bands):
                weight = jnp.where(of_band(lane1, b), wtab[1, s, side, b : b + 1, :], weight)
            hi, lo = split(full * weight)
            hi, lo = split(dot(hi, fold) + dot(lo, fold))
            last[0, at, s * BOX : (s + 1) * BOX] = hi
            last[1, at, s * BOX : (s + 1) * BOX] = lo

    totals = [jnp.zeros((BOX, BOX), F32) for _ in range(2)]
    for b in range(bands):
        gradient = columns(1, b, back[b])
        grad[b] = gradient
        halves = (gradient[:, 0:BOX], gradient[:, BOX:])
        for s in range(2):
            for j in range(2):
                totals[s] = totals[s] + wtab[1, s, j, b : b + 1, :] * halves[j]
    for s in range(2):
        grads[s] = totals[s]
    for copy in strips:
        copy.wait_recv()
    for n, (ref, ok) in enumerate(((west2, me > 0), (east2, me < ntx - 1))):
        hi, lo = split(jnp.where(ok, ref[...], 0.0))
        ext_h[0:BOX, n * BOX : (n + 1) * BOX] = hi
        ext_l[0:BOX, n * BOX : (n + 1) * BOX] = lo
    share = three(ext_h[0:BOX], ext_l[0:BOX], last[0], last[1])
    for s in range(2):
        grads[s] += share[:, s * BOX : (s + 1) * BOX]

    for s in range(2):
        for r in range(rows):
            ob3[:, s * rows + r, :] = grads[s, pl.ds(r, ntx, stride=rows), :]
    exchange(ob3, ib3, 2)
    edges[...] = three(ext_h[0:BOX], ext_l[0:BOX], diag[1, 0], diag[1, 1])
    sgacc[...] = jnp.zeros_like(sgacc)

    def spectra(b, carry):
        left = pltpu.roll(edges[:, 0:BOX], lax.rem(BOX - reach * b, BOX), 1)
        right = pltpu.roll(edges[:, BOX:], lax.rem(2 * BOX - reach - reach * b, BOX), 1)
        halves = (
            grad[b, :, 0:BOX] + jnp.where(tile_lane < reach, left, 0.0),
            grad[b, :, BOX:] + jnp.where(tile_lane >= BOX - reach, right, 0.0),
        )
        for s in range(2):
            under = sum(mtab[s, j, pl.ds(b, 1), :] * halves[j] for j in range(2))
            sgacc[s, pl.ds(b, 1), :] = jnp.sum(slots[s] * under, axis=0, keepdims=True)
        return carry

    lax.fori_loop(0, bands, spectra, 0)
    line = jnp.zeros((1, BOX), F32)
    for s in range(2):
        column = jnp.broadcast_to(jnp.sum(sgacc[s], axis=1, keepdims=True), (8, BOX))
        mark = iota((8, BOX), 1) == iota((8, BOX), 0) + 8 * s
        line = line + jnp.sum(jnp.where(mark, column, 0.0), axis=0, keepdims=True)
    sg_send[0] = line
    spread(sg_send, sg_in, 4)

    whole(ib3, 2).wait_recv()
    pieces = jnp.concatenate(
        [
            jnp.concatenate(
                [ib3[:, s * rows + r, :] for r in range(rows)], axis=1
            )
            for s in range(2)
        ],
        axis=0,
    )
    chosen = gather(give, pieces)
    for r in range(rows):
        ob4[:, r, :] = chosen[:, r * BOX : (r + 1) * BOX]
    exchange(ob4, ib4, 3)

    square = jnp.sum(jnp.where(lane1 < bands, info * info, 0.0), axis=1, keepdims=True)
    step_morph = gamma_v[...] / square
    full = morph_v[...]
    norm = jnp.sum(jnp.sum(full * full, axis=0, keepdims=True), axis=1, keepdims=True)
    step_sed = gamma_v[...] / jnp.sqrt(norm)

    whole(sg_in, 4).wait_recv()
    terms = jnp.zeros((1, BOX), F32)
    for d in range(ntx):
        terms = terms + jnp.where(own_tile == float(d), sg_in[d], 0.0)
    terms = jnp.where(own_slot == 0.0, terms, pltpu.roll(terms, BOX - 8, 1))
    nsed_ref[0] = jnp.maximum(info + step_sed * terms, 0.0)[:, 0:bands]

    whole(ib4, 3).wait_recv()
    for r in range(rows):
        at = pl.ds(r, ntx, stride=rows)
        update = step_morph * ib4[:, r, :]
        nmorph_ref[0, 0, at, :] = jnp.maximum(morph_v[at, :] + update, 0.0)

    for phase, arrived in enumerate((ib1, ib2, ib3, ib4, sg_in, info_in)):
        whole(arrived, phase).wait_send()
    for copy in images + waits + strips:
        copy.wait_send()


def write_out(resid, morph, sed, resid_o, morph_o, sed_o, sem):
    pairs = ((resid, resid_o), (morph, morph_o), (sed, sed_o))
    stores = [pltpu.make_async_copy(a, o, sem.at[n]) for n, (a, o) in enumerate(pairs)]
    for copy in stores:
        copy.start()
    for copy in stores:
        copy.wait()


def solution(mesh):
    nty, ntx = mesh.shape["ty"], mesh.shape["tx"]

    def body(observed, inverse_variance, sed, morph, foot_block, gamma, row_kernel, col_kernel):
        bands, height, width = observed.shape
        taps = row_kernel.shape[1]
        rows = BOX // ntx
        deep = 2 * HALO
        ext1, ext2 = height + 2 * deep, height + 2 * HALO

        def vmem(*shape, dtype=F32):
            return pltpu.VMEM(shape, dtype)

        scratch = [
            vmem(bands, ext2, width), vmem(bands, ext2, width),
            vmem(bands, ext1, width), vmem(bands, ext1, width),
            vmem(bands, height, width), vmem(bands, height, width),
            vmem(ext1, BOX), vmem(ext1, BOX), vmem(BOX, BOX), vmem(BOX, BOX),
            vmem(BOX, BOX), vmem(BOX, BOX), vmem(BOX, BOX), vmem(BOX, BOX),
            vmem(ext1, NAR), vmem(BOX, NAR),
            vmem(BOX, BOX), vmem(*sed.shape), vmem(1, 1, dtype=jnp.int32), vmem(1, 1), vmem(8, BOX),
            vmem(1, 1, BOX), vmem(ntx, 1, BOX),
            vmem(ntx, rows, BOX), vmem(ntx, rows, BOX),
            vmem(ntx, 2 * rows, BOX), vmem(ntx, 2 * rows, BOX),
            vmem(ntx, 2 * rows, BOX), vmem(ntx, 2 * rows, BOX),
            vmem(ntx, rows, BOX), vmem(ntx, rows, BOX),
            vmem(1, 1, BOX), vmem(ntx, 1, BOX),
            vmem(2, BOX, BOX), vmem(8, BOX), vmem(2, deep, BOX), vmem(2, deep, BOX),
            vmem(8, BOX), vmem(8, BOX), vmem(2, BOX, BOX), vmem(2, 8, BOX),
            vmem(3, 2, 2, 8, BOX), vmem(2, 2, 8, BOX),
            vmem(bands, taps), vmem(bands, taps),
            vmem(2, 2, 8, WIDE), vmem(2, 2, 8, NAR),
            vmem(2, bands, 2, NAR, NAR, dtype=BF16),
            vmem(bands, 2, ext2, ext1, dtype=BF16), vmem(bands, 2, BOX, ext2, dtype=BF16),
            vmem(2, 2, NAR, NAR, dtype=BF16), vmem(2, NAR, NAR, dtype=BF16),
            vmem(ext1, NAR, dtype=BF16), vmem(ext1, NAR, dtype=BF16),
            pltpu.SemaphoreType.DMA((9,)), pltpu.SemaphoreType.DMA((6,)),
            pltpu.SemaphoreType.DMA((6,)), pltpu.SemaphoreType.DMA((2, 4)),
            pltpu.SemaphoreType.DMA((2, 10)), pltpu.SemaphoreType.DMA((2, 2)),
        ]
        anywhere = pl.BlockSpec(memory_space=pl.ANY)
        vector = pl.BlockSpec(memory_space=pltpu.VMEM)
        shapes = tuple(
            jax.ShapeDtypeStruct(a.shape, F32) for a in (observed, morph, sed)
        )
        operands = (
            observed, inverse_variance, sed, morph, foot_block, gamma, row_kernel, col_kernel
        )
        results = pl.pallas_call(
            functools.partial(kernel, nty, ntx, bands, taps),
            out_shape=shapes,
            in_specs=[pl.BlockSpec(memory_space=pltpu.HBM)] * 8,
            out_specs=(vector, vector, vector),
            scratch_shapes=scratch,
            compiler_params=pltpu.CompilerParams(
                collective_id=0, has_side_effects=True, vmem_limit_bytes=40 * 2**20
            ),
        )(*(a if a.size == 1 else pltpu.with_memory_space_constraint(a, pltpu.HBM) for a in operands))
        return pl.pallas_call(
            write_out,
            out_shape=shapes,
            in_specs=[vector] * 3,
            out_specs=(anywhere,) * 3,
            scratch_shapes=[pltpu.SemaphoreType.DMA((3,))],
            compiler_params=pltpu.CompilerParams(vmem_limit_bytes=8 * 2**20),
        )(*results)

    in_specs = (
        P(None, "ty", "tx"),
        P(None, "ty", "tx"),
        P("ty", "tx", None),
        P("ty", "tx", None, None),
        P("ty", "tx"),
        P("ty", "tx"),
        P(),
        P(),
    )
    out_specs = (P(None, "ty", "tx"), P("ty", "tx", None, None), P("ty", "tx", None))
    return jax.shard_map(body, mesh=mesh, in_specs=in_specs, out_specs=out_specs, check_vma=False)
```

```python
import functools

import jax
import jax.numpy as jnp
from jax import lax
from jax.experimental import pallas as pl
from jax.experimental.pallas import tpu as pltpu
from jax.sharding import PartitionSpec as P

MESH = pl.DeviceIdType.MESH
F32 = jnp.float32
BF16 = jnp.bfloat16
HIGHEST = lax.Precision.HIGHEST
BOX = 128
HALO = 24
WIDE = 384
NAR = 256


def iota(shape, dim):
    return lax.broadcasted_iota(jnp.int32, shape, dim)


def split(x):
    hi = x.astype(BF16)
    return hi, (x - hi.astype(F32)).astype(BF16)


def dot(a, b):
    return jnp.dot(a, b, preferred_element_type=F32)


def exact(a, b):
    return jnp.dot(a, b, preferred_element_type=F32, precision=HIGHEST)


def gather(pick, x):
    hi = x.astype(BF16)
    rest = x - hi.astype(F32)
    mid = rest.astype(BF16)
    low = (rest - mid.astype(F32)).astype(BF16)
    pick = pick.astype(BF16)
    return (dot(pick, hi) + dot(pick, mid)) + dot(pick, low)


def kernel(
    nty, ntx, bands, taps,
    obs_hbm, iv_hbm, sed_hbm, morph_hbm, foot_hbm, gamma_hbm, rk_hbm, ck_hbm,
    resid_ref, nmorph_ref, nsed_ref,
    obs_e, iv_e, model_e, mixed_e, back, grad,
    west1, east1, west2, east2, sw1, se1, sw2, se2, pack, edges,
    morph_v, sed_v, foot_v, gamma_v, info_v, info_send, info_in,
    ob1, ib1, ob2, ib2, ob3, ib3, ob4, ib4, sg_send, sg_in,
    slots, sinfo, nslots, sslots, ninfo, soinfo, grads, sgacc,
    wtab, mtab, rk_v, ck_v, ktab_c, ktab_r, tcol, trow1, trow2, diag, last, ext_h, ext_l,
    loc_sem, send_sem, a2a_sem, obs_sem, sl_sem, st_sem,
):
    ti = lax.axis_index("ty")
    me = lax.axis_index("tx")
    reach = (taps - 1) // 2
    rows = BOX // ntx
    deep = 2 * HALO
    ext1, ext2 = BOX + 2 * deep, BOX + 2 * HALO
    north, south = lax.rem(ti + nty - 1, nty), lax.rem(ti + 1, nty)
    west, east = lax.rem(me + ntx - 1, ntx), lax.rem(me + 1, ntx)

    barrier = pltpu.get_barrier_semaphore()

    def wrapped(j):
        p = me + j
        return jnp.where(p >= ntx, p - ntx, p)

    order = sorted(range(1, ntx), key=lambda j: -min(j, ntx - j))
    for j in order:
        pl.semaphore_signal(barrier, inc=1, device_id=(ti, wrapped(j)), device_id_type=MESH)
    for yy in (north, south):
        for xx in (me, west, east):
            pl.semaphore_signal(barrier, inc=1, device_id=(yy, xx), device_id_type=MESH)

    load_morph = pltpu.make_async_copy(morph_hbm.at[0, 0], morph_v, loc_sem.at[0])
    load_rk = pltpu.make_async_copy(rk_hbm, rk_v, loc_sem.at[1])
    load_ck = pltpu.make_async_copy(ck_hbm, ck_v, loc_sem.at[2])
    load_obs = pltpu.make_async_copy(obs_hbm, obs_e.at[:, HALO : HALO + BOX, :], loc_sem.at[3])
    load_iv = pltpu.make_async_copy(iv_hbm, iv_e.at[:, HALO : HALO + BOX, :], loc_sem.at[4])
    scalars = [
        pltpu.make_async_copy(src, dst, loc_sem.at[6 + n])
        for n, (src, dst) in enumerate(((sed_hbm, sed_v), (foot_hbm, foot_v), (gamma_hbm, gamma_v)))
    ]
    for copy in scalars:
        copy.start()
    load_morph.start()
    load_rk.start()
    load_ck.start()
    load_obs.start()
    load_iv.start()

    lane1 = iota((1, BOX), 1)
    info_v[...] = jnp.zeros_like(info_v)
    for copy in scalars:
        copy.wait()
    tile = foot_v[...] // 2
    box = foot_v[...] - 2 * tile
    info_v[0:1, 0:bands] = sed_v[0]
    info = info_v[0:1, :]
    own_tile = tile.astype(F32)
    info = jnp.where(lane1 == 6, own_tile, info)
    info = jnp.where(lane1 == 7, box.astype(F32), info)
    info_send[0] = info
    load_morph.wait()
    for r in range(rows):
        ob1[:, r, :] = morph_v[pl.ds(r, ntx, stride=rows), :]

    def copy_to(src, dst, phase, p):
        return pltpu.make_async_remote_copy(
            src, dst, send_sem.at[phase], a2a_sem.at[phase],
            device_id=(ti, p), device_id_type=MESH,
        )

    def exchange(out, arrived, phase):
        for j in order:
            copy_to(out.at[wrapped(j)], arrived.at[me], phase, wrapped(j)).start()
        arrived[me] = out[me]

    def spread(out, arrived, phase):
        for j in order:
            copy_to(out.at[0], arrived.at[me], phase, wrapped(j)).start()
        arrived[me] = out[0]

    def whole(arrived, phase):
        part = arrived.at[pl.ds(0, ntx - 1)]
        return copy_to(part, part, phase, east)

    pl.semaphore_wait(barrier, ntx - 1 + 6)
    spread(info_send, info_in, 5)
    exchange(ob1, ib1, 0)

    def send(src, dst, s_sem, r_sem, yy, xx):
        copy = pltpu.make_async_remote_copy(
            src, dst, s_sem, r_sem, device_id=(yy, xx), device_id_type=MESH
        )
        copy.start()
        return copy

    low, high = slice(0, HALO), slice(BOX - HALO, BOX)
    far = slice(HALO + BOX, ext2)
    images = []
    for n, (src, dst) in enumerate(((obs_hbm, obs_e), (iv_hbm, iv_e))):
        images.append(send(src.at[:, high, :], dst.at[:, low, :], obs_sem.at[0, 2 * n], obs_sem.at[1, 2 * n], south, me))
        images.append(send(src.at[:, low, :], dst.at[:, far, :], obs_sem.at[0, 2 * n + 1], obs_sem.at[1, 2 * n + 1], north, me))

    load_rk.wait()
    load_ck.wait()
    flip = (iota((BOX, BOX), 0) + iota((BOX, BOX), 1) == taps - 1).astype(F32)

    for table, values, forward in ((ktab_c, ck_v, 0), (ktab_r, rk_v, 1)):
        table[...] = jnp.zeros_like(table)
        table[forward, 0, 0:bands, 0:taps] = values[...]
        plain = table[forward, 0, :, 0:BOX]
        table[1 - forward, 0, :, 0:BOX] = exact(plain, flip)
        for st in range(2):
            full = table[st, 0, :, 0:BOX]
            hi = full.astype(BF16).astype(F32)
            table[st, 0, :, 0:BOX] = hi
            table[st, 1, :, 0:BOX] = full - hi

    def band_tables(st, b):
        for part in range(2):
            spread = jnp.broadcast_to(ktab_c[st, part, pl.ds(b, 1), :], (BOX, WIDE))
            skew = pltpu.roll(spread, 0, 1, stride=1, stride_axis=0)
            for n in range(2):
                own = pltpu.roll(skew, (WIDE - reach + n * BOX) % WIDE, 1)[:, 0:NAR]
                tcol[st, b, part, n * BOX : (n + 1) * BOX, :] = own.astype(BF16)
            spread = jnp.broadcast_to(ktab_r[st, part, pl.ds(b, 1), :], (BOX, NAR))
            skew = pltpu.roll(spread, 0, 1, stride=1, stride_axis=0)
            out, trow = ((ext2, trow1), (BOX, trow2))[st]
            for n in range(0, out, BOX):
                count = min(BOX, out - n)
                own = pltpu.roll(skew, (HALO - reach + n) % NAR, 1)
                trow[b, part, n : n + count] = own[0:count, 0 : trow.shape[3]].astype(BF16)

    tile_row_i, tile_lane = iota((BOX, BOX), 0), iota((BOX, BOX), 1)

    def of_band(index, b):
        return (index >= reach * b) & (index < reach * b + reach)

    def strip_tables(st):
        together = tile_row_i < 0
        for b in range(bands):
            together = together | (of_band(tile_row_i, b) & of_band(tile_lane, b))
        rows_i = iota((BOX, WIDE), 0)
        for part in range(2):
            spread = jnp.zeros((BOX, WIDE), F32)
            for b in range(bands):
                line = jnp.broadcast_to(ktab_c[st, part, b : b + 1, :], (BOX, WIDE))
                spread = jnp.where(of_band(rows_i, b), line, spread)
            skew = pltpu.roll(spread, 0, 1, stride=1, stride_axis=0)
            left = pltpu.roll(skew, WIDE - 2 * reach, 1)
            empty = jnp.zeros((BOX, BOX), BF16)
            for n, values in enumerate((left, skew)):
                block = jnp.where(together, values[:, 0:BOX], 0.0).astype(BF16)
                at = slice(n * BOX, (n + 1) * BOX)
                diag[st, part, at, at] = block
                diag[st, part, at, slice((1 - n) * BOX, (2 - n) * BOX)] = empty

    for b in range(bands):
        band_tables(0, b)
    strip_tables(0)

    whole(info_in, 5).wait_recv()
    infos = info_in[:, 0, :]
    wide = (ntx, BOX)
    row_i, lane_i = iota(wide, 0), iota(wide, 1)
    tile_col = jnp.broadcast_to(infos[:, 6:7], wide)
    tile_row = jnp.sum(jnp.where(row_i == lane_i, tile_col, 0.0), axis=0, keepdims=True)
    tile_row = jnp.broadcast_to(jnp.where(lane1 < ntx, tile_row, -1.0), wide)
    same = tile_col == tile_row
    slot_row = jnp.sum(jnp.where(same & (row_i < lane_i), 1.0, 0.0), axis=0, keepdims=True)
    slot_row = jnp.broadcast_to(slot_row, wide)
    slot_col = jnp.sum(jnp.where(same & (lane_i < row_i), 1.0, 0.0), axis=1, keepdims=True)
    slot_col = jnp.broadcast_to(slot_col, wide)
    target = row_i.astype(F32)
    pick = [
        jnp.where((tile_row == target) & (slot_row == float(s)), 1.0, 0.0)[:, 0:ntx]
        for s in range(2)
    ]
    whole(ib1, 0).wait_recv()
    pieces = jnp.concatenate([ib1[:, r, :] for r in range(rows)], axis=1)
    chosen = gather(jnp.concatenate(pick, axis=0), pieces)
    for s in range(2):
        for r in range(rows):
            ob2[:, s * rows + r, :] = chosen[
                s * ntx : (s + 1) * ntx, r * BOX : (r + 1) * BOX
            ]
    exchange(ob2, ib2, 1)

    here = me.astype(F32)
    for s in range(2):
        mine = (tile_col == here) & (slot_col == float(s))
        sinfo[pl.ds(s, 1), :] = jnp.sum(jnp.where(mine, infos, 0.0), axis=0, keepdims=True)
    sinfo[2:8, :] = jnp.zeros((6, BOX), F32)
    lane_f = lane_i.astype(F32)
    give = jnp.concatenate(
        [
            jnp.where((tile_col == lane_f) & (slot_col == float(s)), 1.0, 0.0)[:, 0:ntx]
            for s in range(2)
        ],
        axis=1,
    )
    own_slot = jnp.sum(
        jnp.where(row_i[:, 0:1] == me, slot_col[:, 0:1], 0.0), axis=0, keepdims=True
    )

    eye8 = iota((8, BOX), 0) == iota((8, BOX), 1)

    def tables(which, ref, live):
        for s in range(2):
            line = jnp.broadcast_to(ref[pl.ds(s, 1), :], (8, BOX))
            column = jnp.sum(jnp.where(eye8, line, 0.0), axis=1, keepdims=True)
            table = jnp.broadcast_to(column, (8, BOX)) * live
            boxes = jnp.broadcast_to(column[7:8], (8, BOX))
            for j in range(2):
                wtab[which, s, j] = jnp.where(boxes == float(j), table, 0.0)
                if which == 1:
                    mtab[s, j] = jnp.where(boxes == float(j), 1.0, 0.0)

    tables(1, sinfo, 1.0)
    for b in range(bands):
        band_tables(1, b)
    strip_tables(1)

    whole(ib2, 1).wait_recv()
    for s in range(2):
        for r in range(rows):
            slots[s, pl.ds(r, ntx, stride=rows), :] = ib2[:, s * rows + r, :]

    waits = []
    for n, (src, dst, yy) in enumerate(
        (
            (slots.at[:, BOX - deep : BOX, :], nslots, south),
            (slots.at[:, 0:deep, :], sslots, north),
            (sinfo, ninfo, south),
            (sinfo, soinfo, north),
        )
    ):
        waits.append(send(src, dst, sl_sem.at[0, n], sl_sem.at[1, n], yy, me))

    sw1[...] = jnp.zeros_like(sw1)
    se1[...] = jnp.zeros_like(se1)
    for b in range(bands):
        for j in range(2):
            part = sum(wtab[1, s, j, pl.ds(b, 1), :] * slots[s] for s in range(2))
            model_e[b, deep : deep + BOX, j * BOX : (j + 1) * BOX] = part
            keep = of_band(tile_lane, b)
            shift = (reach * b) if j == 0 else (reach * b + reach) % BOX
            moved = pltpu.roll(part, shift, 1) if shift else part
            ref = (sw1, se1)[j]
            ref[...] = jnp.where(keep, moved, ref[...])
    for n, (src, dst, yy, xx) in enumerate(
        (
            (se1.at[BOX - deep : BOX], west1.at[0:deep], south, east),
            (sw1.at[BOX - deep : BOX], east1.at[0:deep], south, west),
            (se1.at[0:deep], west1.at[deep + BOX : ext1], north, east),
            (sw1.at[0:deep], east1.at[deep + BOX : ext1], north, west),
            (se1, west1.at[deep : deep + BOX], ti, east),
            (sw1, east1.at[deep : deep + BOX], ti, west),
        )
    ):
        waits.append(send(src, dst, sl_sem.at[0, 4 + n], sl_sem.at[1, 4 + n], yy, xx))

    def three(hi, lo, right_hi, right_lo):
        return dot(hi, right_hi) + (dot(hi, right_lo) + dot(lo, right_hi))

    def columns(st, b, image):
        hi, lo = split(image)
        return three(hi, lo, tcol[st, b, 0], tcol[st, b, 1])

    def along_rows(trow, b, image):
        hi, lo = split(image)
        count, depth = trow.shape[2:]
        both = dot(trow[b].reshape(2 * count, depth), hi)
        return both[:count] + (both[count:] + dot(trow[b, 0], lo))

    for b in range(bands):
        mixed_e[b, deep : deep + BOX] = columns(0, b, model_e[b, deep : deep + BOX])

    for copy in waits[0:4]:
        copy.wait_recv()
    tables(0, ninfo, jnp.where(ti > 0, 1.0, 0.0))
    tables(2, soinfo, jnp.where(ti < nty - 1, 1.0, 0.0))

    for b in range(bands):
        image = jnp.concatenate(
            [
                jnp.concatenate(
                    [
                        sum(wtab[which, s, j, pl.ds(b, 1), :] * ref[s] for s in range(2))
                        for j in range(2)
                    ],
                    axis=1,
                )
                for which, ref in ((0, nslots), (2, sslots))
            ],
            axis=0,
        )
        image = columns(0, b, image)
        mixed_e[b, 0:deep] = image[0:deep]
        mixed_e[b, deep + BOX : ext1] = image[deep:]

    load_obs.wait()
    load_iv.wait()
    for copy in images:
        copy.wait_recv()
    for copy in waits[4:]:
        copy.wait_recv()

    def halo_parts(left, right, count, edge):
        row = iota((count, BOX), 0)
        inner = ((row >= edge) | (ti > 0)) & ((row < count - edge) | (ti < nty - 1))
        for n, (ref, ok) in enumerate(((left, me > 0), (right, me < ntx - 1))):
            hi, lo = split(jnp.where(inner & ok, ref[...], 0.0))
            ext_h[0:count, n * BOX : (n + 1) * BOX] = hi
            ext_l[0:count, n * BOX : (n + 1) * BOX] = lo

    halo_parts(west1, east1, ext1, deep)
    pack[...] = three(ext_h[...], ext_l[...], diag[0, 0], diag[0, 1])
    row = iota((ext2, 2 * BOX), 0)
    inside = ((row >= HALO) | (ti > 0)) & ((row < HALO + BOX) | (ti < nty - 1))
    first_lanes = iota((ext1, BOX), 1) < reach
    last_lanes = iota((ext1, BOX), 1) >= BOX - reach

    to_west = to_east = jnp.zeros((BOX, BOX), F32)
    for b in range(bands):
        left = pltpu.roll(pack[:, 0:BOX], (BOX - reach * b) % BOX, 1)
        left = mixed_e[b, :, 0:BOX] + jnp.where(first_lanes, left, 0.0)
        right = pltpu.roll(pack[:, BOX:], (2 * BOX - reach - reach * b) % BOX, 1)
        right = mixed_e[b, :, BOX:] + jnp.where(last_lanes, right, 0.0)
        predicted = along_rows(trow1, b, jnp.concatenate([left, right], axis=1))
        residual = jnp.where(inside, iv_e[b] * (obs_e[b] - predicted), 0.0)
        resid_ref[b] = residual[HALO : HALO + BOX]
        image = along_rows(trow2, b, residual)
        back[b] = image
        keep = of_band(tile_lane, b)
        to_west = jnp.where(keep, pltpu.roll(image[:, 0:BOX], reach * b, 1), to_west)
        moved = pltpu.roll(image[:, BOX:], (reach * b + reach) % BOX, 1)
        to_east = jnp.where(keep, moved, to_east)
    sw2[...] = to_west
    se2[...] = to_east
    strips = [
        send(se2, west2, st_sem.at[0, 0], st_sem.at[1, 0], ti, east),
        send(sw2, east2, st_sem.at[0, 1], st_sem.at[1, 1], ti, west),
    ]
    for side in range(2):
        at = slice(side * BOX, (side + 1) * BOX)
        full = diag[1, 0, at, at].astype(F32) + diag[1, 1, at, at].astype(F32)
        fold = jnp.zeros((BOX, BOX), F32)
        for b in range(bands):
            here_lane = tile_lane if side == 0 else tile_lane - (BOX - reach)
            inside_lane = (here_lane >= 0) & (here_lane < reach)
            fold = jnp.where(inside_lane & (tile_row_i - reach * b == here_lane), 1.0, fold)
        fold = fold.astype(BF16)
        for s in range(2):
            weight = jnp.zeros((1, BOX), F32)
            for b in range(bands):
                weight = jnp.where(of_band(lane1, b), wtab[1, s, side, b : b + 1, :], weight)
            hi, lo = split(full * weight)
            hi, lo = split(dot(hi, fold) + dot(lo, fold))
            last[0, at, s * BOX : (s + 1) * BOX] = hi
            last[1, at, s * BOX : (s + 1) * BOX] = lo

    totals = [jnp.zeros((BOX, BOX), F32) for _ in range(2)]
    for b in range(bands):
        gradient = columns(1, b, back[b])
        grad[b] = gradient
        halves = (gradient[:, 0:BOX], gradient[:, BOX:])
        for s in range(2):
            for j in range(2):
                totals[s] = totals[s] + wtab[1, s, j, b : b + 1, :] * halves[j]
    for s in range(2):
        grads[s] = totals[s]
    for copy in strips:
        copy.wait_recv()
    for n, (ref, ok) in enumerate(((west2, me > 0), (east2, me < ntx - 1))):
        hi, lo = split(jnp.where(ok, ref[...], 0.0))
        ext_h[0:BOX, n * BOX : (n + 1) * BOX] = hi
        ext_l[0:BOX, n * BOX : (n + 1) * BOX] = lo
    share = three(ext_h[0:BOX], ext_l[0:BOX], last[0], last[1])
    for s in range(2):
        grads[s] += share[:, s * BOX : (s + 1) * BOX]

    for s in range(2):
        for r in range(rows):
            ob3[:, s * rows + r, :] = grads[s, pl.ds(r, ntx, stride=rows), :]
    exchange(ob3, ib3, 2)
    edges[...] = three(ext_h[0:BOX], ext_l[0:BOX], diag[1, 0], diag[1, 1])
    sgacc[...] = jnp.zeros_like(sgacc)

    def spectra(b, carry):
        left = pltpu.roll(edges[:, 0:BOX], lax.rem(BOX - reach * b, BOX), 1)
        right = pltpu.roll(edges[:, BOX:], lax.rem(2 * BOX - reach - reach * b, BOX), 1)
        halves = (
            grad[b, :, 0:BOX] + jnp.where(tile_lane < reach, left, 0.0),
            grad[b, :, BOX:] + jnp.where(tile_lane >= BOX - reach, right, 0.0),
        )
        for s in range(2):
            under = sum(mtab[s, j, pl.ds(b, 1), :] * halves[j] for j in range(2))
            sgacc[s, pl.ds(b, 1), :] = jnp.sum(slots[s] * under, axis=0, keepdims=True)
        return carry

    lax.fori_loop(0, bands, spectra, 0)
    line = jnp.zeros((1, BOX), F32)
    for s in range(2):
        column = jnp.broadcast_to(jnp.sum(sgacc[s], axis=1, keepdims=True), (8, BOX))
        mark = iota((8, BOX), 1) == iota((8, BOX), 0) + 8 * s
        line = line + jnp.sum(jnp.where(mark, column, 0.0), axis=0, keepdims=True)
    sg_send[0] = line
    spread(sg_send, sg_in, 4)

    whole(ib3, 2).wait_recv()
    pieces = jnp.concatenate(
        [
            jnp.concatenate(
                [ib3[:, s * rows + r, :] for r in range(rows)], axis=1
            )
            for s in range(2)
        ],
        axis=0,
    )
    chosen = gather(give, pieces)
    for r in range(rows):
        ob4[:, r, :] = chosen[:, r * BOX : (r + 1) * BOX]
    exchange(ob4, ib4, 3)

    square = jnp.sum(jnp.where(lane1 < bands, info * info, 0.0), axis=1, keepdims=True)
    step_morph = gamma_v[...] / square
    full = morph_v[...]
    norm = jnp.sum(jnp.sum(full * full, axis=0, keepdims=True), axis=1, keepdims=True)
    step_sed = gamma_v[...] / jnp.sqrt(norm)

    whole(sg_in, 4).wait_recv()
    terms = jnp.zeros((1, BOX), F32)
    for d in range(ntx):
        terms = terms + jnp.where(own_tile == float(d), sg_in[d], 0.0)
    terms = jnp.where(own_slot == 0.0, terms, pltpu.roll(terms, BOX - 8, 1))
    nsed_ref[0] = jnp.maximum(info + step_sed * terms, 0.0)[:, 0:bands]

    whole(ib4, 3).wait_recv()
    for r in range(rows):
        at = pl.ds(r, ntx, stride=rows)
        update = step_morph * ib4[:, r, :]
        nmorph_ref[0, 0, at, :] = jnp.maximum(morph_v[at, :] + update, 0.0)

    for phase, arrived in enumerate((ib1, ib2, ib3, ib4, sg_in, info_in)):
        whole(arrived, phase).wait_send()
    for copy in images + waits + strips:
        copy.wait_send()


def write_out(resid, morph, sed, resid_o, morph_o, sed_o, sem):
    pairs = ((resid, resid_o), (morph, morph_o), (sed, sed_o))
    stores = [pltpu.make_async_copy(a, o, sem.at[n]) for n, (a, o) in enumerate(pairs)]
    for copy in stores:
        copy.start()
    for copy in stores:
        copy.wait()


def solution(mesh):
    nty, ntx = mesh.shape["ty"], mesh.shape["tx"]

    def body(observed, inverse_variance, sed, morph, foot_block, gamma, row_kernel, col_kernel):
        bands, height, width = observed.shape
        taps = row_kernel.shape[1]
        rows = BOX // ntx
        deep = 2 * HALO
        ext1, ext2 = height + 2 * deep, height + 2 * HALO

        def vmem(*shape, dtype=F32):
            return pltpu.VMEM(shape, dtype)

        scratch = [
            vmem(bands, ext2, width), vmem(bands, ext2, width),
            vmem(bands, ext1, width), vmem(bands, ext1, width),
            vmem(bands, height, width), vmem(bands, height, width),
            vmem(ext1, BOX), vmem(ext1, BOX), vmem(BOX, BOX), vmem(BOX, BOX),
            vmem(BOX, BOX), vmem(BOX, BOX), vmem(BOX, BOX), vmem(BOX, BOX),
            vmem(ext1, NAR), vmem(BOX, NAR),
            vmem(BOX, BOX), vmem(*sed.shape), vmem(1, 1, dtype=jnp.int32), vmem(1, 1), vmem(8, BOX),
            vmem(1, 1, BOX), vmem(ntx, 1, BOX),
            vmem(ntx, rows, BOX), vmem(ntx, rows, BOX),
            vmem(ntx, 2 * rows, BOX), vmem(ntx, 2 * rows, BOX),
            vmem(ntx, 2 * rows, BOX), vmem(ntx, 2 * rows, BOX),
            vmem(ntx, rows, BOX), vmem(ntx, rows, BOX),
            vmem(1, 1, BOX), vmem(ntx, 1, BOX),
            vmem(2, BOX, BOX), vmem(8, BOX), vmem(2, deep, BOX), vmem(2, deep, BOX),
            vmem(8, BOX), vmem(8, BOX), vmem(2, BOX, BOX), vmem(2, 8, BOX),
            vmem(3, 2, 2, 8, BOX), vmem(2, 2, 8, BOX),
            vmem(bands, taps), vmem(bands, taps),
            vmem(2, 2, 8, WIDE), vmem(2, 2, 8, NAR),
            vmem(2, bands, 2, NAR, NAR, dtype=BF16),
            vmem(bands, 2, ext2, ext1, dtype=BF16), vmem(bands, 2, BOX, ext2, dtype=BF16),
            vmem(2, 2, NAR, NAR, dtype=BF16), vmem(2, NAR, NAR, dtype=BF16),
            vmem(ext1, NAR, dtype=BF16), vmem(ext1, NAR, dtype=BF16),
            pltpu.SemaphoreType.DMA((9,)), pltpu.SemaphoreType.DMA((6,)),
            pltpu.SemaphoreType.DMA((6,)), pltpu.SemaphoreType.DMA((2, 4)),
            pltpu.SemaphoreType.DMA((2, 10)), pltpu.SemaphoreType.DMA((2, 2)),
        ]
        anywhere = pl.BlockSpec(memory_space=pl.ANY)
        vector = pl.BlockSpec(memory_space=pltpu.VMEM)
        shapes = tuple(
            jax.ShapeDtypeStruct(a.shape, F32) for a in (observed, morph, sed)
        )
        operands = (
            observed, inverse_variance, sed, morph, foot_block, gamma, row_kernel, col_kernel
        )
        results = pl.pallas_call(
            functools.partial(kernel, nty, ntx, bands, taps),
            out_shape=shapes,
            in_specs=[pl.BlockSpec(memory_space=pltpu.HBM)] * 8,
            out_specs=(vector, vector, vector),
            scratch_shapes=scratch,
            compiler_params=pltpu.CompilerParams(
                collective_id=0, has_side_effects=True, vmem_limit_bytes=40 * 2**20
            ),
        )(*(a if a.size == 1 else pltpu.with_memory_space_constraint(a, pltpu.HBM) for a in operands))
        return pl.pallas_call(
            write_out,
            out_shape=shapes,
            in_specs=[vector] * 3,
            out_specs=(anywhere,) * 3,
            scratch_shapes=[pltpu.SemaphoreType.DMA((3,))],
            compiler_params=pltpu.CompilerParams(vmem_limit_bytes=8 * 2**20),
        )(*results)

    in_specs = (
        P(None, "ty", "tx"),
        P(None, "ty", "tx"),
        P("ty", "tx", None),
        P("ty", "tx", None, None),
        P("ty", "tx"),
        P("ty", "tx"),
        P(),
        P(),
    )
    out_specs = (P(None, "ty", "tx"), P("ty", "tx", None, None), P("ty", "tx", None))
    return jax.shard_map(body, mesh=mesh, in_specs=in_specs, out_specs=out_specs, check_vma=False)
```

```python
import functools

import jax
import jax.numpy as jnp
from jax import lax
from jax.experimental import pallas as pl
from jax.experimental.pallas import tpu as pltpu
from jax.sharding import PartitionSpec as P

MESH = pl.DeviceIdType.MESH
F32 = jnp.float32
BF16 = jnp.bfloat16
HIGHEST = lax.Precision.HIGHEST
BOX = 128
HALO = 24
WIDE = 384
NAR = 256


def iota(shape, dim):
    return lax.broadcasted_iota(jnp.int32, shape, dim)


def split(x):
    hi = x.astype(BF16)
    return hi, (x - hi.astype(F32)).astype(BF16)


def dot(a, b):
    return jnp.dot(a, b, preferred_element_type=F32)


def exact(a, b):
    return jnp.dot(a, b, preferred_element_type=F32, precision=HIGHEST)


def gather(pick, x):
    hi = x.astype(BF16)
    rest = x - hi.astype(F32)
    mid = rest.astype(BF16)
    low = (rest - mid.astype(F32)).astype(BF16)
    pick = pick.astype(BF16)
    return (dot(pick, hi) + dot(pick, mid)) + dot(pick, low)


def kernel(
    nty, ntx, bands, taps,
    obs_hbm, iv_hbm, sed_hbm, morph_hbm, foot_hbm, gamma_hbm, rk_hbm, ck_hbm,
    resid_ref, nmorph_ref, nsed_ref,
    obs_e, iv_e, model_e, mixed_e, back, grad,
    west1, east1, west2, east2, sw1, se1, sw2, se2, pack, edges,
    morph_v, sed_v, foot_v, gamma_v, info_v, info_send, info_in,
    ob1, ib1, ob2, ib2, ob3, ib3, ob4, ib4, sg_send, sg_in,
    slots, sinfo, nslots, sslots, ninfo, soinfo, grads, sgacc,
    wtab, mtab, rk_v, ck_v, ktab_c, ktab_r, tcol, trow1, trow2, diag, last, ext_h, ext_l,
    loc_sem, send_sem, a2a_sem, obs_sem, sl_sem, st_sem,
):
    ti = lax.axis_index("ty")
    me = lax.axis_index("tx")
    reach = (taps - 1) // 2
    rows = BOX // ntx
    deep = 2 * HALO
    ext1, ext2 = BOX + 2 * deep, BOX + 2 * HALO
    north, south = lax.rem(ti + nty - 1, nty), lax.rem(ti + 1, nty)
    west, east = lax.rem(me + ntx - 1, ntx), lax.rem(me + 1, ntx)

    barrier = pltpu.get_barrier_semaphore()

    def wrapped(j):
        p = me + j
        return jnp.where(p >= ntx, p - ntx, p)

    order = sorted(range(1, ntx), key=lambda j: -min(j, ntx - j))
    greeted = [(ti, wrapped(j)) for j in order]
    beyond = [(yy, xx) for xx in (west, east, me) for yy in (north, south)]
    for yy, xx in greeted[:12] + beyond + greeted[12:]:
        pl.semaphore_signal(barrier, inc=1, device_id=(yy, xx), device_id_type=MESH)

    load_morph = pltpu.make_async_copy(morph_hbm.at[0, 0], morph_v, loc_sem.at[0])
    load_rk = pltpu.make_async_copy(rk_hbm, rk_v, loc_sem.at[1])
    load_ck = pltpu.make_async_copy(ck_hbm, ck_v, loc_sem.at[2])
    load_obs = pltpu.make_async_copy(obs_hbm, obs_e.at[:, HALO : HALO + BOX, :], loc_sem.at[3])
    load_iv = pltpu.make_async_copy(iv_hbm, iv_e.at[:, HALO : HALO + BOX, :], loc_sem.at[4])
    scalars = [
        pltpu.make_async_copy(src, dst, loc_sem.at[6 + n])
        for n, (src, dst) in enumerate(((sed_hbm, sed_v), (foot_hbm, foot_v), (gamma_hbm, gamma_v)))
    ]
    for copy in scalars:
        copy.start()
    load_morph.start()
    load_rk.start()
    load_ck.start()
    load_obs.start()
    load_iv.start()

    lane1 = iota((1, BOX), 1)
    info_v[...] = jnp.zeros_like(info_v)
    for copy in scalars:
        copy.wait()
    tile = foot_v[...] // 2
    box = foot_v[...] - 2 * tile
    info_v[0:1, 0:bands] = sed_v[0]
    info = info_v[0:1, :]
    own_tile = tile.astype(F32)
    info = jnp.where(lane1 == 6, own_tile, info)
    info = jnp.where(lane1 == 7, box.astype(F32), info)
    info_send[0] = info
    load_morph.wait()
    for r in range(rows):
        ob1[:, r, :] = morph_v[pl.ds(r, ntx, stride=rows), :]

    def copy_to(src, dst, phase, p):
        return pltpu.make_async_remote_copy(
            src, dst, send_sem.at[phase], a2a_sem.at[phase],
            device_id=(ti, p), device_id_type=MESH,
        )

    def exchange(out, arrived, phase):
        for j in order:
            copy_to(out.at[wrapped(j)], arrived.at[me], phase, wrapped(j)).start()
        arrived[me] = out[me]

    def spread(out, arrived, phase):
        for j in order:
            copy_to(out.at[0], arrived.at[me], phase, wrapped(j)).start()
        arrived[me] = out[0]

    def whole(arrived, phase):
        part = arrived.at[pl.ds(0, ntx - 1)]
        return copy_to(part, part, phase, east)

    pl.semaphore_wait(barrier, ntx - 1 + 6)
    spread(info_send, info_in, 5)
    exchange(ob1, ib1, 0)

    def send(src, dst, s_sem, r_sem, yy, xx):
        copy = pltpu.make_async_remote_copy(
            src, dst, s_sem, r_sem, device_id=(yy, xx), device_id_type=MESH
        )
        copy.start()
        return copy

    low, high = slice(0, HALO), slice(BOX - HALO, BOX)
    far = slice(HALO + BOX, ext2)
    images = []
    for n, (src, dst) in enumerate(((obs_hbm, obs_e), (iv_hbm, iv_e))):
        images.append(send(src.at[:, high, :], dst.at[:, low, :], obs_sem.at[0, 2 * n], obs_sem.at[1, 2 * n], south, me))
        images.append(send(src.at[:, low, :], dst.at[:, far, :], obs_sem.at[0, 2 * n + 1], obs_sem.at[1, 2 * n + 1], north, me))

    load_rk.wait()
    load_ck.wait()
    flip = (iota((BOX, BOX), 0) + iota((BOX, BOX), 1) == taps - 1).astype(F32)

    for table, values, forward in ((ktab_c, ck_v, 0), (ktab_r, rk_v, 1)):
        table[...] = jnp.zeros_like(table)
        table[forward, 0, 0:bands, 0:taps] = values[...]
        plain = table[forward, 0, :, 0:BOX]
        table[1 - forward, 0, :, 0:BOX] = exact(plain, flip)
        for st in range(2):
            full = table[st, 0, :, 0:BOX]
            hi = full.astype(BF16).astype(F32)
            table[st, 0, :, 0:BOX] = hi
            table[st, 1, :, 0:BOX] = full - hi

    def band_tables(st, b):
        for part in range(2):
            spread = jnp.broadcast_to(ktab_c[st, part, pl.ds(b, 1), :], (BOX, WIDE))
            skew = pltpu.roll(spread, 0, 1, stride=1, stride_axis=0)
            for n in range(2):
                own = pltpu.roll(skew, (WIDE - reach + n * BOX) % WIDE, 1)[:, 0:NAR]
                tcol[st, b, part, n * BOX : (n + 1) * BOX, :] = own.astype(BF16)
            spread = jnp.broadcast_to(ktab_r[st, part, pl.ds(b, 1), :], (BOX, NAR))
            skew = pltpu.roll(spread, 0, 1, stride=1, stride_axis=0)
            out, trow = ((ext2, trow1), (BOX, trow2))[st]
            for n in range(0, out, BOX):
                count = min(BOX, out - n)
                own = pltpu.roll(skew, (HALO - reach + n) % NAR, 1)
                trow[b, part, n : n + count] = own[0:count, 0 : trow.shape[3]].astype(BF16)

    tile_row_i, tile_lane = iota((BOX, BOX), 0), iota((BOX, BOX), 1)

    def of_band(index, b):
        return (index >= reach * b) & (index < reach * b + reach)

    def strip_tables(st):
        together = tile_row_i < 0
        for b in range(bands):
            together = together | (of_band(tile_row_i, b) & of_band(tile_lane, b))
        rows_i = iota((BOX, WIDE), 0)
        for part in range(2):
            spread = jnp.zeros((BOX, WIDE), F32)
            for b in range(bands):
                line = jnp.broadcast_to(ktab_c[st, part, b : b + 1, :], (BOX, WIDE))
                spread = jnp.where(of_band(rows_i, b), line, spread)
            skew = pltpu.roll(spread, 0, 1, stride=1, stride_axis=0)
            left = pltpu.roll(skew, WIDE - 2 * reach, 1)
            empty = jnp.zeros((BOX, BOX), BF16)
            for n, values in enumerate((left, skew)):
                block = jnp.where(together, values[:, 0:BOX], 0.0).astype(BF16)
                at = slice(n * BOX, (n + 1) * BOX)
                diag[st, part, at, at] = block
                diag[st, part, at, slice((1 - n) * BOX, (2 - n) * BOX)] = empty

    for b in range(bands):
        band_tables(0, b)
    strip_tables(0)

    whole(info_in, 5).wait_recv()
    infos = info_in[:, 0, :]
    wide = (ntx, BOX)
    row_i, lane_i = iota(wide, 0), iota(wide, 1)
    tile_col = jnp.broadcast_to(infos[:, 6:7], wide)
    tile_row = jnp.sum(jnp.where(row_i == lane_i, tile_col, 0.0), axis=0, keepdims=True)
    tile_row = jnp.broadcast_to(jnp.where(lane1 < ntx, tile_row, -1.0), wide)
    same = tile_col == tile_row
    slot_row = jnp.sum(jnp.where(same & (row_i < lane_i), 1.0, 0.0), axis=0, keepdims=True)
    slot_row = jnp.broadcast_to(slot_row, wide)
    slot_col = jnp.sum(jnp.where(same & (lane_i < row_i), 1.0, 0.0), axis=1, keepdims=True)
    slot_col = jnp.broadcast_to(slot_col, wide)
    target = row_i.astype(F32)
    pick = [
        jnp.where((tile_row == target) & (slot_row == float(s)), 1.0, 0.0)[:, 0:ntx]
        for s in range(2)
    ]
    whole(ib1, 0).wait_recv()
    pieces = jnp.concatenate([ib1[:, r, :] for r in range(rows)], axis=1)
    chosen = gather(jnp.concatenate(pick, axis=0), pieces)
    for s in range(2):
        for r in range(rows):
            ob2[:, s * rows + r, :] = chosen[
                s * ntx : (s + 1) * ntx, r * BOX : (r + 1) * BOX
            ]
    exchange(ob2, ib2, 1)

    here = me.astype(F32)
    for s in range(2):
        mine = (tile_col == here) & (slot_col == float(s))
        sinfo[pl.ds(s, 1), :] = jnp.sum(jnp.where(mine, infos, 0.0), axis=0, keepdims=True)
    sinfo[2:8, :] = jnp.zeros((6, BOX), F32)
    lane_f = lane_i.astype(F32)
    give = jnp.concatenate(
        [
            jnp.where((tile_col == lane_f) & (slot_col == float(s)), 1.0, 0.0)[:, 0:ntx]
            for s in range(2)
        ],
        axis=1,
    )
    own_slot = jnp.sum(
        jnp.where(row_i[:, 0:1] == me, slot_col[:, 0:1], 0.0), axis=0, keepdims=True
    )

    eye8 = iota((8, BOX), 0) == iota((8, BOX), 1)

    def tables(which, ref, live):
        for s in range(2):
            line = jnp.broadcast_to(ref[pl.ds(s, 1), :], (8, BOX))
            column = jnp.sum(jnp.where(eye8, line, 0.0), axis=1, keepdims=True)
            table = jnp.broadcast_to(column, (8, BOX)) * live
            boxes = jnp.broadcast_to(column[7:8], (8, BOX))
            for j in range(2):
                wtab[which, s, j] = jnp.where(boxes == float(j), table, 0.0)
                if which == 1:
                    mtab[s, j] = jnp.where(boxes == float(j), 1.0, 0.0)

    tables(1, sinfo, 1.0)
    for b in range(bands):
        band_tables(1, b)
    strip_tables(1)

    whole(ib2, 1).wait_recv()
    for s in range(2):
        for r in range(rows):
            slots[s, pl.ds(r, ntx, stride=rows), :] = ib2[:, s * rows + r, :]

    waits = []
    for n, (src, dst, yy) in enumerate(
        (
            (slots.at[:, BOX - deep : BOX, :], nslots, south),
            (slots.at[:, 0:deep, :], sslots, north),
            (sinfo, ninfo, south),
            (sinfo, soinfo, north),
        )
    ):
        waits.append(send(src, dst, sl_sem.at[0, n], sl_sem.at[1, n], yy, me))

    sw1[...] = jnp.zeros_like(sw1)
    se1[...] = jnp.zeros_like(se1)
    for b in range(bands):
        for j in range(2):
            part = sum(wtab[1, s, j, pl.ds(b, 1), :] * slots[s] for s in range(2))
            model_e[b, deep : deep + BOX, j * BOX : (j + 1) * BOX] = part
            keep = of_band(tile_lane, b)
            shift = (reach * b) if j == 0 else (reach * b + reach) % BOX
            moved = pltpu.roll(part, shift, 1) if shift else part
            ref = (sw1, se1)[j]
            ref[...] = jnp.where(keep, moved, ref[...])
    for n, (src, dst, yy, xx) in enumerate(
        (
            (se1.at[BOX - deep : BOX], west1.at[0:deep], south, east),
            (sw1.at[BOX - deep : BOX], east1.at[0:deep], south, west),
            (se1.at[0:deep], west1.at[deep + BOX : ext1], north, east),
            (sw1.at[0:deep], east1.at[deep + BOX : ext1], north, west),
            (se1, west1.at[deep : deep + BOX], ti, east),
            (sw1, east1.at[deep : deep + BOX], ti, west),
        )
    ):
        waits.append(send(src, dst, sl_sem.at[0, 4 + n], sl_sem.at[1, 4 + n], yy, xx))

    def three(hi, lo, right_hi, right_lo):
        return dot(hi, right_hi) + (dot(hi, right_lo) + dot(lo, right_hi))

    def columns(st, b, image):
        hi, lo = split(image)
        return three(hi, lo, tcol[st, b, 0], tcol[st, b, 1])

    def along_rows(trow, b, image):
        hi, lo = split(image)
        count, depth = trow.shape[2:]
        both = dot(trow[b].reshape(2 * count, depth), hi)
        return both[:count] + (both[count:] + dot(trow[b, 0], lo))

    for b in range(bands):
        mixed_e[b, deep : deep + BOX] = columns(0, b, model_e[b, deep : deep + BOX])

    for copy in waits[0:4]:
        copy.wait_recv()
    tables(0, ninfo, jnp.where(ti > 0, 1.0, 0.0))
    tables(2, soinfo, jnp.where(ti < nty - 1, 1.0, 0.0))

    for b in range(bands):
        image = jnp.concatenate(
            [
                jnp.concatenate(
                    [
                        sum(wtab[which, s, j, pl.ds(b, 1), :] * ref[s] for s in range(2))
                        for j in range(2)
                    ],
                    axis=1,
                )
                for which, ref in ((0, nslots), (2, sslots))
            ],
            axis=0,
        )
        image = columns(0, b, image)
        mixed_e[b, 0:deep] = image[0:deep]
        mixed_e[b, deep + BOX : ext1] = image[deep:]

    load_obs.wait()
    load_iv.wait()
    for copy in images:
        copy.wait_recv()
    for copy in waits[4:]:
        copy.wait_recv()

    def halo_parts(left, right, count, edge):
        row = iota((count, BOX), 0)
        inner = ((row >= edge) | (ti > 0)) & ((row < count - edge) | (ti < nty - 1))
        for n, (ref, ok) in enumerate(((left, me > 0), (right, me < ntx - 1))):
            hi, lo = split(jnp.where(inner & ok, ref[...], 0.0))
            ext_h[0:count, n * BOX : (n + 1) * BOX] = hi
            ext_l[0:count, n * BOX : (n + 1) * BOX] = lo

    halo_parts(west1, east1, ext1, deep)
    pack[...] = three(ext_h[...], ext_l[...], diag[0, 0], diag[0, 1])
    row = iota((ext2, 2 * BOX), 0)
    inside = ((row >= HALO) | (ti > 0)) & ((row < HALO + BOX) | (ti < nty - 1))
    first_lanes = iota((ext1, BOX), 1) < reach
    last_lanes = iota((ext1, BOX), 1) >= BOX - reach

    to_west = to_east = jnp.zeros((BOX, BOX), F32)
    for b in range(bands):
        left = pltpu.roll(pack[:, 0:BOX], (BOX - reach * b) % BOX, 1)
        left = mixed_e[b, :, 0:BOX] + jnp.where(first_lanes, left, 0.0)
        right = pltpu.roll(pack[:, BOX:], (2 * BOX - reach - reach * b) % BOX, 1)
        right = mixed_e[b, :, BOX:] + jnp.where(last_lanes, right, 0.0)
        predicted = along_rows(trow1, b, jnp.concatenate([left, right], axis=1))
        residual = jnp.where(inside, iv_e[b] * (obs_e[b] - predicted), 0.0)
        resid_ref[b] = residual[HALO : HALO + BOX]
        image = along_rows(trow2, b, residual)
        back[b] = image
        keep = of_band(tile_lane, b)
        to_west = jnp.where(keep, pltpu.roll(image[:, 0:BOX], reach * b, 1), to_west)
        moved = pltpu.roll(image[:, BOX:], (reach * b + reach) % BOX, 1)
        to_east = jnp.where(keep, moved, to_east)
    sw2[...] = to_west
    se2[...] = to_east
    strips = [
        send(se2, west2, st_sem.at[0, 0], st_sem.at[1, 0], ti, east),
        send(sw2, east2, st_sem.at[0, 1], st_sem.at[1, 1], ti, west),
    ]
    for side in range(2):
        at = slice(side * BOX, (side + 1) * BOX)
        full = diag[1, 0, at, at].astype(F32) + diag[1, 1, at, at].astype(F32)
        fold = jnp.zeros((BOX, BOX), F32)
        for b in range(bands):
            here_lane = tile_lane if side == 0 else tile_lane - (BOX - reach)
            inside_lane = (here_lane >= 0) & (here_lane < reach)
            fold = jnp.where(inside_lane & (tile_row_i - reach * b == here_lane), 1.0, fold)
        fold = fold.astype(BF16)
        for s in range(2):
            weight = jnp.zeros((1, BOX), F32)
            for b in range(bands):
                weight = jnp.where(of_band(lane1, b), wtab[1, s, side, b : b + 1, :], weight)
            hi, lo = split(full * weight)
            hi, lo = split(dot(hi, fold) + dot(lo, fold))
            last[0, at, s * BOX : (s + 1) * BOX] = hi
            last[1, at, s * BOX : (s + 1) * BOX] = lo

    totals = [jnp.zeros((BOX, BOX), F32) for _ in range(2)]
    for b in range(bands):
        gradient = columns(1, b, back[b])
        grad[b] = gradient
        halves = (gradient[:, 0:BOX], gradient[:, BOX:])
        for s in range(2):
            for j in range(2):
                totals[s] = totals[s] + wtab[1, s, j, b : b + 1, :] * halves[j]
    for s in range(2):
        grads[s] = totals[s]
    for copy in strips:
        copy.wait_recv()
    for n, (ref, ok) in enumerate(((west2, me > 0), (east2, me < ntx - 1))):
        hi, lo = split(jnp.where(ok, ref[...], 0.0))
        ext_h[0:BOX, n * BOX : (n + 1) * BOX] = hi
        ext_l[0:BOX, n * BOX : (n + 1) * BOX] = lo
    share = three(ext_h[0:BOX], ext_l[0:BOX], last[0], last[1])
    for s in range(2):
        grads[s] += share[:, s * BOX : (s + 1) * BOX]

    for s in range(2):
        for r in range(rows):
            ob3[:, s * rows + r, :] = grads[s, pl.ds(r, ntx, stride=rows), :]
    exchange(ob3, ib3, 2)
    edges[...] = three(ext_h[0:BOX], ext_l[0:BOX], diag[1, 0], diag[1, 1])
    sgacc[...] = jnp.zeros_like(sgacc)

    def spectra(b, carry):
        left = pltpu.roll(edges[:, 0:BOX], lax.rem(BOX - reach * b, BOX), 1)
        right = pltpu.roll(edges[:, BOX:], lax.rem(2 * BOX - reach - reach * b, BOX), 1)
        halves = (
            grad[b, :, 0:BOX] + jnp.where(tile_lane < reach, left, 0.0),
            grad[b, :, BOX:] + jnp.where(tile_lane >= BOX - reach, right, 0.0),
        )
        for s in range(2):
            under = sum(mtab[s, j, pl.ds(b, 1), :] * halves[j] for j in range(2))
            sgacc[s, pl.ds(b, 1), :] = jnp.sum(slots[s] * under, axis=0, keepdims=True)
        return carry

    lax.fori_loop(0, bands, spectra, 0)
    line = jnp.zeros((1, BOX), F32)
    for s in range(2):
        column = jnp.broadcast_to(jnp.sum(sgacc[s], axis=1, keepdims=True), (8, BOX))
        mark = iota((8, BOX), 1) == iota((8, BOX), 0) + 8 * s
        line = line + jnp.sum(jnp.where(mark, column, 0.0), axis=0, keepdims=True)
    sg_send[0] = line
    spread(sg_send, sg_in, 4)

    whole(ib3, 2).wait_recv()
    pieces = jnp.concatenate(
        [
            jnp.concatenate(
                [ib3[:, s * rows + r, :] for r in range(rows)], axis=1
            )
            for s in range(2)
        ],
        axis=0,
    )
    chosen = gather(give, pieces)
    for r in range(rows):
        ob4[:, r, :] = chosen[:, r * BOX : (r + 1) * BOX]
    exchange(ob4, ib4, 3)

    square = jnp.sum(jnp.where(lane1 < bands, info * info, 0.0), axis=1, keepdims=True)
    step_morph = gamma_v[...] / square
    full = morph_v[...]
    norm = jnp.sum(jnp.sum(full * full, axis=0, keepdims=True), axis=1, keepdims=True)
    step_sed = gamma_v[...] / jnp.sqrt(norm)

    whole(sg_in, 4).wait_recv()
    terms = jnp.zeros((1, BOX), F32)
    for d in range(ntx):
        terms = terms + jnp.where(own_tile == float(d), sg_in[d], 0.0)
    terms = jnp.where(own_slot == 0.0, terms, pltpu.roll(terms, BOX - 8, 1))
    nsed_ref[0] = jnp.maximum(info + step_sed * terms, 0.0)[:, 0:bands]

    whole(ib4, 3).wait_recv()
    for r in range(rows):
        at = pl.ds(r, ntx, stride=rows)
        update = step_morph * ib4[:, r, :]
        nmorph_ref[0, 0, at, :] = jnp.maximum(morph_v[at, :] + update, 0.0)

    for phase, arrived in enumerate((ib1, ib2, ib3, ib4, sg_in, info_in)):
        whole(arrived, phase).wait_send()
    for copy in images + waits + strips:
        copy.wait_send()


def write_out(resid, morph, sed, resid_o, morph_o, sed_o, sem):
    pairs = ((resid, resid_o), (morph, morph_o), (sed, sed_o))
    stores = [pltpu.make_async_copy(a, o, sem.at[n]) for n, (a, o) in enumerate(pairs)]
    for copy in stores:
        copy.start()
    for copy in stores:
        copy.wait()


def solution(mesh):
    nty, ntx = mesh.shape["ty"], mesh.shape["tx"]

    def body(observed, inverse_variance, sed, morph, foot_block, gamma, row_kernel, col_kernel):
        bands, height, width = observed.shape
        taps = row_kernel.shape[1]
        rows = BOX // ntx
        deep = 2 * HALO
        ext1, ext2 = height + 2 * deep, height + 2 * HALO

        def vmem(*shape, dtype=F32):
            return pltpu.VMEM(shape, dtype)

        scratch = [
            vmem(bands, ext2, width), vmem(bands, ext2, width),
            vmem(bands, ext1, width), vmem(bands, ext1, width),
            vmem(bands, height, width), vmem(bands, height, width),
            vmem(ext1, BOX), vmem(ext1, BOX), vmem(BOX, BOX), vmem(BOX, BOX),
            vmem(BOX, BOX), vmem(BOX, BOX), vmem(BOX, BOX), vmem(BOX, BOX),
            vmem(ext1, NAR), vmem(BOX, NAR),
            vmem(BOX, BOX), vmem(*sed.shape), vmem(1, 1, dtype=jnp.int32), vmem(1, 1), vmem(8, BOX),
            vmem(1, 1, BOX), vmem(ntx, 1, BOX),
            vmem(ntx, rows, BOX), vmem(ntx, rows, BOX),
            vmem(ntx, 2 * rows, BOX), vmem(ntx, 2 * rows, BOX),
            vmem(ntx, 2 * rows, BOX), vmem(ntx, 2 * rows, BOX),
            vmem(ntx, rows, BOX), vmem(ntx, rows, BOX),
            vmem(1, 1, BOX), vmem(ntx, 1, BOX),
            vmem(2, BOX, BOX), vmem(8, BOX), vmem(2, deep, BOX), vmem(2, deep, BOX),
            vmem(8, BOX), vmem(8, BOX), vmem(2, BOX, BOX), vmem(2, 8, BOX),
            vmem(3, 2, 2, 8, BOX), vmem(2, 2, 8, BOX),
            vmem(bands, taps), vmem(bands, taps),
            vmem(2, 2, 8, WIDE), vmem(2, 2, 8, NAR),
            vmem(2, bands, 2, NAR, NAR, dtype=BF16),
            vmem(bands, 2, ext2, ext1, dtype=BF16), vmem(bands, 2, BOX, ext2, dtype=BF16),
            vmem(2, 2, NAR, NAR, dtype=BF16), vmem(2, NAR, NAR, dtype=BF16),
            vmem(ext1, NAR, dtype=BF16), vmem(ext1, NAR, dtype=BF16),
            pltpu.SemaphoreType.DMA((9,)), pltpu.SemaphoreType.DMA((6,)),
            pltpu.SemaphoreType.DMA((6,)), pltpu.SemaphoreType.DMA((2, 4)),
            pltpu.SemaphoreType.DMA((2, 10)), pltpu.SemaphoreType.DMA((2, 2)),
        ]
        anywhere = pl.BlockSpec(memory_space=pl.ANY)
        vector = pl.BlockSpec(memory_space=pltpu.VMEM)
        shapes = tuple(
            jax.ShapeDtypeStruct(a.shape, F32) for a in (observed, morph, sed)
        )
        operands = (
            observed, inverse_variance, sed, morph, foot_block, gamma, row_kernel, col_kernel
        )
        results = pl.pallas_call(
            functools.partial(kernel, nty, ntx, bands, taps),
            out_shape=shapes,
            in_specs=[pl.BlockSpec(memory_space=pltpu.HBM)] * 8,
            out_specs=(vector, vector, vector),
            scratch_shapes=scratch,
            compiler_params=pltpu.CompilerParams(
                collective_id=0, has_side_effects=True, vmem_limit_bytes=40 * 2**20
            ),
        )(*(a if a.size == 1 else pltpu.with_memory_space_constraint(a, pltpu.HBM) for a in operands))
        return pl.pallas_call(
            write_out,
            out_shape=shapes,
            in_specs=[vector] * 3,
            out_specs=(anywhere,) * 3,
            scratch_shapes=[pltpu.SemaphoreType.DMA((3,))],
            compiler_params=pltpu.CompilerParams(vmem_limit_bytes=8 * 2**20),
        )(*results)

    in_specs = (
        P(None, "ty", "tx"),
        P(None, "ty", "tx"),
        P("ty", "tx", None),
        P("ty", "tx", None, None),
        P("ty", "tx"),
        P("ty", "tx"),
        P(),
        P(),
    )
    out_specs = (P(None, "ty", "tx"), P("ty", "tx", None, None), P("ty", "tx", None))
    return jax.shard_map(body, mesh=mesh, in_specs=in_specs, out_specs=out_specs, check_vma=False)
```

```python
import functools

import jax
import jax.numpy as jnp
from jax import lax
from jax.experimental import pallas as pl
from jax.experimental.pallas import tpu as pltpu
from jax.sharding import PartitionSpec as P

MESH = pl.DeviceIdType.MESH
F32 = jnp.float32
BF16 = jnp.bfloat16
HIGHEST = lax.Precision.HIGHEST
BOX = 128
HALO = 24
WIDE = 384
NAR = 256


def iota(shape, dim):
    return lax.broadcasted_iota(jnp.int32, shape, dim)


def split(x):
    hi = x.astype(BF16)
    return hi, (x - hi.astype(F32)).astype(BF16)


def dot(a, b):
    return jnp.dot(a, b, preferred_element_type=F32)


def exact(a, b):
    return jnp.dot(a, b, preferred_element_type=F32, precision=HIGHEST)


def gather(pick, x):
    hi = x.astype(BF16)
    rest = x - hi.astype(F32)
    mid = rest.astype(BF16)
    low = (rest - mid.astype(F32)).astype(BF16)
    pick = pick.astype(BF16)
    return (dot(pick, hi) + dot(pick, mid)) + dot(pick, low)


def kernel(
    nty, ntx, bands, taps,
    obs_hbm, iv_hbm, sed_hbm, morph_hbm, foot_hbm, gamma_hbm, rk_hbm, ck_hbm,
    resid_ref, nmorph_ref, nsed_ref,
    obs_e, iv_e, model_e, mixed_e, back, grad,
    west1, east1, west2, east2, sw1, se1, sw2, se2, pack, edges,
    morph_v, sed_v, foot_v, gamma_v, info_v, info_send, info_in,
    ob1, ib1, ob2, ib2, ob3, ib3, ob4, ib4, sg_send, sg_in,
    slots, sinfo, nslots, sslots, ninfo, soinfo, grads, sgacc,
    wtab, mtab, rk_v, ck_v, ktab_c, ktab_r, tcol, trow1, trow2, diag, last, ext_h, ext_l,
    loc_sem, send_sem, a2a_sem, obs_sem, sl_sem, st_sem,
):
    ti = lax.axis_index("ty")
    me = lax.axis_index("tx")
    reach = (taps - 1) // 2
    rows = BOX // ntx
    deep = 2 * HALO
    ext1, ext2 = BOX + 2 * deep, BOX + 2 * HALO
    north, south = lax.rem(ti + nty - 1, nty), lax.rem(ti + 1, nty)
    west, east = lax.rem(me + ntx - 1, ntx), lax.rem(me + 1, ntx)

    barrier = pltpu.get_barrier_semaphore()

    def wrapped(j):
        p = me + j
        return jnp.where(p >= ntx, p - ntx, p)

    order = sorted(range(1, ntx), key=lambda j: -min(j, ntx - j))
    greeted = [(ti, wrapped(j)) for j in order]
    beyond = [(yy, xx) for xx in (west, east, me) for yy in (north, south)]
    for yy, xx in greeted[:12] + beyond + greeted[12:]:
        pl.semaphore_signal(barrier, inc=1, device_id=(yy, xx), device_id_type=MESH)

    load_morph = pltpu.make_async_copy(morph_hbm.at[0, 0], morph_v, loc_sem.at[0])
    load_rk = pltpu.make_async_copy(rk_hbm, rk_v, loc_sem.at[1])
    load_ck = pltpu.make_async_copy(ck_hbm, ck_v, loc_sem.at[2])
    load_obs = pltpu.make_async_copy(obs_hbm, obs_e.at[:, HALO : HALO + BOX, :], loc_sem.at[3])
    load_iv = pltpu.make_async_copy(iv_hbm, iv_e.at[:, HALO : HALO + BOX, :], loc_sem.at[4])
    scalars = [
        pltpu.make_async_copy(src, dst, loc_sem.at[6 + n])
        for n, (src, dst) in enumerate(((sed_hbm, sed_v), (foot_hbm, foot_v), (gamma_hbm, gamma_v)))
    ]
    for copy in scalars:
        copy.start()
    load_morph.start()
    load_rk.start()
    load_ck.start()
    load_obs.start()
    load_iv.start()

    lane1 = iota((1, BOX), 1)
    info_v[...] = jnp.zeros_like(info_v)
    for copy in scalars:
        copy.wait()
    tile = foot_v[...] // 2
    box = foot_v[...] - 2 * tile
    info_v[0:1, 0:bands] = sed_v[0]
    info = info_v[0:1, :]
    own_tile = tile.astype(F32)
    info = jnp.where(lane1 == 6, own_tile, info)
    info = jnp.where(lane1 == 7, box.astype(F32), info)
    info_send[0] = info
    load_morph.wait()
    for r in range(rows):
        ob1[:, r, :] = morph_v[pl.ds(r, ntx, stride=rows), :]

    def copy_to(src, dst, phase, p):
        return pltpu.make_async_remote_copy(
            src, dst, send_sem.at[phase], a2a_sem.at[phase],
            device_id=(ti, p), device_id_type=MESH,
        )

    def exchange(out, arrived, phase):
        for j in order:
            copy_to(out.at[wrapped(j)], arrived.at[me], phase, wrapped(j)).start()
        arrived[me] = out[me]

    def spread(out, arrived, phase):
        for j in order:
            copy_to(out.at[0], arrived.at[me], phase, wrapped(j)).start()
        arrived[me] = out[0]

    def whole(arrived, phase):
        part = arrived.at[pl.ds(0, ntx - 1)]
        return copy_to(part, part, phase, east)

    pl.semaphore_wait(barrier, ntx - 1 + 6)
    spread(info_send, info_in, 5)
    exchange(ob1, ib1, 0)

    def send(src, dst, s_sem, r_sem, yy, xx):
        copy = pltpu.make_async_remote_copy(
            src, dst, s_sem, r_sem, device_id=(yy, xx), device_id_type=MESH
        )
        copy.start()
        return copy

    low, high = slice(0, HALO), slice(BOX - HALO, BOX)
    far = slice(HALO + BOX, ext2)
    images = []
    for n, (src, dst) in enumerate(((obs_hbm, obs_e), (iv_hbm, iv_e))):
        images.append(send(src.at[:, high, :], dst.at[:, low, :], obs_sem.at[0, 2 * n], obs_sem.at[1, 2 * n], south, me))
        images.append(send(src.at[:, low, :], dst.at[:, far, :], obs_sem.at[0, 2 * n + 1], obs_sem.at[1, 2 * n + 1], north, me))

    load_rk.wait()
    load_ck.wait()
    flip = (iota((BOX, BOX), 0) + iota((BOX, BOX), 1) == taps - 1).astype(F32)

    for table, values, forward in ((ktab_c, ck_v, 0), (ktab_r, rk_v, 1)):
        table[...] = jnp.zeros_like(table)
        table[forward, 0, 0:bands, 0:taps] = values[...]
        plain = table[forward, 0, :, 0:BOX]
        table[1 - forward, 0, :, 0:BOX] = exact(plain, flip)
        for st in range(2):
            full = table[st, 0, :, 0:BOX]
            hi = full.astype(BF16).astype(F32)
            table[st, 0, :, 0:BOX] = hi
            table[st, 1, :, 0:BOX] = full - hi

    def band_tables(st, b):
        for part in range(2):
            spread = jnp.broadcast_to(ktab_c[st, part, pl.ds(b, 1), :], (BOX, WIDE))
            skew = pltpu.roll(spread, 0, 1, stride=1, stride_axis=0)
            for n in range(2):
                own = pltpu.roll(skew, (WIDE - reach + n * BOX) % WIDE, 1)[:, 0:NAR]
                tcol[st, b, part, n * BOX : (n + 1) * BOX, :] = own.astype(BF16)
            spread = jnp.broadcast_to(ktab_r[st, part, pl.ds(b, 1), :], (BOX, NAR))
            skew = pltpu.roll(spread, 0, 1, stride=1, stride_axis=0)
            out, trow = ((ext2, trow1), (BOX, trow2))[st]
            for n in range(0, out, BOX):
                count = min(BOX, out - n)
                own = pltpu.roll(skew, (HALO - reach + n) % NAR, 1)
                trow[b, part, n : n + count] = own[0:count, 0 : trow.shape[3]].astype(BF16)

    tile_row_i, tile_lane = iota((BOX, BOX), 0), iota((BOX, BOX), 1)

    def of_band(index, b):
        return (index >= reach * b) & (index < reach * b + reach)

    def strip_tables(st):
        together = tile_row_i < 0
        for b in range(bands):
            together = together | (of_band(tile_row_i, b) & of_band(tile_lane, b))
        rows_i = iota((BOX, WIDE), 0)
        for part in range(2):
            spread = jnp.zeros((BOX, WIDE), F32)
            for b in range(bands):
                line = jnp.broadcast_to(ktab_c[st, part, b : b + 1, :], (BOX, WIDE))
                spread = jnp.where(of_band(rows_i, b), line, spread)
            skew = pltpu.roll(spread, 0, 1, stride=1, stride_axis=0)
            left = pltpu.roll(skew, WIDE - 2 * reach, 1)
            empty = jnp.zeros((BOX, BOX), BF16)
            for n, values in enumerate((left, skew)):
                block = jnp.where(together, values[:, 0:BOX], 0.0).astype(BF16)
                at = slice(n * BOX, (n + 1) * BOX)
                diag[st, part, at, at] = block
                diag[st, part, at, slice((1 - n) * BOX, (2 - n) * BOX)] = empty

    for b in range(bands):
        band_tables(0, b)
    strip_tables(0)

    whole(info_in, 5).wait_recv()
    infos = info_in[:, 0, :]
    wide = (ntx, BOX)
    row_i, lane_i = iota(wide, 0), iota(wide, 1)
    tile_col = jnp.broadcast_to(infos[:, 6:7], wide)
    tile_row = jnp.sum(jnp.where(row_i == lane_i, tile_col, 0.0), axis=0, keepdims=True)
    tile_row = jnp.broadcast_to(jnp.where(lane1 < ntx, tile_row, -1.0), wide)
    same = tile_col == tile_row
    slot_row = jnp.sum(jnp.where(same & (row_i < lane_i), 1.0, 0.0), axis=0, keepdims=True)
    slot_row = jnp.broadcast_to(slot_row, wide)
    slot_col = jnp.sum(jnp.where(same & (lane_i < row_i), 1.0, 0.0), axis=1, keepdims=True)
    slot_col = jnp.broadcast_to(slot_col, wide)
    target = row_i.astype(F32)
    pick = [
        jnp.where((tile_row == target) & (slot_row == float(s)), 1.0, 0.0)[:, 0:ntx]
        for s in range(2)
    ]
    whole(ib1, 0).wait_recv()
    pieces = jnp.concatenate([ib1[:, r, :] for r in range(rows)], axis=1)
    chosen = gather(jnp.concatenate(pick, axis=0), pieces)
    for s in range(2):
        for r in range(rows):
            ob2[:, s * rows + r, :] = chosen[
                s * ntx : (s + 1) * ntx, r * BOX : (r + 1) * BOX
            ]
    exchange(ob2, ib2, 1)

    here = me.astype(F32)
    for s in range(2):
        mine = (tile_col == here) & (slot_col == float(s))
        sinfo[pl.ds(s, 1), :] = jnp.sum(jnp.where(mine, infos, 0.0), axis=0, keepdims=True)
    sinfo[2:8, :] = jnp.zeros((6, BOX), F32)
    heads = [
        send(sinfo, ninfo, sl_sem.at[0, 2], sl_sem.at[1, 2], south, me),
        send(sinfo, soinfo, sl_sem.at[0, 3], sl_sem.at[1, 3], north, me),
    ]
    lane_f = lane_i.astype(F32)
    give = jnp.concatenate(
        [
            jnp.where((tile_col == lane_f) & (slot_col == float(s)), 1.0, 0.0)[:, 0:ntx]
            for s in range(2)
        ],
        axis=1,
    )
    own_slot = jnp.sum(
        jnp.where(row_i[:, 0:1] == me, slot_col[:, 0:1], 0.0), axis=0, keepdims=True
    )

    eye8 = iota((8, BOX), 0) == iota((8, BOX), 1)

    def tables(which, ref, live):
        for s in range(2):
            line = jnp.broadcast_to(ref[pl.ds(s, 1), :], (8, BOX))
            column = jnp.sum(jnp.where(eye8, line, 0.0), axis=1, keepdims=True)
            table = jnp.broadcast_to(column, (8, BOX)) * live
            boxes = jnp.broadcast_to(column[7:8], (8, BOX))
            for j in range(2):
                wtab[which, s, j] = jnp.where(boxes == float(j), table, 0.0)
                if which == 1:
                    mtab[s, j] = jnp.where(boxes == float(j), 1.0, 0.0)

    tables(1, sinfo, 1.0)
    for b in range(bands):
        band_tables(1, b)
    strip_tables(1)

    whole(ib2, 1).wait_recv()
    for s in range(2):
        for r in range(rows):
            slots[s, pl.ds(r, ntx, stride=rows), :] = ib2[:, s * rows + r, :]

    waits = []
    for n, (src, dst, yy) in enumerate(
        (
            (slots.at[:, BOX - deep : BOX, :], nslots, south),
            (slots.at[:, 0:deep, :], sslots, north),
        )
    ):
        waits.append(send(src, dst, sl_sem.at[0, n], sl_sem.at[1, n], yy, me))

    sw1[...] = jnp.zeros_like(sw1)
    se1[...] = jnp.zeros_like(se1)
    for b in range(bands):
        for j in range(2):
            part = sum(wtab[1, s, j, pl.ds(b, 1), :] * slots[s] for s in range(2))
            model_e[b, deep : deep + BOX, j * BOX : (j + 1) * BOX] = part
            keep = of_band(tile_lane, b)
            shift = (reach * b) if j == 0 else (reach * b + reach) % BOX
            moved = pltpu.roll(part, shift, 1) if shift else part
            ref = (sw1, se1)[j]
            ref[...] = jnp.where(keep, moved, ref[...])
    for n, (src, dst, yy, xx) in enumerate(
        (
            (se1.at[BOX - deep : BOX], west1.at[0:deep], south, east),
            (sw1.at[BOX - deep : BOX], east1.at[0:deep], south, west),
            (se1.at[0:deep], west1.at[deep + BOX : ext1], north, east),
            (sw1.at[0:deep], east1.at[deep + BOX : ext1], north, west),
            (se1, west1.at[deep : deep + BOX], ti, east),
            (sw1, east1.at[deep : deep + BOX], ti, west),
        )
    ):
        waits.append(send(src, dst, sl_sem.at[0, 4 + n], sl_sem.at[1, 4 + n], yy, xx))

    def three(hi, lo, right_hi, right_lo):
        return dot(hi, right_hi) + (dot(hi, right_lo) + dot(lo, right_hi))

    def columns(st, b, image):
        hi, lo = split(image)
        return three(hi, lo, tcol[st, b, 0], tcol[st, b, 1])

    def along_rows(trow, b, image):
        hi, lo = split(image)
        count, depth = trow.shape[2:]
        both = dot(trow[b].reshape(2 * count, depth), hi)
        return both[:count] + (both[count:] + dot(trow[b, 0], lo))

    for b in range(bands):
        mixed_e[b, deep : deep + BOX] = columns(0, b, model_e[b, deep : deep + BOX])

    for copy in heads:
        copy.wait_recv()
    tables(0, ninfo, jnp.where(ti > 0, 1.0, 0.0))
    tables(2, soinfo, jnp.where(ti < nty - 1, 1.0, 0.0))
    for copy in waits[0:2]:
        copy.wait_recv()

    for b in range(bands):
        image = jnp.concatenate(
            [
                jnp.concatenate(
                    [
                        sum(wtab[which, s, j, pl.ds(b, 1), :] * ref[s] for s in range(2))
                        for j in range(2)
                    ],
                    axis=1,
                )
                for which, ref in ((0, nslots), (2, sslots))
            ],
            axis=0,
        )
        image = columns(0, b, image)
        mixed_e[b, 0:deep] = image[0:deep]
        mixed_e[b, deep + BOX : ext1] = image[deep:]

    load_obs.wait()
    load_iv.wait()
    for copy in images:
        copy.wait_recv()
    for copy in waits[2:]:
        copy.wait_recv()

    def halo_parts(left, right, count, edge):
        row = iota((count, BOX), 0)
        inner = ((row >= edge) | (ti > 0)) & ((row < count - edge) | (ti < nty - 1))
        for n, (ref, ok) in enumerate(((left, me > 0), (right, me < ntx - 1))):
            hi, lo = split(jnp.where(inner & ok, ref[...], 0.0))
            ext_h[0:count, n * BOX : (n + 1) * BOX] = hi
            ext_l[0:count, n * BOX : (n + 1) * BOX] = lo

    halo_parts(west1, east1, ext1, deep)
    pack[...] = three(ext_h[...], ext_l[...], diag[0, 0], diag[0, 1])
    row = iota((ext2, 2 * BOX), 0)
    inside = ((row >= HALO) | (ti > 0)) & ((row < HALO + BOX) | (ti < nty - 1))
    first_lanes = iota((ext1, BOX), 1) < reach
    last_lanes = iota((ext1, BOX), 1) >= BOX - reach

    to_west = to_east = jnp.zeros((BOX, BOX), F32)
    for b in range(bands):
        left = pltpu.roll(pack[:, 0:BOX], (BOX - reach * b) % BOX, 1)
        left = mixed_e[b, :, 0:BOX] + jnp.where(first_lanes, left, 0.0)
        right = pltpu.roll(pack[:, BOX:], (2 * BOX - reach - reach * b) % BOX, 1)
        right = mixed_e[b, :, BOX:] + jnp.where(last_lanes, right, 0.0)
        predicted = along_rows(trow1, b, jnp.concatenate([left, right], axis=1))
        residual = jnp.where(inside, iv_e[b] * (obs_e[b] - predicted), 0.0)
        resid_ref[b] = residual[HALO : HALO + BOX]
        image = along_rows(trow2, b, residual)
        back[b] = image
        keep = of_band(tile_lane, b)
        to_west = jnp.where(keep, pltpu.roll(image[:, 0:BOX], reach * b, 1), to_west)
        moved = pltpu.roll(image[:, BOX:], (reach * b + reach) % BOX, 1)
        to_east = jnp.where(keep, moved, to_east)
    sw2[...] = to_west
    se2[...] = to_east
    strips = [
        send(se2, west2, st_sem.at[0, 0], st_sem.at[1, 0], ti, east),
        send(sw2, east2, st_sem.at[0, 1], st_sem.at[1, 1], ti, west),
    ]
    for side in range(2):
        at = slice(side * BOX, (side + 1) * BOX)
        full = diag[1, 0, at, at].astype(F32) + diag[1, 1, at, at].astype(F32)
        fold = jnp.zeros((BOX, BOX), F32)
        for b in range(bands):
            here_lane = tile_lane if side == 0 else tile_lane - (BOX - reach)
            inside_lane = (here_lane >= 0) & (here_lane < reach)
            fold = jnp.where(inside_lane & (tile_row_i - reach * b == here_lane), 1.0, fold)
        fold = fold.astype(BF16)
        for s in range(2):
            weight = jnp.zeros((1, BOX), F32)
            for b in range(bands):
                weight = jnp.where(of_band(lane1, b), wtab[1, s, side, b : b + 1, :], weight)
            hi, lo = split(full * weight)
            hi, lo = split(dot(hi, fold) + dot(lo, fold))
            last[0, at, s * BOX : (s + 1) * BOX] = hi
            last[1, at, s * BOX : (s + 1) * BOX] = lo

    totals = [jnp.zeros((BOX, BOX), F32) for _ in range(2)]
    for b in range(bands):
        gradient = columns(1, b, back[b])
        grad[b] = gradient
        halves = (gradient[:, 0:BOX], gradient[:, BOX:])
        for s in range(2):
            for j in range(2):
                totals[s] = totals[s] + wtab[1, s, j, b : b + 1, :] * halves[j]
    for s in range(2):
        grads[s] = totals[s]
    for copy in strips:
        copy.wait_recv()
    for n, (ref, ok) in enumerate(((west2, me > 0), (east2, me < ntx - 1))):
        hi, lo = split(jnp.where(ok, ref[...], 0.0))
        ext_h[0:BOX, n * BOX : (n + 1) * BOX] = hi
        ext_l[0:BOX, n * BOX : (n + 1) * BOX] = lo
    share = three(ext_h[0:BOX], ext_l[0:BOX], last[0], last[1])
    for s in range(2):
        grads[s] += share[:, s * BOX : (s + 1) * BOX]

    for s in range(2):
        for r in range(rows):
            ob3[:, s * rows + r, :] = grads[s, pl.ds(r, ntx, stride=rows), :]
    exchange(ob3, ib3, 2)
    edges[...] = three(ext_h[0:BOX], ext_l[0:BOX], diag[1, 0], diag[1, 1])
    sgacc[...] = jnp.zeros_like(sgacc)

    def spectra(b, carry):
        left = pltpu.roll(edges[:, 0:BOX], lax.rem(BOX - reach * b, BOX), 1)
        right = pltpu.roll(edges[:, BOX:], lax.rem(2 * BOX - reach - reach * b, BOX), 1)
        halves = (
            grad[b, :, 0:BOX] + jnp.where(tile_lane < reach, left, 0.0),
            grad[b, :, BOX:] + jnp.where(tile_lane >= BOX - reach, right, 0.0),
        )
        for s in range(2):
            under = sum(mtab[s, j, pl.ds(b, 1), :] * halves[j] for j in range(2))
            sgacc[s, pl.ds(b, 1), :] = jnp.sum(slots[s] * under, axis=0, keepdims=True)
        return carry

    lax.fori_loop(0, bands, spectra, 0)
    line = jnp.zeros((1, BOX), F32)
    for s in range(2):
        column = jnp.broadcast_to(jnp.sum(sgacc[s], axis=1, keepdims=True), (8, BOX))
        mark = iota((8, BOX), 1) == iota((8, BOX), 0) + 8 * s
        line = line + jnp.sum(jnp.where(mark, column, 0.0), axis=0, keepdims=True)
    sg_send[0] = line
    spread(sg_send, sg_in, 4)

    whole(ib3, 2).wait_recv()
    pieces = jnp.concatenate(
        [
            jnp.concatenate(
                [ib3[:, s * rows + r, :] for r in range(rows)], axis=1
            )
            for s in range(2)
        ],
        axis=0,
    )
    chosen = gather(give, pieces)
    for r in range(rows):
        ob4[:, r, :] = chosen[:, r * BOX : (r + 1) * BOX]
    exchange(ob4, ib4, 3)

    square = jnp.sum(jnp.where(lane1 < bands, info * info, 0.0), axis=1, keepdims=True)
    step_morph = gamma_v[...] / square
    full = morph_v[...]
    norm = jnp.sum(jnp.sum(full * full, axis=0, keepdims=True), axis=1, keepdims=True)
    step_sed = gamma_v[...] / jnp.sqrt(norm)

    whole(sg_in, 4).wait_recv()
    terms = jnp.zeros((1, BOX), F32)
    for d in range(ntx):
        terms = terms + jnp.where(own_tile == float(d), sg_in[d], 0.0)
    terms = jnp.where(own_slot == 0.0, terms, pltpu.roll(terms, BOX - 8, 1))
    nsed_ref[0] = jnp.maximum(info + step_sed * terms, 0.0)[:, 0:bands]

    whole(ib4, 3).wait_recv()
    for r in range(rows):
        at = pl.ds(r, ntx, stride=rows)
        update = step_morph * ib4[:, r, :]
        nmorph_ref[0, 0, at, :] = jnp.maximum(morph_v[at, :] + update, 0.0)

    for phase, arrived in enumerate((ib1, ib2, ib3, ib4, sg_in, info_in)):
        whole(arrived, phase).wait_send()
    for copy in images + heads + waits + strips:
        copy.wait_send()


def write_out(resid, morph, sed, resid_o, morph_o, sed_o, sem):
    pairs = ((resid, resid_o), (morph, morph_o), (sed, sed_o))
    stores = [pltpu.make_async_copy(a, o, sem.at[n]) for n, (a, o) in enumerate(pairs)]
    for copy in stores:
        copy.start()
    for copy in stores:
        copy.wait()


def solution(mesh):
    nty, ntx = mesh.shape["ty"], mesh.shape["tx"]

    def body(observed, inverse_variance, sed, morph, foot_block, gamma, row_kernel, col_kernel):
        bands, height, width = observed.shape
        taps = row_kernel.shape[1]
        rows = BOX // ntx
        deep = 2 * HALO
        ext1, ext2 = height + 2 * deep, height + 2 * HALO

        def vmem(*shape, dtype=F32):
            return pltpu.VMEM(shape, dtype)

        scratch = [
            vmem(bands, ext2, width), vmem(bands, ext2, width),
            vmem(bands, ext1, width), vmem(bands, ext1, width),
            vmem(bands, height, width), vmem(bands, height, width),
            vmem(ext1, BOX), vmem(ext1, BOX), vmem(BOX, BOX), vmem(BOX, BOX),
            vmem(BOX, BOX), vmem(BOX, BOX), vmem(BOX, BOX), vmem(BOX, BOX),
            vmem(ext1, NAR), vmem(BOX, NAR),
            vmem(BOX, BOX), vmem(*sed.shape), vmem(1, 1, dtype=jnp.int32), vmem(1, 1), vmem(8, BOX),
            vmem(1, 1, BOX), vmem(ntx, 1, BOX),
            vmem(ntx, rows, BOX), vmem(ntx, rows, BOX),
            vmem(ntx, 2 * rows, BOX), vmem(ntx, 2 * rows, BOX),
            vmem(ntx, 2 * rows, BOX), vmem(ntx, 2 * rows, BOX),
            vmem(ntx, rows, BOX), vmem(ntx, rows, BOX),
            vmem(1, 1, BOX), vmem(ntx, 1, BOX),
            vmem(2, BOX, BOX), vmem(8, BOX), vmem(2, deep, BOX), vmem(2, deep, BOX),
            vmem(8, BOX), vmem(8, BOX), vmem(2, BOX, BOX), vmem(2, 8, BOX),
            vmem(3, 2, 2, 8, BOX), vmem(2, 2, 8, BOX),
            vmem(bands, taps), vmem(bands, taps),
            vmem(2, 2, 8, WIDE), vmem(2, 2, 8, NAR),
            vmem(2, bands, 2, NAR, NAR, dtype=BF16),
            vmem(bands, 2, ext2, ext1, dtype=BF16), vmem(bands, 2, BOX, ext2, dtype=BF16),
            vmem(2, 2, NAR, NAR, dtype=BF16), vmem(2, NAR, NAR, dtype=BF16),
            vmem(ext1, NAR, dtype=BF16), vmem(ext1, NAR, dtype=BF16),
            pltpu.SemaphoreType.DMA((9,)), pltpu.SemaphoreType.DMA((6,)),
            pltpu.SemaphoreType.DMA((6,)), pltpu.SemaphoreType.DMA((2, 4)),
            pltpu.SemaphoreType.DMA((2, 10)), pltpu.SemaphoreType.DMA((2, 2)),
        ]
        anywhere = pl.BlockSpec(memory_space=pl.ANY)
        vector = pl.BlockSpec(memory_space=pltpu.VMEM)
        shapes = tuple(
            jax.ShapeDtypeStruct(a.shape, F32) for a in (observed, morph, sed)
        )
        operands = (
            observed, inverse_variance, sed, morph, foot_block, gamma, row_kernel, col_kernel
        )
        results = pl.pallas_call(
            functools.partial(kernel, nty, ntx, bands, taps),
            out_shape=shapes,
            in_specs=[pl.BlockSpec(memory_space=pltpu.HBM)] * 8,
            out_specs=(vector, vector, vector),
            scratch_shapes=scratch,
            compiler_params=pltpu.CompilerParams(
                collective_id=0, has_side_effects=True, vmem_limit_bytes=40 * 2**20
            ),
        )(*(a if a.size == 1 else pltpu.with_memory_space_constraint(a, pltpu.HBM) for a in operands))
        return pl.pallas_call(
            write_out,
            out_shape=shapes,
            in_specs=[vector] * 3,
            out_specs=(anywhere,) * 3,
            scratch_shapes=[pltpu.SemaphoreType.DMA((3,))],
            compiler_params=pltpu.CompilerParams(vmem_limit_bytes=8 * 2**20),
        )(*results)

    in_specs = (
        P(None, "ty", "tx"),
        P(None, "ty", "tx"),
        P("ty", "tx", None),
        P("ty", "tx", None, None),
        P("ty", "tx"),
        P("ty", "tx"),
        P(),
        P(),
    )
    out_specs = (P(None, "ty", "tx"), P("ty", "tx", None, None), P("ty", "tx", None))
    return jax.shard_map(body, mesh=mesh, in_specs=in_specs, out_specs=out_specs, check_vma=False)
```
